32 devices in a mesh: dp: 8 (over y, x, core), tensor: 4 (over z).
Axes of the slice: x: 2, y: 2, z: 4, core: 2. Of those that a mesh axis runs over, the one named last changes fastest.
Arguments:
- block_input: float32 [8192, 1536], P(('dp', 'tensor')), may hold values from -17 to 17
- positions: int32 [8192], P('dp'), may hold values from 0 to 2047, as said below
- attn_gain: float32 [1536], replicated, may hold values from 0.5 to 1.5
- w_query: bfloat16 [1536, 1536], P(None, 'tensor'), may hold values from -0.102062073 to 0.102062073
- key_weight: bfloat16 [1536, 768], P(None, 'tensor'), may hold values from -3.0873777 to 3.0873777
- value_weight: bfloat16 [1536, 768], P(None, 'tensor'), may hold values from -0.15625 to 0.15625
- w_out: bfloat16 [1536, 1536], P('tensor'), may hold values from -1.25 to 1.25
- mlp_gain: float32 [1536], replicated, may hold values from 0.5 to 1.5
- w_gate: bfloat16 [1536, 4096], P(None, 'tensor'), may hold values from -0.15625 to 0.15625
- w_up: bfloat16 [1536, 4096], P(None, 'tensor'), may hold values from -0.15625 to 0.15625
- w_down: bfloat16 [4096, 1536], P('tensor'), may hold values from -0.09375 to 0.09375
- out_grad: float32 [8192, 1536], P(('dp', 'tensor')), may hold values from -30 to 30
Outputs:
- block_output: float32 [8192, 1536], P(('dp', 'tensor'))
- input_grad: float32 [8192, 1536], P(('dp', 'tensor'))
- grad_query: float32 [1536, 1536], P(None, 'tensor')
- grad_key: float32 [1536, 768], P(None, 'tensor')
- grad_value: float32 [1536, 768], P(None, 'tensor')
- grad_out: float32 [1536, 1536], P('tensor')
- grad_gate: float32 [1536, 4096], P(None, 'tensor')
- grad_up: float32 [1536, 4096], P(None, 'tensor')
- grad_down: float32 [4096, 1536], P('tensor')
- grad_attn_gain: float32 [1536], replicated
- grad_mlp_gain: float32 [1536], replicated
The draws below stay inside these ranges and needn't reach their ends.
Inputs may be any that keep to these rules, and one draw needn't show every extreme that they name: positions[t] is t minus the index of the first token of t's document, so each document starts at 0; documents hold 1 to 2048 tokens and one of them exactly 2048.
All inputs are finite; a program needn't handle non-finite values.
Results may differ from the reference program's by a relative error of at most 0.014.
The reference program's roundings to bfloat16 on the way count: a program that leaves them out, or rounds other values in their place, can miss the bound.
Values may be sent and summed in bfloat16 or wider, within the bound.
No kernel may reach another device: no remote copies, remote signals or barrier semaphores. Data moves between devices by JAX's collectives and lax.ppermute only.
A program may use at most 192 MiB of HBM per device.

```python
import math
import jax
import jax.numpy as jnp
from jax import lax

MODEL_WIDTH = 1536
QUERY_HEADS = 16
KEY_VALUE_HEADS = 8
HEAD_SIZE = 96
FF = 4096
TOK_DEV = 1024
LONGEST_DOCUMENT = 2048
PACKED_TOKENS = 8192


def draw_positions(key, part):
    shortest = LONGEST_DOCUMENT // 10
    doc_count = PACKED_TOKENS // shortest + 2
    key_lengths, key_start = jax.random.split(key)
    lengths = jax.random.randint(key_lengths, (doc_count,), shortest, LONGEST_DOCUMENT + 1)
    bounds = jnp.cumsum(lengths).astype(jnp.int32)
    long_start = jax.random.randint(key_start, (), 0, PACKED_TOKENS - LONGEST_DOCUMENT + 1).astype(jnp.int32)
    token_index = jnp.arange(PACKED_TOKENS, dtype=jnp.int32)
    boundary = jnp.zeros((PACKED_TOKENS,), jnp.int32)
    earlier_bounds = jnp.where(bounds < long_start, bounds, PACKED_TOKENS)
    later_bounds = jnp.where(long_start + LONGEST_DOCUMENT + bounds < PACKED_TOKENS, long_start + LONGEST_DOCUMENT + bounds, PACKED_TOKENS)
    boundary = boundary.at[0].set(1).at[long_start].set(1)
    boundary = boundary.at[long_start + LONGEST_DOCUMENT].set(1, mode='drop')
    boundary = boundary.at[earlier_bounds].set(1, mode='drop')
    boundary = boundary.at[later_bounds].set(1, mode='drop')
    doc_first = lax.cummax(jnp.where(boundary > 0, token_index, 0), axis=0)
    return token_index - doc_first


def draw_block_input(key, part):
    key_base = jax.random.fold_in(key, 0)
    base_rows = jax.random.normal(key_base, (PACKED_TOKENS, MODEL_WIDTH), jnp.float32)
    return jnp.clip(base_rows, -6.0, 6.0)


def query_key_pair(key):
    key_query, random_key_seed = jax.random.split(jax.random.fold_in(key, 11), 2)
    fanin_scale = MODEL_WIDTH ** (-0.5)
    query_columns = jnp.clip(jax.random.normal(key_query, (MODEL_WIDTH, QUERY_HEADS * HEAD_SIZE), jnp.float32), -4.0, 4.0) * fanin_scale
    key_columns = jnp.clip(jax.random.normal(random_key_seed, (MODEL_WIDTH, KEY_VALUE_HEADS * HEAD_SIZE), jnp.float32), -4.0, 4.0) * fanin_scale
    return (query_columns, key_columns)


def draw_w_query(key, part):
    return query_key_pair(key)[0].astype(jnp.bfloat16)


def draw_key_weight(key, part):
    return query_key_pair(key)[1].astype(jnp.bfloat16)


def draw_out_grad(key, part):
    key_noise, key_scale = jax.random.split(key, 2)
    ramp = 1.0 + 2.0 * jnp.arange(PACKED_TOKENS, dtype=jnp.float32)[:, None] / PACKED_TOKENS
    row_scale = jnp.exp(jax.random.uniform(key_scale, (PACKED_TOKENS, 1), jnp.float32, 0.0, math.log(2.0)))
    noise = jnp.clip(jax.random.normal(key_noise, (PACKED_TOKENS, MODEL_WIDTH), jnp.float32), -4.0, 4.0)
    return noise * row_scale * ramp


def shard_levels(key, shape, cuts, least, high):
    loudness, own = 1.0, jax.random.fold_in(key, 6)
    for dim, parts in cuts:
        draws = jnp.exp(jax.random.uniform(jax.random.fold_in(own, dim), (parts,), jnp.float32, least / len(cuts), high / len(cuts)))
        loudness = loudness * jnp.repeat(draws, shape[dim] // parts).reshape([-1 if axis == dim else 1 for axis in range(len(shape))])
    return loudness


def normal_values(key, dims, scale, limit, cuts=(), kind=jnp.bfloat16):
    result = jax.random.normal(key, dims, jnp.float32) * scale
    if len(cuts) > 0:
        result = shard_levels(key, dims, cuts, -0.22, 0.18) * result
    return jnp.clip(result, min=-limit, max=limit).astype(kind)


def setup_inputs(seed: int = 0) -> dict:
    arg_keys = jax.random.split(jax.random.key(seed), 13)
    return {
        "block_input": draw_block_input(jax.random.fold_in(arg_keys[12], 71), 0),
        "positions": draw_positions(jax.random.fold_in(arg_keys[12], 71), 0),
        "attn_gain": jnp.clip(1.0 + 0.1 * jax.random.normal(arg_keys[2], (MODEL_WIDTH,), jnp.float32), 0.5, 1.5),
        "w_query": draw_w_query(jax.random.fold_in(arg_keys[12], 71), 0),
        "key_weight": draw_key_weight(jax.random.fold_in(arg_keys[12], 71), 0),
        "value_weight": normal_values(arg_keys[5], (MODEL_WIDTH, KEY_VALUE_HEADS * HEAD_SIZE), MODEL_WIDTH ** -0.5, 0.15625, ((1, 4),)),
        "w_out": normal_values(arg_keys[6], (QUERY_HEADS * HEAD_SIZE, MODEL_WIDTH), (HEAD_SIZE // 4) ** -0.5, 1.25, ((0, 4),)),
        "mlp_gain": jnp.clip(1.0 + 0.1 * jax.random.normal(arg_keys[7], (MODEL_WIDTH,), jnp.float32), 0.5, 1.5),
        "w_gate": normal_values(arg_keys[8], (MODEL_WIDTH, FF), MODEL_WIDTH ** -0.5, 0.15625, ((1, 4),)),
        "w_up": normal_values(arg_keys[9], (MODEL_WIDTH, FF), MODEL_WIDTH ** -0.5, 0.15625, ((1, 4),)),
        "w_down": normal_values(arg_keys[10], (FF, MODEL_WIDTH), FF ** -0.5, 0.09375, ((0, 4),)),
        "out_grad": draw_out_grad(jax.random.fold_in(arg_keys[12], 71), 0),
    }


epsilon = 1e-05
rope_base = 100000.0

def rope_tables(positions):
    half_size = HEAD_SIZE // 2
    frequency = rope_base ** (-jnp.arange(half_size, dtype=jnp.float32) * 2.0 / HEAD_SIZE)
    angles = positions.astype(jnp.float32)[:, None] * frequency[None, :]
    return (jnp.cos(angles), jnp.sin(angles))

def apply_rotation(values, cosine_table, sine_table):
    half_size = HEAD_SIZE // 2
    first_half = values[..., :half_size]
    second_half = values[..., half_size:]
    cos_rows = cosine_table[:, None, :]
    sin_rows = sine_table[:, None, :]
    return jnp.concatenate([first_half * cos_rows - second_half * sin_rows, second_half * cos_rows + first_half * sin_rows], axis=-1)

def rotation_backward(grads, cosine_table, sine_table):
    half_size = HEAD_SIZE // 2
    first_half = grads[..., :half_size]
    second_half = grads[..., half_size:]
    cos_rows = cosine_table[:, None, :]
    sin_rows = sine_table[:, None, :]
    return jnp.concatenate([first_half * cos_rows + second_half * sin_rows, second_half * cos_rows - first_half * sin_rows], axis=-1)

def normalize(rows, gain):
    inv_rms = lax.rsqrt(lax.optimization_barrier(jnp.mean(rows * rows, axis=-1, keepdims=True)) + epsilon)
    return ((rows * inv_rms * gain).astype(jnp.bfloat16), inv_rms)

def normalize_back(rows, inv_rms, gain, normed_grad):
    weighted = normed_grad * gain
    inner = lax.optimization_barrier(jnp.mean(weighted * rows, axis=-1, keepdims=True))
    rows_grad = inv_rms * weighted - rows * inv_rms ** 3 * inner
    gain_grad = lax.optimization_barrier(jnp.sum(normed_grad * rows * inv_rms, axis=0))
    return (rows_grad, gain_grad)

def masked_scores(query_block, key_block, index_block, start_block, key_index):
    score_scale = HEAD_SIZE ** (-0.5)
    scores = jnp.einsum('igrd,jgd->grij', query_block.astype(jnp.float32), key_block.astype(jnp.float32)) * score_scale
    allowed = (key_index[None, :] <= index_block[:, None]) & (key_index[None, :] >= start_block[:, None])
    return jnp.where(allowed[None, None], scores, -1e+30)

def reference(block_input, positions, attn_gain, w_query, key_weight, value_weight, w_out, mlp_gain, w_gate, w_up, w_down, out_grad):
    query_group = QUERY_HEADS // KEY_VALUE_HEADS
    span = LONGEST_DOCUMENT + TOK_DEV
    blocks = PACKED_TOKENS // TOK_DEV
    score_scale = HEAD_SIZE ** (-0.5)
    token_index = jnp.arange(PACKED_TOKENS, dtype=jnp.int32)
    doc_starts = token_index - positions
    cosine_table, sine_table = rope_tables(positions)
    attention_normed, inv_rms_attn = normalize(block_input, attn_gain)
    query_rows = apply_rotation(jnp.dot(attention_normed, w_query, preferred_element_type=jnp.float32).reshape(PACKED_TOKENS, QUERY_HEADS, HEAD_SIZE), cosine_table, sine_table).astype(jnp.bfloat16)
    query_rows = query_rows.reshape(PACKED_TOKENS, KEY_VALUE_HEADS, query_group, HEAD_SIZE)
    every_key = apply_rotation(jnp.dot(attention_normed, key_weight, preferred_element_type=jnp.float32).reshape(PACKED_TOKENS, KEY_VALUE_HEADS, HEAD_SIZE), cosine_table, sine_table).astype(jnp.bfloat16)
    every_value = jnp.dot(attention_normed, value_weight, preferred_element_type=jnp.float32).astype(jnp.bfloat16).reshape(PACKED_TOKENS, KEY_VALUE_HEADS, HEAD_SIZE)
    pad_amount = jnp.zeros((LONGEST_DOCUMENT, KEY_VALUE_HEADS, HEAD_SIZE), jnp.bfloat16)
    keys_padded = jnp.concatenate([pad_amount, every_key], axis=0)
    values_padded = jnp.concatenate([pad_amount, every_value], axis=0)

    def block_parts(number):
        first_row = (number * TOK_DEV).astype(jnp.int32)
        query_block = lax.dynamic_slice_in_dim(query_rows, first_row, TOK_DEV, 0)
        key_block = lax.dynamic_slice_in_dim(keys_padded, first_row, span, 0)
        value_block = lax.dynamic_slice_in_dim(values_padded, first_row, span, 0)
        index_block = first_row + jnp.arange(TOK_DEV, dtype=jnp.int32)
        start_block = lax.dynamic_slice_in_dim(doc_starts, first_row, TOK_DEV, 0)
        key_index = first_row - LONGEST_DOCUMENT + jnp.arange(span, dtype=jnp.int32)
        return (first_row, query_block, key_block, value_block, index_block, start_block, key_index)

    def forward_block(number):
        first_row, query_block, key_block, value_block, index_block, start_block, key_index = block_parts(number)
        scores = masked_scores(query_block, key_block, index_block, start_block, key_index)
        row_max = lax.optimization_barrier(jnp.max(scores, axis=-1, keepdims=True))
        log_total = row_max + jnp.log(lax.optimization_barrier(jnp.sum(jnp.exp(scores - row_max), axis=-1, keepdims=True)))
        weights = jnp.exp(scores - log_total).astype(jnp.bfloat16)
        mixed = jnp.einsum('grij,jgd->igrd', weights.astype(jnp.float32), value_block.astype(jnp.float32)).astype(jnp.bfloat16)
        return (mixed, log_total)
    numbers = jnp.arange(blocks, dtype=jnp.int32)
    mixed_blocks, log_blocks = lax.map(forward_block, numbers)
    attended = mixed_blocks.reshape(PACKED_TOKENS, QUERY_HEADS * HEAD_SIZE)
    residual = block_input + jnp.dot(attended, w_out, preferred_element_type=jnp.float32)

    def mlp_block(carry, rows):
        grad_gate, grad_up, grad_down, gain_total = carry
        residual_rows, cot_rows = rows
        normed_mlp, inv_rms_mlp = normalize(residual_rows, mlp_gain)
        gate_pre = jnp.dot(normed_mlp, w_gate, preferred_element_type=jnp.float32)
        up_proj = jnp.dot(normed_mlp, w_up, preferred_element_type=jnp.float32)
        sigmoid_gate = jax.nn.sigmoid(gate_pre)
        silu_gate = gate_pre * sigmoid_gate
        hidden = (silu_gate * up_proj).astype(jnp.bfloat16)
        output_rows = residual_rows + jnp.dot(hidden, w_down, preferred_element_type=jnp.float32)
        out_low = cot_rows.astype(jnp.bfloat16)
        grad_down = grad_down + jnp.dot(hidden.T, out_low, preferred_element_type=jnp.float32)
        hidden_grad = jnp.dot(out_low, w_down.T, preferred_element_type=jnp.float32)
        gate_grad = (hidden_grad * up_proj * sigmoid_gate * (1.0 + gate_pre * (1.0 - sigmoid_gate))).astype(jnp.bfloat16)
        up_grad = (hidden_grad * silu_gate).astype(jnp.bfloat16)
        grad_gate = grad_gate + jnp.dot(normed_mlp.T, gate_grad, preferred_element_type=jnp.float32)
        grad_up = grad_up + jnp.dot(normed_mlp.T, up_grad, preferred_element_type=jnp.float32)
        normed_grad = jnp.dot(gate_grad, w_gate.T, preferred_element_type=jnp.float32) + jnp.dot(up_grad, w_up.T, preferred_element_type=jnp.float32)
        rows_grad, gain_grad = normalize_back(residual_rows, inv_rms_mlp, mlp_gain, normed_grad)
        return ((grad_gate, grad_up, grad_down, gain_total + gain_grad), (output_rows, cot_rows + rows_grad))
    start_carry = (jnp.zeros((MODEL_WIDTH, FF), jnp.float32), jnp.zeros((MODEL_WIDTH, FF), jnp.float32), jnp.zeros((FF, MODEL_WIDTH), jnp.float32), jnp.zeros((MODEL_WIDTH,), jnp.float32))
    (grad_gate, grad_up, grad_down, grad_mlp_gain), (output_blocks, residual_grad_blocks) = lax.scan(mlp_block, start_carry, (residual.reshape(blocks, TOK_DEV, MODEL_WIDTH), out_grad.reshape(blocks, TOK_DEV, MODEL_WIDTH)))
    block_output = output_blocks.reshape(PACKED_TOKENS, MODEL_WIDTH)
    residual_grad = residual_grad_blocks.reshape(PACKED_TOKENS, MODEL_WIDTH)
    residual_low = residual_grad.astype(jnp.bfloat16)
    grad_out = jnp.dot(attended.T, residual_low, preferred_element_type=jnp.float32)
    attended_gradient = jnp.dot(residual_low, w_out.T, preferred_element_type=jnp.float32).astype(jnp.bfloat16)
    attended_gradient = attended_gradient.reshape(PACKED_TOKENS, KEY_VALUE_HEADS, query_group, HEAD_SIZE)

    def backward_block(carry, number):
        key_gradient_total, value_gradient_total = carry
        first_row, query_block, key_block, value_block, index_block, start_block, key_index = block_parts(number)
        log_total = log_blocks[number]
        mixed_block = mixed_blocks[number]
        grad_block = lax.dynamic_slice_in_dim(attended_gradient, first_row, TOK_DEV, 0)
        scores = masked_scores(query_block, key_block, index_block, start_block, key_index)
        weights = jnp.exp(scores - log_total)
        weights_low = weights.astype(jnp.bfloat16)
        weight_grad = jnp.einsum('igrd,jgd->grij', grad_block.astype(jnp.float32), value_block.astype(jnp.float32))
        row_inner = jnp.transpose(lax.optimization_barrier(jnp.sum(grad_block.astype(jnp.float32) * mixed_block.astype(jnp.float32), axis=-1)), (1, 2, 0))
        score_grad = (weights * (weight_grad - row_inner[..., None]) * score_scale).astype(jnp.bfloat16)
        query_grad = jnp.einsum('grij,jgd->igrd', score_grad.astype(jnp.float32), key_block.astype(jnp.float32))
        key_part = jnp.einsum('grij,igrd->jgd', score_grad.astype(jnp.float32), query_block.astype(jnp.float32))
        value_part = jnp.einsum('grij,igrd->jgd', weights_low.astype(jnp.float32), grad_block.astype(jnp.float32))
        key_gradient_total = lax.dynamic_update_slice_in_dim(key_gradient_total, lax.dynamic_slice_in_dim(key_gradient_total, first_row, span, 0) + key_part, first_row, 0)
        value_gradient_total = lax.dynamic_update_slice_in_dim(value_gradient_total, lax.dynamic_slice_in_dim(value_gradient_total, first_row, span, 0) + value_part, first_row, 0)
        return ((key_gradient_total, value_gradient_total), query_grad)
    empty_window = jnp.zeros((LONGEST_DOCUMENT + PACKED_TOKENS, KEY_VALUE_HEADS, HEAD_SIZE), jnp.float32)
    (key_gradient_total, value_gradient_total), query_grads = lax.scan(backward_block, (empty_window, empty_window), numbers)
    query_grad = rotation_backward(query_grads.reshape(PACKED_TOKENS, QUERY_HEADS, HEAD_SIZE), cosine_table, sine_table).astype(jnp.bfloat16).reshape(PACKED_TOKENS, QUERY_HEADS * HEAD_SIZE)
    key_gradient = rotation_backward(key_gradient_total[LONGEST_DOCUMENT:], cosine_table, sine_table).astype(jnp.bfloat16).reshape(PACKED_TOKENS, KEY_VALUE_HEADS * HEAD_SIZE)
    value_reduced = value_gradient_total[LONGEST_DOCUMENT:].astype(jnp.bfloat16).reshape(PACKED_TOKENS, KEY_VALUE_HEADS * HEAD_SIZE)
    grad_query = jnp.dot(attention_normed.T, query_grad, preferred_element_type=jnp.float32)
    grad_key = jnp.dot(attention_normed.T, key_gradient, preferred_element_type=jnp.float32)
    grad_value = jnp.dot(attention_normed.T, value_reduced, preferred_element_type=jnp.float32)
    attn_normed_grad = jnp.dot(query_grad, w_query.T, preferred_element_type=jnp.float32)
    attn_normed_grad = attn_normed_grad + jnp.dot(key_gradient, key_weight.T, preferred_element_type=jnp.float32)
    attn_normed_grad = attn_normed_grad + jnp.dot(value_reduced, value_weight.T, preferred_element_type=jnp.float32)
    input_part, grad_attn_gain = normalize_back(block_input, inv_rms_attn, attn_gain, attn_normed_grad)
    input_grad = residual_grad + input_part
    return (block_output, input_grad, grad_query, grad_key, grad_value, grad_out, grad_gate, grad_up, grad_down, grad_attn_gain, grad_mlp_gain)
```

```python
import functools
import math

import jax
import jax.numpy as jnp
from jax import lax
from jax.experimental import pallas as pl
from jax.experimental.pallas import tpu as pltpu
from jax.sharding import PartitionSpec as P

QUERY_HEADS = 16
KEY_VALUE_HEADS = 8
HEAD_SIZE = 96
LONGEST_DOCUMENT = 2048

LANES = 128
HALF_LANES = LANES // 2
FAR = -1e30

epsilon = 1e-05
rope_base = 100000.0

f32 = jnp.float32
bf16 = jnp.bfloat16


def from_behind(value, axis, steps):
    count = lax.axis_size(axis)
    leading, last = (max(0, -steps), min(count, count - steps))
    return lax.ppermute(value, axis, [(source, source + steps) for source in range(leading, last)])


def exchange(value, axis, distance):
    count = lax.axis_size(axis)
    return lax.ppermute(value, axis, [(i, i ^ distance) for i in range(count)])


def rope_tables(positions):
    half_size = HEAD_SIZE // 2
    frequency = rope_base ** (-jnp.arange(half_size, dtype=f32) * 2.0 / HEAD_SIZE)
    rest = jnp.zeros((HALF_LANES - half_size,), f32)
    spread = jnp.concatenate([frequency, rest, frequency, rest])
    sign = jnp.where(jnp.arange(LANES) < HALF_LANES, -1.0, 1.0).astype(f32)
    angles = positions.astype(f32)[:, None] * spread[None, :]
    return (jnp.cos(angles), jnp.sin(angles) * sign[None, :])


def spread_matrix(heads, dtype=bf16):
    half_size = HEAD_SIZE // 2
    rows = jnp.arange(heads * HEAD_SIZE, dtype=jnp.int32)
    inner = rows % HEAD_SIZE
    lane = (rows // HEAD_SIZE) * LANES + jnp.where(
        inner < half_size, inner, inner - half_size + HALF_LANES
    )
    columns = jnp.arange(heads * LANES, dtype=jnp.int32)
    return (lane[:, None] == columns[None, :]).astype(dtype)


def normalize(rows, gain):
    inv_rms = lax.rsqrt(jnp.mean(rows * rows, axis=-1, keepdims=True) + epsilon)
    return ((rows * inv_rms * gain).astype(bf16), inv_rms)


def normalize_back(rows, inv_rms, gain, normed_grad):
    weighted = normed_grad * gain
    inner = jnp.mean(weighted * rows, axis=-1, keepdims=True)
    return inv_rms * weighted - rows * inv_rms**3 * inner


def turn(value, cosine, sine):
    return value * cosine + pltpu.roll(value, HALF_LANES, 1) * sine


def turn_back(value, cosine, sine):
    return value * cosine - pltpu.roll(value, HALF_LANES, 1) * sine


def project_kernel(rotated, rows_ref, weight_ref, cosine_ref, sine_ref, out_ref):
    product = jnp.dot(rows_ref[...], weight_ref[...], preferred_element_type=f32)
    cosine = cosine_ref[...]
    sine = sine_ref[...]
    for head in range(out_ref.shape[1] // LANES):
        part = product[:, head * LANES : (head + 1) * LANES]
        if head < rotated:
            part = turn(part, cosine, sine)
        out_ref[:, head * LANES : (head + 1) * LANES] = part.astype(bf16)


def project(rows, weight, cosine, sine, rotated, block):
    count, depth = rows.shape
    width = weight.shape[1]
    return pl.pallas_call(
        functools.partial(project_kernel, rotated),
        grid=(count // block,),
        in_specs=[
            pl.BlockSpec((block, depth), lambda i: (i, 0)),
            pl.BlockSpec((depth, width), lambda i: (0, 0)),
            pl.BlockSpec((block, LANES), lambda i: (i, 0)),
            pl.BlockSpec((block, LANES), lambda i: (i, 0)),
        ],
        out_specs=pl.BlockSpec((block, width), lambda i: (i, 0)),
        out_shape=jax.ShapeDtypeStruct((count, width), bf16),
        cost_estimate=pl.CostEstimate(
            flops=2 * count * depth * width,
            bytes_accessed=2 * (count * depth + depth * width + count * width),
            transcendentals=0,
        ),
        name="project",
    )(rows, weight, cosine, sine)


def pair_rows(ref, group):
    return jnp.concatenate([ref[:, h * LANES : (h + 1) * LANES] for h in range(group)], axis=0)


def place_row(ref, group):
    row = ref[0]
    return jnp.concatenate([row] * group, axis=1)


def masked(scores, first, last, base):
    index = lax.broadcasted_iota(jnp.int32, scores.shape, 0)
    allowed = (index >= first - base) & (index <= last - base)
    return jnp.where(allowed, scores, FAR)


def bounds(low_ref, query_block, rows, tile_rows, offset):
    high = (offset + (query_block + 1) * rows - 1) // tile_rows + 1
    return low_ref[query_block], high


def attend_kernel(tiles, group, factor, low_ref, query_ref, first_ref, *refs):
    keys = refs[:tiles]
    values = refs[tiles : 2 * tiles]
    out_ref, log_ref, key_window, value_turned, top, total, mixed = refs[2 * tiles :]
    query_block = pl.program_id(1)
    rows = query_ref.shape[0]
    stretch = keys[0].shape[0]
    tile_rows = key_window.shape[1]
    per_tile = stretch // tile_rows

    @pl.when(query_block == 0)
    def _():
        for tile in range(tiles):
            for part in range(per_tile):
                at = pl.ds(part * tile_rows, tile_rows)
                key_window[tile * per_tile + part] = keys[tile][at, :]
                value_turned[tile * per_tile + part] = values[tile][at, :].T

    offset = (tiles - 1) * stretch
    query = pair_rows(query_ref, group)
    first = place_row(first_ref, group)
    lane = lax.broadcasted_iota(jnp.int32, (1, rows), 1)
    last = jnp.concatenate([lane] * group, axis=1) + (offset + query_block * rows)
    top[...] = jnp.full_like(top, FAR)
    total[...] = jnp.zeros_like(total)
    mixed[...] = jnp.zeros_like(mixed)
    low, high = bounds(low_ref, query_block, rows, tile_rows, offset)

    def step(tile, unused):
        scores = lax.dot_general(
            key_window[tile], query, (((1,), (1,)), ((), ())), preferred_element_type=f32
        )
        scores = masked(scores, first, last, tile * tile_rows)
        before = top[...]
        after = jnp.maximum(before, jnp.max(scores, axis=0, keepdims=True))
        weights = jnp.exp2(scores * factor - after * factor)
        fade = jnp.exp2((before - after) * factor)
        top[...] = after
        total[...] = total[...] * fade + jnp.sum(weights, axis=0, keepdims=True)
        mixed[...] = mixed[...] * fade + jnp.dot(
            value_turned[tile], weights.astype(bf16), preferred_element_type=f32
        )
        return unused

    lax.fori_loop(low, high, step, 0)
    result = (mixed[...] / total[...]).T.astype(bf16)
    for head in range(group):
        out_ref[:, head * LANES : (head + 1) * LANES] = result[head * rows : (head + 1) * rows]
    log_ref[0, 0] = top[...] * factor + jnp.log2(total[...])


def window_specs(tiles, stretch, first_column):
    return [
        pl.BlockSpec((stretch, LANES), lambda g, i, *s, c=c: (0, c + g)) for c in first_column
    ]


def attend(queries_joined, windows, firsts, low, kv_heads, group, rows, tile_rows):
    stretch = queries_joined.shape[0]
    tiles = len(windows)
    blocks = stretch // rows
    pairs = group * rows
    window_tiles = tiles * stretch // tile_rows
    factor = HEAD_SIZE ** (-0.5) * math.log2(math.e)
    key_columns = [at for _, at in windows]
    value_columns = [at + kv_heads for _, at in windows]
    arrays = [a for a, _ in windows]
    grid_spec = pltpu.PrefetchScalarGridSpec(
        num_scalar_prefetch=1,
        grid=(kv_heads, blocks),
        in_specs=[
            pl.BlockSpec((rows, group * LANES), lambda g, i, *s: (i, g)),
            pl.BlockSpec((1, 1, rows), lambda g, i, *s: (i, 0, 0)),
        ]
        + window_specs(tiles, stretch, key_columns)
        + window_specs(tiles, stretch, value_columns),
        out_specs=[
            pl.BlockSpec((rows, group * LANES), lambda g, i, *s: (i, g)),
            pl.BlockSpec((1, 1, 1, pairs), lambda g, i, *s: (g, i, 0, 0)),
        ],
        scratch_shapes=[
            pltpu.VMEM((window_tiles, tile_rows, LANES), bf16),
            pltpu.VMEM((window_tiles, LANES, tile_rows), bf16),
            pltpu.VMEM((1, pairs), f32),
            pltpu.VMEM((1, pairs), f32),
            pltpu.VMEM((LANES, pairs), f32),
        ],
    )
    work = stretch * stretch * kv_heads * group
    return pl.pallas_call(
        functools.partial(attend_kernel, tiles, group, factor),
        grid_spec=grid_spec,
        out_shape=[
            jax.ShapeDtypeStruct((stretch, kv_heads * group * LANES), bf16),
            jax.ShapeDtypeStruct((kv_heads, blocks, 1, pairs), f32),
        ],
        cost_estimate=pl.CostEstimate(
            flops=16 * LANES * work, bytes_accessed=8 * stretch * stretch, transcendentals=work
        ),
        name="attend",
    )(low, queries_joined, firsts, *arrays, *arrays)


def attend_back_kernel(tiles, group, factor, scale, low_ref, query_ref, first_ref, *refs):
    mixed_ref, grad_ref, log_ref, cosine_ref, sine_ref = refs[:5]
    keys = refs[5 : 5 + tiles]
    values = refs[5 + tiles : 5 + 2 * tiles]
    (
        query_out,
        key_out,
        value_out,
        key_window,
        value_window,
        key_turned,
        query_total,
    ) = refs[5 + 2 * tiles :]
    query_block = pl.program_id(1)
    rows = query_ref.shape[0]
    stretch = keys[0].shape[0]
    tile_rows = key_window.shape[1]
    per_tile = stretch // tile_rows

    @pl.when(query_block == 0)
    def _():
        key_out[...] = jnp.zeros_like(key_out)
        value_out[...] = jnp.zeros_like(value_out)
        for tile in range(tiles):
            for part in range(per_tile):
                at = pl.ds(part * tile_rows, tile_rows)
                key_window[tile * per_tile + part] = keys[tile][at, :]
                key_turned[tile * per_tile + part] = keys[tile][at, :].T
                value_window[tile * per_tile + part] = values[tile][at, :]

    offset = (tiles - 1) * stretch
    query = pair_rows(query_ref, group)
    grad = pair_rows(grad_ref, group)
    mixed = pair_rows(mixed_ref, group)
    inner = jnp.sum((grad.astype(f32) * mixed.astype(f32)).T, axis=0, keepdims=True)
    log_total = log_ref[0, 0]
    first = place_row(first_ref, group)
    lane = lax.broadcasted_iota(jnp.int32, (1, rows), 1)
    last = jnp.concatenate([lane] * group, axis=1) + (offset + query_block * rows)
    query_total[...] = jnp.zeros_like(query_total)
    low, high = bounds(low_ref, query_block, rows, tile_rows, offset)
    both_last = (((1,), (1,)), ((), ()))

    def step(tile, unused):
        scores = lax.dot_general(key_window[tile], query, both_last, preferred_element_type=f32)
        scores = masked(scores, first, last, tile * tile_rows)
        weights = jnp.exp2(scores * factor - log_total)
        weight_grad = lax.dot_general(
            value_window[tile], grad, both_last, preferred_element_type=f32
        )
        score_grad = (weights * (weight_grad - inner) * scale).astype(bf16)
        at = pl.ds(pl.multiple_of(tile * tile_rows, tile_rows), tile_rows)
        value_out[at, :] += jnp.dot(weights.astype(bf16), grad, preferred_element_type=f32)
        key_out[at, :] += jnp.dot(score_grad, query, preferred_element_type=f32)
        query_total[...] += jnp.dot(key_turned[tile], score_grad, preferred_element_type=f32)
        return unused

    lax.fori_loop(low, high, step, 0)
    result = query_total[...].T
    for head in range(group):
        part = result[head * rows : (head + 1) * rows]
        query_out[:, head * LANES : (head + 1) * LANES] = turn_back(
            part, cosine_ref[...], sine_ref[...]
        ).astype(bf16)


def attend_back(
    queries_joined, windows, firsts, low, mixed, grads, logs, cosine, sine,
    kv_heads, group, rows, tile_rows,
):
    stretch = queries_joined.shape[0]
    tiles = len(windows)
    blocks = stretch // rows
    pairs = group * rows
    window_tiles = tiles * stretch // tile_rows
    scale = HEAD_SIZE ** (-0.5)
    factor = scale * math.log2(math.e)
    key_columns = [at for _, at in windows]
    value_columns = [at + kv_heads for _, at in windows]
    arrays = [a for a, _ in windows]
    heads_spec = pl.BlockSpec((rows, group * LANES), lambda g, i, *s: (i, g))
    table_spec = pl.BlockSpec((rows, LANES), lambda g, i, *s: (i, 0))
    total_spec = pl.BlockSpec((tiles * stretch, LANES), lambda g, i, *s: (0, g))
    grid_spec = pltpu.PrefetchScalarGridSpec(
        num_scalar_prefetch=1,
        grid=(kv_heads, blocks),
        in_specs=[
            heads_spec,
            pl.BlockSpec((1, 1, rows), lambda g, i, *s: (i, 0, 0)),
            heads_spec,
            heads_spec,
            pl.BlockSpec((1, 1, 1, pairs), lambda g, i, *s: (g, i, 0, 0)),
            table_spec,
            table_spec,
        ]
        + window_specs(tiles, stretch, key_columns)
        + window_specs(tiles, stretch, value_columns),
        out_specs=[heads_spec, total_spec, total_spec],
        scratch_shapes=[
            pltpu.VMEM((window_tiles, tile_rows, LANES), bf16),
            pltpu.VMEM((window_tiles, tile_rows, LANES), bf16),
            pltpu.VMEM((window_tiles, LANES, tile_rows), bf16),
            pltpu.VMEM((LANES, pairs), f32),
        ],
    )
    work = stretch * stretch * kv_heads * group
    return pl.pallas_call(
        functools.partial(attend_back_kernel, tiles, group, factor, scale),
        grid_spec=grid_spec,
        out_shape=[
            jax.ShapeDtypeStruct((stretch, kv_heads * group * LANES), bf16),
            jax.ShapeDtypeStruct((tiles * stretch, kv_heads * LANES), f32),
            jax.ShapeDtypeStruct((tiles * stretch, kv_heads * LANES), f32),
        ],
        cost_estimate=pl.CostEstimate(
            flops=40 * LANES * work, bytes_accessed=16 * stretch * stretch, transcendentals=work
        ),
        name="attend_back",
    )(low, queries_joined, firsts, mixed, grads, logs, cosine, sine, *arrays, *arrays)


def gather_back_kernel(kv_heads, parts, key_ref, value_ref, cosine_ref, sine_ref, *refs):
    out_ref = refs[2 * parts]
    for head in range(kv_heads):
        at = pl.ds(head * LANES, LANES)
        key = key_ref[:, at]
        value = value_ref[:, at]
        for part in range(parts):
            key = key + refs[2 * part][:, at].astype(f32)
            value = value + refs[2 * part + 1][:, at].astype(f32)
        out_ref[:, at] = turn_back(key, cosine_ref[...], sine_ref[...]).astype(bf16)
        out_ref[:, pl.ds((kv_heads + head) * LANES, LANES)] = value.astype(bf16)


def gather_back(key_totals, value_totals, received, cosine, sine, kv_heads, stretch, block):
    skipped = key_totals.shape[0] // block - stretch // block
    width = kv_heads * LANES
    own = pl.BlockSpec((block, width), lambda i: (i + skipped, 0))
    other = pl.BlockSpec((block, width), lambda i: (i, 0))
    table = pl.BlockSpec((block, LANES), lambda i: (i, 0))
    flat = [array for pair in received for array in pair]
    return pl.pallas_call(
        functools.partial(gather_back_kernel, kv_heads, len(received)),
        grid=(stretch // block,),
        in_specs=[own, own, table, table] + [other] * len(flat),
        out_specs=pl.BlockSpec((block, 2 * width), lambda i: (i, 0)),
        out_shape=jax.ShapeDtypeStruct((stretch, 2 * width), bf16),
        name="gather_back",
    )(key_totals, value_totals, cosine, sine, *flat)


def product_over(left, right, axis, order):
    count = lax.axis_size(axis)
    index = lax.axis_index(axis)
    size = left.shape[1] // 2

    def times(offset):
        part = lax.dynamic_slice_in_dim(left, offset, size, 1)
        return jnp.dot(part.T, right, preferred_element_type=f32)

    kept = None
    for place in order:
        bit = (index >> place) & 1
        if kept is None:
            sent = times((1 - bit) * size).astype(bf16)
            got = exchange(sent, axis, 1 << place)
            kept = times(bit * size) + got.astype(f32)
        else:
            size //= 2
            sent = lax.dynamic_slice_in_dim(kept, (1 - bit) * size, size, 0).astype(bf16)
            got = exchange(sent, axis, 1 << place)
            kept = lax.dynamic_slice_in_dim(kept, bit * size, size, 0) + got.astype(f32)
    whole = kept.astype(bf16)
    for place in reversed(order):
        bit = (index >> place) & 1
        got = exchange(whole, axis, 1 << place)
        whole = jnp.where(
            bit == 1,
            jnp.concatenate([got, whole], axis=0),
            jnp.concatenate([whole, got], axis=0),
        )
    return whole.astype(f32)


def sum_everywhere(value, axes):
    for axis in axes:
        count = lax.axis_size(axis)
        place = 1
        while place < count:
            value = value + exchange(value, axis, place)
            place *= 2
    return value


def scatter_sum(product):
    return lax.psum_scatter(
        product.astype(bf16), "tensor", scatter_dimension=0, tiled=True
    ).astype(f32)


def gather_rows(rows):
    return lax.all_gather(rows, "tensor", axis=0, tiled=True)


def after(value, *others):
    return lax.optimization_barrier((value,) + others)[0]


def per_device(
    block_input,
    positions,
    attn_gain,
    w_query,
    key_weight,
    value_weight,
    w_out,
    mlp_gain,
    w_gate,
    w_up,
    w_down,
    out_grad,
):
    stretch = positions.shape[0]
    reach = LONGEST_DOCUMENT // stretch
    heads = w_query.shape[1] // HEAD_SIZE
    kv_heads = key_weight.shape[1] // HEAD_SIZE
    group = heads // kv_heads
    rows = min(256, stretch)
    tile_rows = min(512, stretch)
    blocks = stretch // rows
    places = list(range((lax.axis_size("dp") - 1).bit_length()))
    crossed = places[:1] + places[:0:-1]

    normed_own, inv_rms_attn = normalize(block_input, attn_gain)
    attention_normed = gather_rows(normed_own)
    out_low = gather_rows(after(out_grad.astype(bf16), attention_normed))

    query_spread = spread_matrix(heads)
    kv_spread = spread_matrix(2 * kv_heads)
    all_spread = spread_matrix(heads + 2 * kv_heads)
    w_joined = jnp.dot(
        jnp.concatenate([w_query, key_weight, value_weight], axis=1), all_spread,
        preferred_element_type=bf16,
    )
    w_out_spread = jnp.dot(query_spread.T, w_out, preferred_element_type=bf16)
    cosine, sine = rope_tables(positions)
    local = jnp.arange(stretch, dtype=jnp.int32)
    window_first = reach * stretch + local - positions
    firsts = window_first.reshape(blocks, 1, rows)
    low = jnp.min(window_first.reshape(blocks, rows), axis=1) // tile_rows

    joined = project(attention_normed, w_joined, cosine, sine, heads + kv_heads, rows)
    key_value = joined[:, heads * LANES :]
    windows = [(from_behind(key_value, "dp", d), 0) for d in range(reach, 0, -1)]
    windows = windows + [(joined, heads)]
    attended, logs = attend(joined, windows, firsts, low, kv_heads, group, rows, tile_rows)

    residual = block_input + scatter_sum(
        jnp.dot(attended, w_out_spread, preferred_element_type=f32)
    )
    mlp_normed_own, inv_rms_mlp = normalize(residual, mlp_gain)
    normed_mlp = gather_rows(mlp_normed_own)
    gate_pre = jnp.dot(normed_mlp, w_gate, preferred_element_type=f32)
    up_proj = jnp.dot(normed_mlp, w_up, preferred_element_type=f32)
    sigmoid_gate = jax.nn.sigmoid(gate_pre)
    silu_gate = gate_pre * sigmoid_gate
    hidden = (silu_gate * up_proj).astype(bf16)
    hidden_grad = jnp.dot(out_low, w_down.T, preferred_element_type=f32)
    gate_grad = (
        hidden_grad * up_proj * sigmoid_gate * (1.0 + gate_pre * (1.0 - sigmoid_gate))
    ).astype(bf16)
    up_grad = (hidden_grad * silu_gate).astype(bf16)
    mlp_normed_grad = scatter_sum(
        jnp.dot(gate_grad, w_gate.T, preferred_element_type=f32)
        + jnp.dot(up_grad, w_up.T, preferred_element_type=f32)
    )
    residual_part = normalize_back(residual, inv_rms_mlp, mlp_gain, mlp_normed_grad)
    residual_grad = out_grad + residual_part
    residual_low = gather_rows(residual_grad.astype(bf16))

    down_product = after(
        jnp.dot(hidden, w_down, preferred_element_type=f32).astype(bf16), residual_low
    )
    block_output = residual + scatter_sum(down_product)

    grad_gate = product_over(normed_mlp, gate_grad, "dp", places)
    grad_up = product_over(normed_mlp, up_grad, "dp", crossed)
    grad_down = product_over(hidden, out_low, "dp", places)

    attended_plain = jnp.dot(attended, query_spread.T, preferred_element_type=bf16)
    grad_out = product_over(attended_plain, residual_low, "dp", crossed)
    attended_gradient = jnp.dot(residual_low, w_out_spread.T, preferred_element_type=f32).astype(
        bf16
    )
    query_grad, key_totals, value_totals = attend_back(
        joined, windows, firsts, low, attended, attended_gradient, logs, cosine, sine,
        kv_heads, group, rows, tile_rows,
    )
    received = []
    for distance in range(1, reach + 1):
        begin = (reach - distance) * stretch
        received.append(
            [
                from_behind(total[begin : begin + stretch].astype(bf16), "dp", -distance)
                for total in (key_totals, value_totals)
            ]
        )
    key_value_grad = gather_back(
        key_totals, value_totals, received, cosine, sine, kv_heads, stretch, rows
    )
    split = heads * LANES
    attn_normed_part = jnp.dot(
        query_grad, w_joined[:, :split].T, preferred_element_type=f32
    ) + jnp.dot(key_value_grad, w_joined[:, split:].T, preferred_element_type=f32)
    attn_normed_grad = scatter_sum(attn_normed_part)
    input_part = normalize_back(block_input, inv_rms_attn, attn_gain, attn_normed_grad)
    input_grad = residual_grad + input_part

    query_plain = jnp.dot(query_grad, query_spread.T, preferred_element_type=bf16)
    kv_plain = jnp.dot(key_value_grad, kv_spread.T, preferred_element_type=bf16)
    grad_query = product_over(attention_normed, query_plain, "dp", places)
    grad_key_value = product_over(attention_normed, kv_plain, "dp", crossed)
    grad_key = grad_key_value[:, : kv_heads * HEAD_SIZE]
    grad_value = grad_key_value[:, kv_heads * HEAD_SIZE :]

    mlp_gain_part = jnp.sum(mlp_normed_grad * residual * inv_rms_mlp, axis=0, keepdims=True)
    attn_gain_part = jnp.sum(attn_normed_grad * block_input * inv_rms_attn, axis=0, keepdims=True)
    grad_mlp_gain = sum_everywhere(mlp_gain_part, ("tensor", "dp"))[0]
    grad_attn_gain = sum_everywhere(attn_gain_part, ("tensor", "dp"))[0]
    return (
        block_output,
        input_grad,
        grad_query,
        grad_key,
        grad_value,
        grad_out,
        grad_gate,
        grad_up,
        grad_down,
        grad_attn_gain,
        grad_mlp_gain,
    )


def solution(mesh):
    in_specs = (
        P(("dp", "tensor"), None),
        P("dp"),
        P(),
        P(None, "tensor"),
        P(None, "tensor"),
        P(None, "tensor"),
        P("tensor", None),
        P(),
        P(None, "tensor"),
        P(None, "tensor"),
        P("tensor", None),
        P(("dp", "tensor"), None),
    )
    out_specs = (
        P(("dp", "tensor"), None),
        P(("dp", "tensor"), None),
        P(None, "tensor"),
        P(None, "tensor"),
        P(None, "tensor"),
        P("tensor", None),
        P(None, "tensor"),
        P(None, "tensor"),
        P("tensor", None),
        P(),
        P(),
    )
    return jax.shard_map(
        per_device, mesh=mesh, in_specs=in_specs, out_specs=out_specs, check_vma=False
    )
```

```python
import functools
import math

import jax
import jax.numpy as jnp
from jax import lax
from jax.experimental import pallas as pl
from jax.experimental.pallas import tpu as pltpu
from jax.sharding import PartitionSpec as P


HEAD_SIZE = 96
LONGEST_DOCUMENT = 2048

LANES = 128
HALF_LANES = LANES // 2
FAR = -1e30


epsilon = 1e-05
rope_base = 100000.0

f32 = jnp.float32
bf16 = jnp.bfloat16


def from_behind(value, axis, steps):
    count = lax.axis_size(axis)
    leading, last = (max(0, -steps), min(count, count - steps))
    return lax.ppermute(value, axis, [(source, source + steps) for source in range(leading, last)])


def exchange(value, axis, distance):
    count = lax.axis_size(axis)
    return lax.ppermute(value, axis, [(i, i ^ distance) for i in range(count)])


def rope_tables(positions):
    half_size = HEAD_SIZE // 2
    frequency = rope_base ** (-jnp.arange(half_size, dtype=f32) * 2.0 / HEAD_SIZE)
    rest = jnp.zeros((HALF_LANES - half_size,), f32)
    spread = jnp.concatenate([frequency, rest, frequency, rest])
    sign = jnp.where(jnp.arange(LANES) < HALF_LANES, -1.0, 1.0).astype(f32)
    angles = positions.astype(f32)[:, None] * spread[None, :]
    return (jnp.cos(angles), jnp.sin(angles) * sign[None, :])


def spread_matrix(heads, dtype=bf16):
    half_size = HEAD_SIZE // 2
    rows = jnp.arange(heads * HEAD_SIZE, dtype=jnp.int32)
    inner = rows % HEAD_SIZE
    lane = (rows // HEAD_SIZE) * LANES + jnp.where(
        inner < half_size, inner, inner - half_size + HALF_LANES
    )
    columns = jnp.arange(heads * LANES, dtype=jnp.int32)
    return (lane[:, None] == columns[None, :]).astype(dtype)


def normalize(rows, gain):
    inv_rms = lax.rsqrt(jnp.mean(rows * rows, axis=-1, keepdims=True) + epsilon)
    return ((rows * inv_rms * gain).astype(bf16), inv_rms)


def normalize_back(rows, inv_rms, gain, normed_grad):
    weighted = normed_grad * gain
    inner = jnp.mean(weighted * rows, axis=-1, keepdims=True)
    return inv_rms * weighted - rows * inv_rms**3 * inner


def turn(value, cosine, sine):
    return value * cosine + pltpu.roll(value, HALF_LANES, 1) * sine


def turn_back(value, cosine, sine):
    return value * cosine - pltpu.roll(value, HALF_LANES, 1) * sine


def project_kernel(rotated, rows_ref, weight_ref, cosine_ref, sine_ref, out_ref):
    product = jnp.dot(rows_ref[...], weight_ref[...], preferred_element_type=f32)
    cosine = cosine_ref[...]
    sine = sine_ref[...]
    for head in range(out_ref.shape[1] // LANES):
        part = product[:, head * LANES : (head + 1) * LANES]
        if head < rotated:
            part = turn(part, cosine, sine)
        out_ref[:, head * LANES : (head + 1) * LANES] = part.astype(bf16)


def project(rows, weight, cosine, sine, rotated, block):
    count, depth = rows.shape
    width = weight.shape[1]
    return pl.pallas_call(
        functools.partial(project_kernel, rotated),
        grid=(count // block,),
        in_specs=[
            pl.BlockSpec((block, depth), lambda i: (i, 0)),
            pl.BlockSpec((depth, width), lambda i: (0, 0)),
            pl.BlockSpec((block, LANES), lambda i: (i, 0)),
            pl.BlockSpec((block, LANES), lambda i: (i, 0)),
        ],
        out_specs=pl.BlockSpec((block, width), lambda i: (i, 0)),
        out_shape=jax.ShapeDtypeStruct((count, width), bf16),
        cost_estimate=pl.CostEstimate(
            flops=2 * count * depth * width,
            bytes_accessed=2 * (count * depth + depth * width + count * width),
            transcendentals=0,
        ),
        name="project",
    )(rows, weight, cosine, sine)


def pair_rows(ref, group):
    return jnp.concatenate([ref[:, h * LANES : (h + 1) * LANES] for h in range(group)], axis=0)


def place_row(ref, group):
    row = ref[0]
    return jnp.concatenate([row] * group, axis=1)


def masked(scores, first, last, base):
    index = lax.broadcasted_iota(jnp.int32, scores.shape, 0)
    allowed = (index >= first - base) & (index <= last - base)
    return jnp.where(allowed, scores, FAR)


def bounds(low_ref, query_block, rows, tile_rows, offset):
    high = (offset + (query_block + 1) * rows - 1) // tile_rows + 1
    return low_ref[query_block], high


def attend_kernel(tiles, group, factor, low_ref, query_ref, first_ref, *refs):
    keys = refs[:tiles]
    values = refs[tiles : 2 * tiles]
    out_ref, log_ref, key_window, value_turned, top, total, mixed = refs[2 * tiles :]
    query_block = pl.program_id(1)
    rows = query_ref.shape[0]
    stretch = keys[0].shape[0]
    tile_rows = key_window.shape[1]
    per_tile = stretch // tile_rows

    @pl.when(query_block == 0)
    def _():
        for tile in range(tiles):
            for part in range(per_tile):
                at = pl.ds(part * tile_rows, tile_rows)
                key_window[tile * per_tile + part] = keys[tile][at, :]
                value_turned[tile * per_tile + part] = values[tile][at, :].T

    offset = (tiles - 1) * stretch
    query = pair_rows(query_ref, group)
    first = place_row(first_ref, group)
    lane = lax.broadcasted_iota(jnp.int32, (1, rows), 1)
    last = jnp.concatenate([lane] * group, axis=1) + (offset + query_block * rows)
    top[...] = jnp.full_like(top, FAR)
    total[...] = jnp.zeros_like(total)
    mixed[...] = jnp.zeros_like(mixed)
    low, high = bounds(low_ref, query_block, rows, tile_rows, offset)

    def step(tile, unused):
        scores = lax.dot_general(
            key_window[tile], query, (((1,), (1,)), ((), ())), preferred_element_type=f32
        )
        scores = masked(scores, first, last, tile * tile_rows)
        before = top[...]
        after = jnp.maximum(before, jnp.max(scores, axis=0, keepdims=True))
        weights = jnp.exp2(scores * factor - after * factor)
        fade = jnp.exp2((before - after) * factor)
        top[...] = after
        total[...] = total[...] * fade + jnp.sum(weights, axis=0, keepdims=True)
        mixed[...] = mixed[...] * fade + jnp.dot(
            value_turned[tile], weights.astype(bf16), preferred_element_type=f32
        )
        return unused

    lax.fori_loop(low, high, step, 0)
    result = (mixed[...] / total[...]).T.astype(bf16)
    for head in range(group):
        out_ref[:, head * LANES : (head + 1) * LANES] = result[head * rows : (head + 1) * rows]
    log_ref[0, 0] = top[...] * factor + jnp.log2(total[...])


def window_specs(stretch, first_column):
    return [
        pl.BlockSpec((stretch, LANES), lambda g, i, *s, c=c: (0, c + g)) for c in first_column
    ]


def attend(queries_joined, windows, firsts, low, kv_heads, group, rows, tile_rows):
    stretch = queries_joined.shape[0]
    tiles = len(windows)
    blocks = stretch // rows
    pairs = group * rows
    window_tiles = tiles * stretch // tile_rows
    factor = HEAD_SIZE ** (-0.5) * math.log2(math.e)
    key_columns = [at for _, at in windows]
    value_columns = [at + kv_heads for _, at in windows]
    arrays = [a for a, _ in windows]
    grid_spec = pltpu.PrefetchScalarGridSpec(
        num_scalar_prefetch=1,
        grid=(kv_heads, blocks),
        in_specs=[
            pl.BlockSpec((rows, group * LANES), lambda g, i, *s: (i, g)),
            pl.BlockSpec((1, 1, rows), lambda g, i, *s: (i, 0, 0)),
        ]
        + window_specs(stretch, key_columns)
        + window_specs(stretch, value_columns),
        out_specs=[
            pl.BlockSpec((rows, group * LANES), lambda g, i, *s: (i, g)),
            pl.BlockSpec((1, 1, 1, pairs), lambda g, i, *s: (g, i, 0, 0)),
        ],
        scratch_shapes=[
            pltpu.VMEM((window_tiles, tile_rows, LANES), bf16),
            pltpu.VMEM((window_tiles, LANES, tile_rows), bf16),
            pltpu.VMEM((1, pairs), f32),
            pltpu.VMEM((1, pairs), f32),
            pltpu.VMEM((LANES, pairs), f32),
        ],
    )
    work = stretch * stretch * kv_heads * group
    return pl.pallas_call(
        functools.partial(attend_kernel, tiles, group, factor),
        grid_spec=grid_spec,
        out_shape=[
            jax.ShapeDtypeStruct((stretch, kv_heads * group * LANES), bf16),
            jax.ShapeDtypeStruct((kv_heads, blocks, 1, pairs), f32),
        ],
        cost_estimate=pl.CostEstimate(
            flops=16 * LANES * work, bytes_accessed=8 * stretch * stretch, transcendentals=work
        ),
        name="attend",
    )(low, queries_joined, firsts, *arrays, *arrays)


def attend_back_kernel(tiles, chunks, group, factor, scale, low_ref, query_ref, first_ref, *refs):
    mixed_ref, log_ref, cosine_ref, sine_ref = refs[:4]
    grad_refs = refs[4 : 4 + chunks]
    refs = refs[4 + chunks :]
    keys = refs[:tiles]
    values = refs[tiles : 2 * tiles]
    (
        query_out,
        key_out,
        value_out,
        key_window,
        value_window,
        key_turned,
        query_total,
    ) = refs[2 * tiles :]
    query_block = pl.program_id(1)
    rows = query_ref.shape[0]
    stretch = keys[0].shape[0]
    tile_rows = key_window.shape[1]
    per_tile = stretch // tile_rows

    @pl.when(query_block == 0)
    def _():
        key_out[...] = jnp.zeros_like(key_out)
        value_out[...] = jnp.zeros_like(value_out)
        for tile in range(tiles):
            for part in range(per_tile):
                at = pl.ds(part * tile_rows, tile_rows)
                key_window[tile * per_tile + part] = keys[tile][at, :]
                key_turned[tile * per_tile + part] = keys[tile][at, :].T
                value_window[tile * per_tile + part] = values[tile][at, :]

    offset = (tiles - 1) * stretch
    query = pair_rows(query_ref, group)
    grad = jnp.concatenate(
        [ref[:, h * LANES : (h + 1) * LANES] for h in range(group) for ref in grad_refs], axis=0
    )
    mixed = pair_rows(mixed_ref, group)
    inner = jnp.sum((grad.astype(f32) * mixed.astype(f32)).T, axis=0, keepdims=True)
    log_total = log_ref[0, 0]
    first = place_row(first_ref, group)
    lane = lax.broadcasted_iota(jnp.int32, (1, rows), 1)
    last = jnp.concatenate([lane] * group, axis=1) + (offset + query_block * rows)
    query_total[...] = jnp.zeros_like(query_total)
    low, high = bounds(low_ref, query_block, rows, tile_rows, offset)
    both_last = (((1,), (1,)), ((), ()))

    def step(tile, unused):
        scores = lax.dot_general(key_window[tile], query, both_last, preferred_element_type=f32)
        scores = masked(scores, first, last, tile * tile_rows)
        weights = jnp.exp2(scores * factor - log_total)
        weight_grad = lax.dot_general(
            value_window[tile], grad, both_last, preferred_element_type=f32
        )
        score_grad = (weights * (weight_grad - inner) * scale).astype(bf16)
        at = pl.ds(pl.multiple_of(tile * tile_rows, tile_rows), tile_rows)
        value_out[at, :] += jnp.dot(weights.astype(bf16), grad, preferred_element_type=f32)
        key_out[at, :] += jnp.dot(score_grad, query, preferred_element_type=f32)
        query_total[...] += jnp.dot(key_turned[tile], score_grad, preferred_element_type=f32)
        return unused

    lax.fori_loop(low, high, step, 0)
    result = query_total[...].T
    for head in range(group):
        part = result[head * rows : (head + 1) * rows]
        query_out[:, head * LANES : (head + 1) * LANES] = turn_back(
            part, cosine_ref[...], sine_ref[...]
        ).astype(bf16)


def attend_back(
    queries_joined, windows, firsts, low, mixed, grads, logs, cosine, sine,
    kv_heads, group, rows, tile_rows,
):
    stretch = queries_joined.shape[0]
    tiles = len(windows)
    blocks = stretch // rows
    pairs = group * rows
    window_tiles = tiles * stretch // tile_rows
    chunks = len(grads)
    scale = HEAD_SIZE ** (-0.5)
    factor = scale * math.log2(math.e)
    key_columns = [at for _, at in windows]
    value_columns = [at + kv_heads for _, at in windows]
    arrays = [a for a, _ in windows]
    heads_spec = pl.BlockSpec((rows, group * LANES), lambda g, i, *s: (i, g))
    table_spec = pl.BlockSpec((rows, LANES), lambda g, i, *s: (i, 0))
    total_spec = pl.BlockSpec((tiles * stretch, LANES), lambda g, i, *s: (0, g))
    grid_spec = pltpu.PrefetchScalarGridSpec(
        num_scalar_prefetch=1,
        grid=(kv_heads, blocks),
        in_specs=[
            heads_spec,
            pl.BlockSpec((1, 1, rows), lambda g, i, *s: (i, 0, 0)),
            heads_spec,
            pl.BlockSpec((1, 1, 1, pairs), lambda g, i, *s: (g, i, 0, 0)),
            table_spec,
            table_spec,
        ]
        + [pl.BlockSpec((rows // chunks, group * LANES), lambda g, i, *s: (i, g))] * chunks
        + window_specs(stretch, key_columns)
        + window_specs(stretch, value_columns),
        out_specs=[heads_spec, total_spec, total_spec],
        scratch_shapes=[
            pltpu.VMEM((window_tiles, tile_rows, LANES), bf16),
            pltpu.VMEM((window_tiles, tile_rows, LANES), bf16),
            pltpu.VMEM((window_tiles, LANES, tile_rows), bf16),
            pltpu.VMEM((LANES, pairs), f32),
        ],
    )
    work = stretch * stretch * kv_heads * group
    return pl.pallas_call(
        functools.partial(attend_back_kernel, tiles, chunks, group, factor, scale),
        grid_spec=grid_spec,
        out_shape=[
            jax.ShapeDtypeStruct((stretch, kv_heads * group * LANES), bf16),
            jax.ShapeDtypeStruct((tiles * stretch, kv_heads * LANES), f32),
            jax.ShapeDtypeStruct((tiles * stretch, kv_heads * LANES), f32),
        ],
        cost_estimate=pl.CostEstimate(
            flops=40 * LANES * work, bytes_accessed=16 * stretch * stretch, transcendentals=work
        ),
        name="attend_back",
    )(low, queries_joined, firsts, mixed, logs, cosine, sine, *grads, *arrays, *arrays)


def gather_back_kernel(kv_heads, parts, key_ref, value_ref, cosine_ref, sine_ref, *refs):
    out_ref = refs[2 * parts]
    for head in range(kv_heads):
        at = pl.ds(head * LANES, LANES)
        key = key_ref[:, at]
        value = value_ref[:, at]
        for part in range(parts):
            key = key + refs[2 * part][:, at].astype(f32)
            value = value + refs[2 * part + 1][:, at].astype(f32)
        out_ref[:, at] = turn_back(key, cosine_ref[...], sine_ref[...]).astype(bf16)
        out_ref[:, pl.ds((kv_heads + head) * LANES, LANES)] = value.astype(bf16)


def gather_back(key_totals, value_totals, received, cosine, sine, kv_heads, stretch, block):
    skipped = key_totals.shape[0] // block - stretch // block
    width = kv_heads * LANES
    own = pl.BlockSpec((block, width), lambda i: (i + skipped, 0))
    other = pl.BlockSpec((block, width), lambda i: (i, 0))
    table = pl.BlockSpec((block, LANES), lambda i: (i, 0))
    flat = [array for pair in received for array in pair]
    return pl.pallas_call(
        functools.partial(gather_back_kernel, kv_heads, len(received)),
        grid=(stretch // block,),
        in_specs=[own, own, table, table] + [other] * len(flat),
        out_specs=pl.BlockSpec((block, 2 * width), lambda i: (i, 0)),
        out_shape=jax.ShapeDtypeStruct((stretch, 2 * width), bf16),
        name="gather_back",
    )(key_totals, value_totals, cosine, sine, *flat)


class SharedProduct:

    def __init__(self, left, right, axis, order):
        self.left, self.right, self.axis, self.order = left, right, axis, order
        self.size = left.shape[1] // 2
        self.sent = self.times(0, True).astype(bf16)

    def bit(self, place):
        return (lax.axis_index(self.axis) >> place) & 1

    def times(self, place, other):
        bit = self.bit(self.order[place])
        offset = ((1 - bit) if other else bit) * self.size
        part = lax.dynamic_slice_in_dim(self.left, offset, self.size, 1)
        return jnp.dot(part.T, self.right, preferred_element_type=f32)

    def meet(self):
        got = exchange(self.sent, self.axis, 1 << self.order[0])
        self.kept = self.times(0, False) + got.astype(f32)
        return self.kept

    def finish(self):
        axis, kept, size = self.axis, self.kept, self.size
        for place in self.order[1:]:
            bit = self.bit(place)
            size //= 2
            sent = lax.dynamic_slice_in_dim(kept, (1 - bit) * size, size, 0).astype(bf16)
            got = exchange(sent, axis, 1 << place)
            kept = lax.dynamic_slice_in_dim(kept, bit * size, size, 0) + got.astype(f32)
        whole = kept.astype(bf16)
        for place in reversed(self.order):
            bit = self.bit(place)
            got = exchange(whole, axis, 1 << place)
            whole = jnp.where(
                bit == 1,
                jnp.concatenate([got, whole], axis=0),
                jnp.concatenate([whole, got], axis=0),
            )
        return whole.astype(f32)


def sum_everywhere(value, axes):
    for axis in axes:
        count = lax.axis_size(axis)
        place = 1
        while place < count:
            value = value + exchange(value, axis, place)
            place *= 2
    return value


def scatter_sum(product):
    return lax.psum_scatter(
        product.astype(bf16), "tensor", scatter_dimension=0, tiled=True
    ).astype(f32)


def chain_scatter(product, axis, fillers=()):
    count = lax.axis_size(axis)
    index = lax.axis_index(axis)
    rows = product.shape[0] // count

    def piece(offset):
        start = lax.rem(index + offset, count) * rows
        return lax.dynamic_slice_in_dim(product, start, rows, 0).astype(f32)

    right = left = None
    for step in range(1, count):
        to_right = piece((count - step) % count)
        to_left = piece(step % count)
        if right is not None:
            to_right = to_right + right.astype(f32)
            to_left = to_left + left.astype(f32)
        others = fillers[step - 2] if 0 <= step - 2 < len(fillers) else ()
        to_right, to_left = lax.optimization_barrier(
            (to_right.astype(bf16), to_left.astype(bf16)) + tuple(others)
        )[:2]
        right = lax.ppermute(to_right, axis, [(i, i + 1) for i in range(min(step, count - 1))])
        left = lax.ppermute(
            to_left, axis, [(i, i - 1) for i in range(max(count - step, 1), count)]
        )
    return piece(0) + right.astype(f32) + left.astype(f32)


def gather_rows(rows):
    return lax.all_gather(rows, "tensor", axis=0, tiled=True)


def after(value, *others):
    return lax.optimization_barrier((value,) + others)[0]


def per_device(
    block_input,
    positions,
    attn_gain,
    w_query,
    key_weight,
    value_weight,
    w_out,
    mlp_gain,
    w_gate,
    w_up,
    w_down,
    out_grad,
):
    stretch = positions.shape[0]
    reach = LONGEST_DOCUMENT // stretch
    heads = w_query.shape[1] // HEAD_SIZE
    kv_heads = key_weight.shape[1] // HEAD_SIZE
    group = heads // kv_heads
    rows = block_input.shape[0]
    tile_rows = min(512, stretch)
    blocks = stretch // rows
    chunks = 2
    part_rows = rows // chunks
    places = list(range((lax.axis_size("dp") - 1).bit_length()))
    crossed = places[:1] + places[:0:-1]

    def own_parts(value):
        return [value[c * part_rows : (c + 1) * part_rows] for c in range(chunks)]

    def whole_parts(value):
        cut = value.reshape(blocks, chunks, part_rows, value.shape[1])
        return [cut[:, c].reshape(blocks * part_rows, value.shape[1]) for c in range(chunks)]

    def whole_order(parts):
        cut = [part.reshape(blocks, 1, part_rows, part.shape[1]) for part in parts]
        return jnp.concatenate(cut, axis=1).reshape(stretch, parts[0].shape[1])

    normed_own, inv_rms_attn = normalize(block_input, attn_gain)
    attention_normed = gather_rows(normed_own)
    out_low = gather_rows(after(out_grad.astype(bf16), attention_normed))

    query_spread = spread_matrix(heads)
    kv_spread = spread_matrix(2 * kv_heads)
    all_spread = spread_matrix(heads + 2 * kv_heads)
    w_joined = jnp.dot(
        jnp.concatenate([w_query, key_weight, value_weight], axis=1), all_spread,
        preferred_element_type=bf16,
    )
    w_out_spread = jnp.dot(query_spread.T, w_out, preferred_element_type=bf16)
    cosine, sine = rope_tables(positions)
    local = jnp.arange(stretch, dtype=jnp.int32)
    window_first = reach * stretch + local - positions
    firsts = window_first.reshape(blocks, 1, rows)
    low = jnp.min(window_first.reshape(blocks, rows), axis=1) // tile_rows

    joined = project(attention_normed, w_joined, cosine, sine, heads + kv_heads, rows)
    key_value = joined[:, heads * LANES :]
    windows = [(from_behind(key_value, "dp", d), 0) for d in range(reach, 0, -1)]
    windows = windows + [(joined, heads)]
    attended, logs = attend(joined, windows, firsts, low, kv_heads, group, rows, tile_rows)

    out_parts = whole_parts(out_low)
    mixed_product = jnp.dot(attended, w_out_spread, preferred_element_type=f32).astype(bf16)
    residuals, inv_rms_mlps, normed_mlps, c_normed = [], [], [], []
    for part, product in zip(own_parts(block_input), whole_parts(mixed_product)):
        if c_normed:
            product = after(product, c_normed[-1])
        residual = part + chain_scatter(product, "tensor")
        mlp_normed_own, inv_rms_mlp = normalize(residual, mlp_gain)
        c_normed.append(mlp_normed_own)
        residuals.append(residual)
        inv_rms_mlps.append(inv_rms_mlp)
        normed_mlps.append(gather_rows(mlp_normed_own))

    hiddens, gate_grads, up_grads, residual_grads, residual_lows = [], [], [], [], []
    own_lows = []
    gate_pres = [jnp.dot(part, w_gate, preferred_element_type=f32) for part in normed_mlps]
    up_projs = [jnp.dot(part, w_up, preferred_element_type=f32) for part in normed_mlps]
    mlp_gain_part = 0.0
    for c in range(chunks):
        gate_pre, up_proj = gate_pres[c], up_projs[c]
        sigmoid_gate = jax.nn.sigmoid(gate_pre)
        silu_gate = gate_pre * sigmoid_gate
        hiddens.append((silu_gate * up_proj).astype(bf16))
        hidden_grad = jnp.dot(out_parts[c], w_down.T, preferred_element_type=f32)
        gate_grad = (
            hidden_grad * up_proj * sigmoid_gate * (1.0 + gate_pre * (1.0 - sigmoid_gate))
        ).astype(bf16)
        up_grad = (hidden_grad * silu_gate).astype(bf16)
        gate_grads.append(gate_grad)
        up_grads.append(up_grad)
        product = (
            jnp.dot(gate_grad, w_gate.T, preferred_element_type=f32)
            + jnp.dot(up_grad, w_up.T, preferred_element_type=f32)
        ).astype(bf16)
        fillers = ()
        if c + 1 < chunks:
            product = after(product, c_normed[c + 1])
            fillers = ((), (gate_pres[c + 1], up_projs[c + 1]))
        else:
            normed_joined = jnp.concatenate(normed_mlps, axis=0)
            shared = [
                SharedProduct(normed_joined, jnp.concatenate(gate_grads, axis=0), "dp", places),
                SharedProduct(normed_joined, jnp.concatenate(up_grads, axis=0), "dp", crossed),
                SharedProduct(
                    jnp.concatenate(hiddens, axis=0), jnp.concatenate(out_parts, axis=0),
                    "dp", places,
                ),
            ]
            fillers = ([p.sent for p in shared], [p.meet() for p in shared])
        if c > 0:
            product = after(product, own_lows[-1])
        mlp_normed_grad = chain_scatter(product, "tensor", fillers)
        residual_part = normalize_back(residuals[c], inv_rms_mlps[c], mlp_gain, mlp_normed_grad)
        residual_grad = own_parts(out_grad)[c] + residual_part
        residual_grads.append(residual_grad)
        own_lows.append(residual_grad.astype(bf16))
        residual_lows.append(gather_rows(own_lows[-1]))
        mlp_gain_part = mlp_gain_part + jnp.sum(
            mlp_normed_grad * residuals[c] * inv_rms_mlps[c], axis=0, keepdims=True
        )

    grad_gate, grad_up, grad_down = [p.finish() for p in shared]
    grad_mlp_gain = sum_everywhere(mlp_gain_part, ("tensor", "dp"))[0]

    down_product = after(
        whole_order(
            [jnp.dot(h, w_down, preferred_element_type=f32).astype(bf16) for h in hiddens]
        ),
        *residual_lows,
    )
    block_scattered = scatter_sum(down_product)
    block_output = jnp.concatenate(residuals, axis=0) + block_scattered

    attended_plain = jnp.concatenate(
        whole_parts(jnp.dot(attended, query_spread.T, preferred_element_type=bf16)), axis=0
    )
    out_shared = SharedProduct(
        attended_plain, jnp.concatenate(residual_lows, axis=0), "dp", crossed
    )
    out_shared.meet()
    grad_out = out_shared.finish()
    attended_gradients = [
        jnp.dot(low_rows, w_out_spread.T, preferred_element_type=f32).astype(bf16)
        for low_rows in residual_lows
    ]
    query_grad, key_totals, value_totals = attend_back(
        joined, windows, firsts, low, attended, attended_gradients, logs, cosine, sine,
        kv_heads, group, rows, tile_rows,
    )
    received = []
    for distance in range(1, reach + 1):
        begin = (reach - distance) * stretch
        received.append(
            [
                from_behind(total[begin : begin + stretch].astype(bf16), "dp", -distance)
                for total in (key_totals, value_totals)
            ]
        )
    key_value_grad = gather_back(
        key_totals, value_totals, received, cosine, sine, kv_heads, stretch, rows
    )
    split = heads * LANES
    attn_normed_part = (
        jnp.dot(query_grad, w_joined[:, :split].T, preferred_element_type=f32)
        + jnp.dot(key_value_grad, w_joined[:, split:].T, preferred_element_type=f32)
    ).astype(bf16)
    query_plain = jnp.dot(query_grad, query_spread.T, preferred_element_type=bf16)
    kv_plain = jnp.dot(key_value_grad, kv_spread.T, preferred_element_type=bf16)
    query_shared = SharedProduct(attention_normed, query_plain, "dp", places)
    kv_shared = SharedProduct(attention_normed, kv_plain, "dp", crossed)
    attn_gain_part = (
        jnp.sum(
            attn_normed_part.astype(f32) * attention_normed.astype(f32), axis=0, keepdims=True
        )
        / attn_gain
    )
    attn_normed_grad = chain_scatter(
        attn_normed_part, "tensor",
        (
            [query_shared.sent, kv_shared.sent, attn_gain_part],
            [query_shared.meet(), kv_shared.meet()],
        ),
    )
    input_part = normalize_back(block_input, inv_rms_attn, attn_gain, attn_normed_grad)
    input_grad = jnp.concatenate(residual_grads, axis=0) + input_part
    grad_query = query_shared.finish()
    grad_key_value = kv_shared.finish()
    grad_key = grad_key_value[:, : kv_heads * HEAD_SIZE]
    grad_value = grad_key_value[:, kv_heads * HEAD_SIZE :]

    grad_attn_gain = sum_everywhere(attn_gain_part, ("tensor", "dp"))[0]
    return (
        block_output,
        input_grad,
        grad_query,
        grad_key,
        grad_value,
        grad_out,
        grad_gate,
        grad_up,
        grad_down,
        grad_attn_gain,
        grad_mlp_gain,
    )


def solution(mesh):
    in_specs = (
        P(("dp", "tensor"), None),
        P("dp"),
        P(),
        P(None, "tensor"),
        P(None, "tensor"),
        P(None, "tensor"),
        P("tensor", None),
        P(),
        P(None, "tensor"),
        P(None, "tensor"),
        P("tensor", None),
        P(("dp", "tensor"), None),
    )
    out_specs = (
        P(("dp", "tensor"), None),
        P(("dp", "tensor"), None),
        P(None, "tensor"),
        P(None, "tensor"),
        P(None, "tensor"),
        P("tensor", None),
        P(None, "tensor"),
        P(None, "tensor"),
        P("tensor", None),
        P(),
        P(),
    )

    return jax.shard_map(
        per_device, mesh=mesh, in_specs=in_specs, out_specs=out_specs, check_vma=False
    )
```

```python
import functools
import math

import jax
import jax.numpy as jnp
from jax import lax
from jax.experimental import pallas as pl
from jax.experimental.pallas import tpu as pltpu
from jax.sharding import PartitionSpec as P


HEAD_SIZE = 96
LONGEST_DOCUMENT = 2048

LANES = 128
HALF_LANES = LANES // 2
FAR = -1e30


epsilon = 1e-05
rope_base = 100000.0

f32 = jnp.float32
bf16 = jnp.bfloat16


def from_behind(value, axis, steps):
    count = lax.axis_size(axis)
    leading, last = (max(0, -steps), min(count, count - steps))
    return lax.ppermute(value, axis, [(source, source + steps) for source in range(leading, last)])


def exchange(value, axis, distance):
    count = lax.axis_size(axis)
    return lax.ppermute(value, axis, [(i, i ^ distance) for i in range(count)])


def rope_tables(positions):
    half_size = HEAD_SIZE // 2
    frequency = rope_base ** (-jnp.arange(half_size, dtype=f32) * 2.0 / HEAD_SIZE)
    rest = jnp.zeros((HALF_LANES - half_size,), f32)
    spread = jnp.concatenate([frequency, rest, frequency, rest])
    sign = jnp.where(jnp.arange(LANES) < HALF_LANES, -1.0, 1.0).astype(f32)
    angles = positions.astype(f32)[:, None] * spread[None, :]
    return (jnp.cos(angles), jnp.sin(angles) * sign[None, :])


def spread_matrix(heads, dtype=bf16):
    half_size = HEAD_SIZE // 2
    rows = jnp.arange(heads * HEAD_SIZE, dtype=jnp.int32)
    inner = rows % HEAD_SIZE
    lane = (rows // HEAD_SIZE) * LANES + jnp.where(
        inner < half_size, inner, inner - half_size + HALF_LANES
    )
    columns = jnp.arange(heads * LANES, dtype=jnp.int32)
    return (lane[:, None] == columns[None, :]).astype(dtype)


def normalize(rows, gain):
    inv_rms = lax.rsqrt(jnp.mean(rows * rows, axis=-1, keepdims=True) + epsilon)
    return ((rows * inv_rms * gain).astype(bf16), inv_rms)


def normalize_back(rows, inv_rms, gain, normed_grad):
    weighted = normed_grad * gain
    inner = jnp.mean(weighted * rows, axis=-1, keepdims=True)
    return inv_rms * weighted - rows * inv_rms**3 * inner


def turn(value, cosine, sine):
    return value * cosine + pltpu.roll(value, HALF_LANES, 1) * sine


def turn_back(value, cosine, sine):
    return value * cosine - pltpu.roll(value, HALF_LANES, 1) * sine


def project_kernel(rotated, rows_ref, weight_ref, cosine_ref, sine_ref, out_ref):
    product = jnp.dot(rows_ref[...], weight_ref[...], preferred_element_type=f32)
    cosine = cosine_ref[...]
    sine = sine_ref[...]
    for head in range(out_ref.shape[1] // LANES):
        part = product[:, head * LANES : (head + 1) * LANES]
        if head < rotated:
            part = turn(part, cosine, sine)
        out_ref[:, head * LANES : (head + 1) * LANES] = part.astype(bf16)


def project(rows, weight, cosine, sine, rotated, block):
    count, depth = rows.shape
    width = weight.shape[1]
    return pl.pallas_call(
        functools.partial(project_kernel, rotated),
        grid=(count // block,),
        in_specs=[
            pl.BlockSpec((block, depth), lambda i: (i, 0)),
            pl.BlockSpec((depth, width), lambda i: (0, 0)),
            pl.BlockSpec((block, LANES), lambda i: (i, 0)),
            pl.BlockSpec((block, LANES), lambda i: (i, 0)),
        ],
        out_specs=pl.BlockSpec((block, width), lambda i: (i, 0)),
        out_shape=jax.ShapeDtypeStruct((count, width), bf16),
        cost_estimate=pl.CostEstimate(
            flops=2 * count * depth * width,
            bytes_accessed=2 * (count * depth + depth * width + count * width),
            transcendentals=0,
        ),
        name="project",
    )(rows, weight, cosine, sine)


def pair_rows(ref, group):
    return jnp.concatenate([ref[:, h * LANES : (h + 1) * LANES] for h in range(group)], axis=0)


def place_row(ref, group):
    row = ref[0]
    return jnp.concatenate([row] * group, axis=1)


def masked(scores, first, last, base):
    index = lax.broadcasted_iota(jnp.int32, scores.shape, 0)
    allowed = (index >= first - base) & (index <= last - base)
    return jnp.where(allowed, scores, FAR)


def bounds(low_ref, query_block, rows, tile_rows, offset):
    high = (offset + (query_block + 1) * rows - 1) // tile_rows + 1
    return low_ref[query_block], high


def attend_kernel(tiles, group, factor, low_ref, query_ref, first_ref, *refs):
    keys = refs[:tiles]
    values = refs[tiles : 2 * tiles]
    out_ref, log_ref, key_window, value_turned, top, total, mixed = refs[2 * tiles :]
    query_block = pl.program_id(1)
    rows = query_ref.shape[0]
    stretch = keys[0].shape[0]
    tile_rows = key_window.shape[1]
    per_tile = stretch // tile_rows

    @pl.when(query_block == 0)
    def _():
        for tile in range(tiles):
            for part in range(per_tile):
                at = pl.ds(part * tile_rows, tile_rows)
                key_window[tile * per_tile + part] = keys[tile][at, :]
                value_turned[tile * per_tile + part] = values[tile][at, :].T

    offset = (tiles - 1) * stretch
    query = pair_rows(query_ref, group)
    first = place_row(first_ref, group)
    lane = lax.broadcasted_iota(jnp.int32, (1, rows), 1)
    last = jnp.concatenate([lane] * group, axis=1) + (offset + query_block * rows)
    top[...] = jnp.full_like(top, FAR)
    total[...] = jnp.zeros_like(total)
    mixed[...] = jnp.zeros_like(mixed)
    low, high = bounds(low_ref, query_block, rows, tile_rows, offset)

    def step(tile, unused):
        scores = lax.dot_general(
            key_window[tile], query, (((1,), (1,)), ((), ())), preferred_element_type=f32
        )
        scores = masked(scores, first, last, tile * tile_rows)
        before = top[...]
        after = jnp.maximum(before, jnp.max(scores, axis=0, keepdims=True))
        weights = jnp.exp2(scores * factor - after * factor)
        fade = jnp.exp2((before - after) * factor)
        top[...] = after
        total[...] = total[...] * fade + jnp.sum(weights, axis=0, keepdims=True)
        mixed[...] = mixed[...] * fade + jnp.dot(
            value_turned[tile], weights.astype(bf16), preferred_element_type=f32
        )
        return unused

    lax.fori_loop(low, high, step, 0)
    result = (mixed[...] / total[...]).T.astype(bf16)
    for head in range(group):
        out_ref[:, head * LANES : (head + 1) * LANES] = result[head * rows : (head + 1) * rows]
    log_ref[0, 0] = top[...] * factor + jnp.log2(total[...])


def window_specs(stretch, first_column):
    return [
        pl.BlockSpec((stretch, LANES), lambda g, i, *s, c=c: (0, c + g)) for c in first_column
    ]


def attend(queries_joined, windows, firsts, low, kv_heads, group, rows, tile_rows):
    stretch = queries_joined.shape[0]
    tiles = len(windows)
    blocks = stretch // rows
    pairs = group * rows
    window_tiles = tiles * stretch // tile_rows
    factor = HEAD_SIZE ** (-0.5) * math.log2(math.e)
    key_columns = [at for _, at in windows]
    value_columns = [at + kv_heads for _, at in windows]
    arrays = [a for a, _ in windows]
    grid_spec = pltpu.PrefetchScalarGridSpec(
        num_scalar_prefetch=1,
        grid=(kv_heads, blocks),
        in_specs=[
            pl.BlockSpec((rows, group * LANES), lambda g, i, *s: (i, g)),
            pl.BlockSpec((1, 1, rows), lambda g, i, *s: (i, 0, 0)),
        ]
        + window_specs(stretch, key_columns)
        + window_specs(stretch, value_columns),
        out_specs=[
            pl.BlockSpec((rows, group * LANES), lambda g, i, *s: (i, g)),
            pl.BlockSpec((1, 1, 1, pairs), lambda g, i, *s: (g, i, 0, 0)),
        ],
        scratch_shapes=[
            pltpu.VMEM((window_tiles, tile_rows, LANES), bf16),
            pltpu.VMEM((window_tiles, LANES, tile_rows), bf16),
            pltpu.VMEM((1, pairs), f32),
            pltpu.VMEM((1, pairs), f32),
            pltpu.VMEM((LANES, pairs), f32),
        ],
    )
    work = stretch * stretch * kv_heads * group
    return pl.pallas_call(
        functools.partial(attend_kernel, tiles, group, factor),
        grid_spec=grid_spec,
        out_shape=[
            jax.ShapeDtypeStruct((stretch, kv_heads * group * LANES), bf16),
            jax.ShapeDtypeStruct((kv_heads, blocks, 1, pairs), f32),
        ],
        cost_estimate=pl.CostEstimate(
            flops=16 * LANES * work, bytes_accessed=8 * stretch * stretch, transcendentals=work
        ),
        name="attend",
    )(low, queries_joined, firsts, *arrays, *arrays)


def attend_back_kernel(
    tiles, chunks, group, factor, scale, low_ref, slot_ref, query_ref, first_ref, *refs
):
    mixed_ref, log_ref, cosine_ref, sine_ref = refs[:4]
    grad_refs = refs[4 : 4 + chunks]
    refs = refs[4 + chunks :]
    keys = refs[:tiles]
    values = refs[tiles : 2 * tiles]
    (
        query_out,
        key_out,
        value_out,
        key_window,
        value_window,
        key_turned,
        query_total,
    ) = refs[2 * tiles :]
    query_block = pl.program_id(1)
    rows = query_ref.shape[0]
    stretch = keys[0].shape[0]
    tile_rows = key_window.shape[1]
    per_tile = stretch // tile_rows

    @pl.when(query_block == 0)
    def _():
        key_out[...] = jnp.zeros_like(key_out)
        value_out[...] = jnp.zeros_like(value_out)
        for tile in range(tiles):
            for part in range(per_tile):
                at = pl.ds(part * tile_rows, tile_rows)
                key_window[tile * per_tile + part] = keys[tile][at, :]
                key_turned[tile * per_tile + part] = keys[tile][at, :].T
                value_window[tile * per_tile + part] = values[tile][at, :]

    offset = (tiles - 1) * stretch
    query = pair_rows(query_ref, group)
    grad = jnp.concatenate(
        [ref[:, h * LANES : (h + 1) * LANES] for h in range(group) for ref in grad_refs], axis=0
    )
    mixed = pair_rows(mixed_ref, group)
    inner = jnp.sum((grad.astype(f32) * mixed.astype(f32)).T, axis=0, keepdims=True)
    log_total = log_ref[0, 0]
    first = place_row(first_ref, group)
    lane = lax.broadcasted_iota(jnp.int32, (1, rows), 1)
    last = jnp.concatenate([lane] * group, axis=1) + (offset + query_block * rows)
    query_total[...] = jnp.zeros_like(query_total)
    low, high = bounds(low_ref, query_block, rows, tile_rows, offset)
    both_last = (((1,), (1,)), ((), ()))

    def step(tile, unused):
        scores = lax.dot_general(key_window[tile], query, both_last, preferred_element_type=f32)
        scores = masked(scores, first, last, tile * tile_rows)
        weights = jnp.exp2(scores * factor - log_total)
        weight_grad = lax.dot_general(
            value_window[tile], grad, both_last, preferred_element_type=f32
        )
        score_grad = (weights * (weight_grad - inner) * scale).astype(bf16)
        at = pl.ds(pl.multiple_of(tile * tile_rows, tile_rows), tile_rows)
        value_out[at, :] += jnp.dot(weights.astype(bf16), grad, preferred_element_type=f32)
        key_out[at, :] += jnp.dot(score_grad, query, preferred_element_type=f32)
        query_total[...] += jnp.dot(key_turned[tile], score_grad, preferred_element_type=f32)
        return unused

    lax.fori_loop(low, high, step, 0)
    result = query_total[...].T
    for head in range(group):
        part = result[head * rows : (head + 1) * rows]
        query_out[:, head * LANES : (head + 1) * LANES] = turn_back(
            part, cosine_ref[...], sine_ref[...]
        ).astype(bf16)


def attend_back(
    queries_joined, windows, firsts, low, slots, mixed, grads, logs, cosine, sine,
    kv_heads, group, rows, tile_rows,
):
    stretch = queries_joined.shape[0]
    tiles = len(windows)
    blocks = stretch // rows
    pairs = group * rows
    window_tiles = tiles * stretch // tile_rows
    chunks = len(grads)
    scale = HEAD_SIZE ** (-0.5)
    factor = scale * math.log2(math.e)
    key_columns = [at for _, at in windows]
    value_columns = [at + kv_heads for _, at in windows]
    arrays = [a for a, _ in windows]
    heads_spec = pl.BlockSpec((rows, group * LANES), lambda g, i, *s: (i, g))
    table_spec = pl.BlockSpec((rows, LANES), lambda g, i, *s: (i, 0))
    total_spec = pl.BlockSpec((tiles * stretch, LANES), lambda g, i, *s: (0, g))
    grid_spec = pltpu.PrefetchScalarGridSpec(
        num_scalar_prefetch=2,
        grid=(kv_heads, blocks),
        in_specs=[
            heads_spec,
            pl.BlockSpec((1, 1, rows), lambda g, i, *s: (i, 0, 0)),
            heads_spec,
            pl.BlockSpec((1, 1, 1, pairs), lambda g, i, *s: (g, i, 0, 0)),
            table_spec,
            table_spec,
        ]
        + [
            pl.BlockSpec((rows // chunks, group * LANES), lambda g, i, low, slot: (slot[i], g))
        ]
        * chunks
        + window_specs(stretch, key_columns)
        + window_specs(stretch, value_columns),
        out_specs=[heads_spec, total_spec, total_spec],
        scratch_shapes=[
            pltpu.VMEM((window_tiles, tile_rows, LANES), bf16),
            pltpu.VMEM((window_tiles, tile_rows, LANES), bf16),
            pltpu.VMEM((window_tiles, LANES, tile_rows), bf16),
            pltpu.VMEM((LANES, pairs), f32),
        ],
    )
    work = stretch * stretch * kv_heads * group
    return pl.pallas_call(
        functools.partial(attend_back_kernel, tiles, chunks, group, factor, scale),
        grid_spec=grid_spec,
        out_shape=[
            jax.ShapeDtypeStruct((stretch, kv_heads * group * LANES), bf16),
            jax.ShapeDtypeStruct((tiles * stretch, kv_heads * LANES), f32),
            jax.ShapeDtypeStruct((tiles * stretch, kv_heads * LANES), f32),
        ],
        cost_estimate=pl.CostEstimate(
            flops=40 * LANES * work, bytes_accessed=16 * stretch * stretch, transcendentals=work
        ),
        name="attend_back",
    )(low, slots, queries_joined, firsts, mixed, logs, cosine, sine, *grads, *arrays, *arrays)


def gather_back_kernel(kv_heads, parts, key_ref, value_ref, cosine_ref, sine_ref, *refs):
    out_ref = refs[2 * parts]
    for head in range(kv_heads):
        at = pl.ds(head * LANES, LANES)
        key = key_ref[:, at]
        value = value_ref[:, at]
        for part in range(parts):
            key = key + refs[2 * part][:, at].astype(f32)
            value = value + refs[2 * part + 1][:, at].astype(f32)
        out_ref[:, at] = turn_back(key, cosine_ref[...], sine_ref[...]).astype(bf16)
        out_ref[:, pl.ds((kv_heads + head) * LANES, LANES)] = value.astype(bf16)


def gather_back(key_totals, value_totals, received, cosine, sine, kv_heads, stretch, block):
    skipped = key_totals.shape[0] // block - stretch // block
    width = kv_heads * LANES
    own = pl.BlockSpec((block, width), lambda i: (i + skipped, 0))
    other = pl.BlockSpec((block, width), lambda i: (i, 0))
    table = pl.BlockSpec((block, LANES), lambda i: (i, 0))
    flat = [array for pair in received for array in pair]
    return pl.pallas_call(
        functools.partial(gather_back_kernel, kv_heads, len(received)),
        grid=(stretch // block,),
        in_specs=[own, own, table, table] + [other] * len(flat),
        out_specs=pl.BlockSpec((block, 2 * width), lambda i: (i, 0)),
        out_shape=jax.ShapeDtypeStruct((stretch, 2 * width), bf16),
        name="gather_back",
    )(key_totals, value_totals, cosine, sine, *flat)


class SharedProduct:

    def __init__(self, left, right, axis, order):
        self.left, self.right, self.axis, self.order = left, right, axis, order
        self.size = left.shape[1] // 2
        self.sent = self.times(0, True).astype(bf16)

    def bit(self, place):
        return (lax.axis_index(self.axis) >> place) & 1

    def times(self, place, other):
        bit = self.bit(self.order[place])
        offset = ((1 - bit) if other else bit) * self.size
        part = lax.dynamic_slice_in_dim(self.left, offset, self.size, 1)
        return jnp.dot(part.T, self.right, preferred_element_type=f32)

    def meet(self):
        got = exchange(self.sent, self.axis, 1 << self.order[0])
        self.value = self.times(0, False) + got.astype(f32)
        self.down = list(self.order[1:])
        self.up = list(reversed(self.order))
        return self.value

    def step(self):
        if self.down:
            place = self.down.pop(0)
            bit = self.bit(place)
            size = self.value.shape[0] // 2
            sent = lax.dynamic_slice_in_dim(self.value, (1 - bit) * size, size, 0).astype(bf16)
            got = exchange(sent, self.axis, 1 << place)
            kept = lax.dynamic_slice_in_dim(self.value, bit * size, size, 0)
            self.value = kept + got.astype(f32)
            return self.value
        place = self.up.pop(0)
        whole = self.value.astype(bf16)
        got = exchange(whole, self.axis, 1 << place)
        self.value = jnp.where(
            self.bit(place) == 1,
            jnp.concatenate([got, whole], axis=0),
            jnp.concatenate([whole, got], axis=0),
        )
        return self.value

    def finish(self):
        while self.up:
            self.step()
        return self.value.astype(f32)


def sum_everywhere(value, axes):
    for axis in axes:
        count = lax.axis_size(axis)
        place = 1
        while place < count:
            value = value + exchange(value, axis, place)
            place *= 2
    return value


def scatter_sum(product):
    return lax.psum_scatter(
        product.astype(bf16), "tensor", scatter_dimension=0, tiled=True
    ).astype(f32)


class ChainSum:

    def __init__(self, piece, axis):
        self.piece, self.axis = piece, axis
        self.count = lax.axis_size(axis)
        self.step = 0
        self.right = self.left = None

    def outgoing(self):
        self.step += 1
        to_right = self.piece((self.count - self.step) % self.count)
        to_left = self.piece(self.step % self.count)
        if self.right is not None:
            to_right = to_right.astype(f32) + self.right.astype(f32)
            to_left = to_left.astype(f32) + self.left.astype(f32)
        return to_right.astype(bf16), to_left.astype(bf16)

    def send(self, to_right, to_left):
        count, step = self.count, self.step
        self.right = lax.ppermute(
            to_right, self.axis, [(i, i + 1) for i in range(min(step, count - 1))]
        )
        self.left = lax.ppermute(
            to_left, self.axis, [(i, i - 1) for i in range(max(count - step, 1), count)]
        )

    def result(self):
        return self.piece(0).astype(f32) + self.right.astype(f32) + self.left.astype(f32)


class ChainGather:

    def __init__(self, own, axis):
        self.own, self.axis = own, axis
        self.count = lax.axis_size(axis)
        self.step = 0
        self.from_left, self.from_right = [own], [own]

    def outgoing(self):
        self.step += 1
        return self.from_left[-1], self.from_right[-1]

    def send(self, to_right, to_left):
        count, step = self.count, self.step
        self.from_left.append(
            lax.ppermute(to_right, self.axis, [(i, i + 1) for i in range(step - 1, count - 1)])
        )
        self.from_right.append(
            lax.ppermute(to_left, self.axis, [(i, i - 1) for i in range(1, count - step + 1)])
        )

    def result(self):
        others = [
            self.from_right[d] + self.from_left[self.count - d] for d in range(1, self.count)
        ]
        return jnp.concatenate([self.own] + others, axis=0)


def hop(chains, fillers=()):
    values = [value for chain in chains for value in chain.outgoing()]
    values = lax.optimization_barrier(tuple(values) + tuple(fillers))[: 2 * len(chains)]
    for place, chain in enumerate(chains):
        chain.send(values[2 * place], values[2 * place + 1])


def run_chain(chain, fillers=()):
    for step in range(lax.axis_size(chain.axis) - 1):
        hop([chain], fillers[step - 1] if 0 < step <= len(fillers) else ())
    return chain.result()


def gather_rows(rows):
    return lax.all_gather(rows, "tensor", axis=0, tiled=True)


def after(value, *others):
    return lax.optimization_barrier((value,) + others)[0]


def per_device(
    block_input,
    positions,
    attn_gain,
    w_query,
    key_weight,
    value_weight,
    w_out,
    mlp_gain,
    w_gate,
    w_up,
    w_down,
    out_grad,
):
    stretch = positions.shape[0]
    reach = LONGEST_DOCUMENT // stretch
    heads = w_query.shape[1] // HEAD_SIZE
    kv_heads = key_weight.shape[1] // HEAD_SIZE
    group = heads // kv_heads
    rows = block_input.shape[0]
    tile_rows = min(512, stretch)
    blocks = stretch // rows
    chunks = 2
    part_rows = rows // chunks
    places = list(range((lax.axis_size("dp") - 1).bit_length()))
    crossed = places[:1] + places[:0:-1]

    here = lax.axis_index("tensor")
    devices = lax.axis_size("tensor")
    hops = devices - 1
    slots = lax.rem(jnp.arange(devices, dtype=jnp.int32) + devices - here, devices)

    def own_parts(value):
        return [value[c * part_rows : (c + 1) * part_rows] for c in range(chunks)]

    def piece_of(value, c, d):
        start = lax.rem(here + d, devices) * rows + c * part_rows
        return lax.dynamic_slice_in_dim(value, start, part_rows, 0)

    def turned_part(value, c):
        return jnp.concatenate([piece_of(value, c, d) for d in range(devices)], axis=0)

    def in_order(parts):
        pieces = [
            lax.dynamic_slice_in_dim(part, slots[t] * part_rows, part_rows, 0)
            for t in range(devices)
            for part in parts
        ]
        return jnp.concatenate(pieces, axis=0)

    normed_own, inv_rms_attn = normalize(block_input, attn_gain)
    attention_normed = gather_rows(normed_own)
    out_low = gather_rows(after(out_grad.astype(bf16), attention_normed))

    query_spread = spread_matrix(heads)
    kv_spread = spread_matrix(2 * kv_heads)
    all_spread = spread_matrix(heads + 2 * kv_heads)
    w_joined = jnp.dot(
        jnp.concatenate([w_query, key_weight, value_weight], axis=1), all_spread,
        preferred_element_type=bf16,
    )
    w_out_spread = jnp.dot(query_spread.T, w_out, preferred_element_type=bf16)
    cosine, sine = rope_tables(positions)
    local = jnp.arange(stretch, dtype=jnp.int32)
    window_first = reach * stretch + local - positions
    firsts = window_first.reshape(blocks, 1, rows)
    low = jnp.min(window_first.reshape(blocks, rows), axis=1) // tile_rows

    joined = project(attention_normed, w_joined, cosine, sine, heads + kv_heads, rows)
    key_value = joined[:, heads * LANES :]
    windows = [(from_behind(key_value, "dp", d), 0) for d in range(reach, 0, -1)]
    windows = windows + [(joined, heads)]
    attended, logs = attend(joined, windows, firsts, low, kv_heads, group, rows, tile_rows)

    mixed_product = jnp.dot(attended, w_out_spread, preferred_element_type=f32).astype(bf16)
    inputs = own_parts(block_input)
    cotangents = own_parts(out_grad)
    residuals, inv_rms_mlps = {}, {}
    normed_mlps, out_parts, hidden_grads, gate_pres, up_projs = {}, {}, {}, {}, {}
    hiddens, gate_grads, up_grads = {}, {}, {}
    residual_grads, residual_lows, gain_parts = {}, {}, {}
    scatter_out, gather_mlp, scatter_mlp, gather_low = {}, {}, {}, {}
    shared = []

    def begin_scatter_out(c):
        scatter_out[c] = ChainSum(lambda d: piece_of(mixed_product, c, d), "tensor")
        return scatter_out[c]

    def begin_gather_mlp(c):
        residuals[c] = inputs[c] + scatter_out[c].result()
        own, inv_rms_mlps[c] = normalize(residuals[c], mlp_gain)
        gather_mlp[c] = ChainGather(own, "tensor")
        return gather_mlp[c]

    def back_product(c):
        out_parts[c] = turned_part(out_low, c)
        hidden_grads[c] = jnp.dot(out_parts[c], w_down.T, preferred_element_type=f32)
        return (hidden_grads[c],)

    def hidden_products(c):
        normed_mlps[c] = gather_mlp[c].result()
        gate_pres[c] = jnp.dot(normed_mlps[c], w_gate, preferred_element_type=f32)
        up_projs[c] = jnp.dot(normed_mlps[c], w_up, preferred_element_type=f32)
        return (gate_pres[c], up_projs[c])

    def begin_scatter_mlp(c):
        gate_pre, up_proj, hidden_grad = gate_pres[c], up_projs[c], hidden_grads[c]
        sigmoid_gate = jax.nn.sigmoid(gate_pre)
        silu_gate = gate_pre * sigmoid_gate
        hiddens[c] = (silu_gate * up_proj).astype(bf16)
        gate_grads[c] = (
            hidden_grad * up_proj * sigmoid_gate * (1.0 + gate_pre * (1.0 - sigmoid_gate))
        ).astype(bf16)
        up_grads[c] = (hidden_grad * silu_gate).astype(bf16)
        product = (
            jnp.dot(gate_grads[c], w_gate.T, preferred_element_type=f32)
            + jnp.dot(up_grads[c], w_up.T, preferred_element_type=f32)
        ).astype(bf16)
        scatter_mlp[c] = ChainSum(
            lambda d: product[d * part_rows : (d + 1) * part_rows], "tensor"
        )
        return scatter_mlp[c]

    def begin_gather_low(c):
        normed_grad = scatter_mlp[c].result()
        part = normalize_back(residuals[c], inv_rms_mlps[c], mlp_gain, normed_grad)
        residual_grads[c] = cotangents[c] + part
        gain_parts[c] = jnp.sum(
            normed_grad * residuals[c] * inv_rms_mlps[c], axis=0, keepdims=True
        )
        gather_low[c] = ChainGather(residual_grads[c].astype(bf16), "tensor")
        return gather_low[c]

    def joined_parts(parts):
        return jnp.concatenate([parts[c] for c in range(chunks)], axis=0)

    def share_halves():
        normed_joined = joined_parts(normed_mlps)
        shared.append(SharedProduct(normed_joined, joined_parts(gate_grads), "dp", places))
        shared.append(SharedProduct(normed_joined, joined_parts(up_grads), "dp", crossed))
        shared.append(
            SharedProduct(joined_parts(hiddens), joined_parts(out_parts), "dp", places)
        )
        return [p.sent for p in shared]

    plan = [
        (0, begin_scatter_out, 0),
        (hops, begin_scatter_out, 1),
        (hops, begin_gather_mlp, 0),
        (2 * hops, begin_gather_mlp, 1),
        (2 * hops + 2, begin_scatter_mlp, 0),
        (3 * hops + 2, begin_scatter_mlp, 1),
        (3 * hops + 2, begin_gather_low, 0),
        (4 * hops + 2, begin_gather_low, 1),
    ]
    between = {
        hops + 1: lambda: back_product(0),
        hops + 2: lambda: back_product(1),
        2 * hops + 1: lambda: hidden_products(0),
        3 * hops + 1: lambda: hidden_products(1),
        3 * hops + 3: share_halves,
        3 * hops + 4: lambda: [p.meet() for p in shared],
        5 * hops + 1: lambda: [p.step() for p in shared],
    }
    running = []
    for moment in range(5 * hops + 2):
        fillers = between[moment]() if moment in between else ()
        running = [chain for chain in running if chain.step < hops]
        running = running + [begin(c) for start, begin, c in plan if start == moment]
        hop(running, fillers)
    for c in range(chunks):
        residual_lows[c] = gather_low[c].result()

    grad_mlp_gain = sum_everywhere(gain_parts[0] + gain_parts[1], ("tensor", "dp"))[0]

    down_product = in_order(
        [
            jnp.dot(hiddens[c], w_down, preferred_element_type=f32).astype(bf16)
            for c in range(chunks)
        ]
    )
    down_product, residual_lows = lax.optimization_barrier((down_product, residual_lows))
    block_scattered = scatter_sum(down_product)
    block_output = joined_parts(residuals) + block_scattered

    attended_gradients = [
        jnp.dot(residual_lows[c], w_out_spread.T, preferred_element_type=f32).astype(bf16)
        for c in range(chunks)
    ]
    query_grad, key_totals, value_totals = attend_back(
        joined, windows, firsts, low, slots, attended, attended_gradients, logs, cosine,
        sine, kv_heads, group, rows, tile_rows,
    )
    received = []
    for distance in range(1, reach + 1):
        begin = (reach - distance) * stretch
        received.append(
            [
                from_behind(total[begin : begin + stretch].astype(bf16), "dp", -distance)
                for total in (key_totals, value_totals)
            ]
        )
    shared[2].step()
    shared[2].value, received = lax.optimization_barrier((shared[2].value, received))
    grad_gate, grad_up, grad_down = [p.finish() for p in shared]
    attended_plain = jnp.dot(
        after(attended, key_totals), query_spread.T, preferred_element_type=bf16
    )
    out_shared = SharedProduct(
        jnp.concatenate([turned_part(attended_plain, c) for c in range(chunks)], axis=0),
        joined_parts(residual_lows), "dp", crossed,
    )
    key_value_grad = gather_back(
        key_totals, value_totals, received, cosine, sine, kv_heads, stretch, rows
    )
    split = heads * LANES
    attn_normed_part = (
        jnp.dot(query_grad, w_joined[:, :split].T, preferred_element_type=f32)
        + jnp.dot(key_value_grad, w_joined[:, split:].T, preferred_element_type=f32)
    ).astype(bf16)
    query_plain = jnp.dot(query_grad, query_spread.T, preferred_element_type=bf16)
    kv_plain = jnp.dot(key_value_grad, kv_spread.T, preferred_element_type=bf16)
    query_shared = SharedProduct(attention_normed, query_plain, "dp", places)
    kv_shared = SharedProduct(attention_normed, kv_plain, "dp", crossed)
    attn_gain_part = (
        jnp.sum(
            attn_normed_part.astype(f32) * attention_normed.astype(f32), axis=0, keepdims=True
        )
        / attn_gain
    )
    small = (query_shared, kv_shared, out_shared)
    attn_normed_grad = run_chain(
        ChainSum(
            lambda d: lax.dynamic_slice_in_dim(
                attn_normed_part, lax.rem(here + d, devices) * rows, rows, 0
            ),
            "tensor",
        ),
        ([p.sent for p in small] + [attn_gain_part], [p.meet() for p in small]),
    )
    input_part = normalize_back(block_input, inv_rms_attn, attn_gain, attn_normed_grad)
    input_grad = joined_parts(residual_grads) + input_part
    grad_query = query_shared.finish()
    grad_key_value = kv_shared.finish()
    grad_out = out_shared.finish()
    grad_key = grad_key_value[:, : kv_heads * HEAD_SIZE]
    grad_value = grad_key_value[:, kv_heads * HEAD_SIZE :]

    grad_attn_gain = sum_everywhere(attn_gain_part, ("tensor", "dp"))[0]
    return (
        block_output,
        input_grad,
        grad_query,
        grad_key,
        grad_value,
        grad_out,
        grad_gate,
        grad_up,
        grad_down,
        grad_attn_gain,
        grad_mlp_gain,
    )


def solution(mesh):
    in_specs = (
        P(("dp", "tensor"), None),
        P("dp"),
        P(),
        P(None, "tensor"),
        P(None, "tensor"),
        P(None, "tensor"),
        P("tensor", None),
        P(),
        P(None, "tensor"),
        P(None, "tensor"),
        P("tensor", None),
        P(("dp", "tensor"), None),
    )
    out_specs = (
        P(("dp", "tensor"), None),
        P(("dp", "tensor"), None),
        P(None, "tensor"),
        P(None, "tensor"),
        P(None, "tensor"),
        P("tensor", None),
        P(None, "tensor"),
        P(None, "tensor"),
        P("tensor", None),
        P(),
        P(),
    )

    return jax.shard_map(
        per_device, mesh=mesh, in_specs=in_specs, out_specs=out_specs, check_vma=False
    )
```

```python
import functools
import math

import jax
import jax.numpy as jnp
from jax import lax
from jax.experimental import pallas as pl
from jax.experimental.pallas import tpu as pltpu
from jax.sharding import PartitionSpec as P


HEAD_SIZE = 96
LONGEST_DOCUMENT = 2048

LANES = 128
HALF_LANES = LANES // 2
FAR = -1e30


epsilon = 1e-05
rope_base = 100000.0

f32 = jnp.float32
bf16 = jnp.bfloat16


def from_behind(value, axis, steps):
    if steps == 0:
        return value
    count = lax.axis_size(axis)
    leading, last = (max(0, -steps), min(count, count - steps))
    return lax.ppermute(value, axis, [(source, source + steps) for source in range(leading, last)])


def exchange(value, axis, distance):
    count = lax.axis_size(axis)
    return lax.ppermute(value, axis, [(i, i ^ distance) for i in range(count)])


def rope_tables(positions):
    half_size = HEAD_SIZE // 2
    frequency = rope_base ** (-jnp.arange(half_size, dtype=f32) * 2.0 / HEAD_SIZE)
    rest = jnp.zeros((HALF_LANES - half_size,), f32)
    spread = jnp.concatenate([frequency, rest, frequency, rest])
    sign = jnp.where(jnp.arange(LANES) < HALF_LANES, -1.0, 1.0).astype(f32)
    angles = positions.astype(f32)[:, None] * spread[None, :]
    return (jnp.cos(angles), jnp.sin(angles) * sign[None, :])


def spread_matrix(heads, gap_after=0, gap=0, dtype=bf16):
    half_size = HEAD_SIZE // 2
    rows = jnp.arange(heads * HEAD_SIZE, dtype=jnp.int32)
    inner = rows % HEAD_SIZE
    lane = (rows // HEAD_SIZE) * LANES + jnp.where(
        inner < half_size, inner, inner - half_size + HALF_LANES
    )
    if gap:
        cut = gap_after * HEAD_SIZE
        lane = jnp.concatenate([lane[:cut], jnp.full((gap,), -1, jnp.int32), lane[cut:]])
    columns = jnp.arange(heads * LANES, dtype=jnp.int32)
    return (lane[:, None] == columns[None, :]).astype(dtype)


def normalize(rows, gain):
    inv_rms = lax.rsqrt(jnp.mean(rows * rows, axis=-1, keepdims=True) + epsilon)
    return ((rows * inv_rms * gain).astype(bf16), inv_rms)


def normalize_back(rows, inv_rms, gain, normed_grad):
    weighted = normed_grad * gain
    inner = jnp.mean(weighted * rows, axis=-1, keepdims=True)
    return inv_rms * weighted - rows * inv_rms**3 * inner


def turn(value, cosine, sine):
    return value * cosine + pltpu.roll(value, HALF_LANES, 1) * sine


def turn_back(value, cosine, sine):
    return value * cosine - pltpu.roll(value, HALF_LANES, 1) * sine


def project_kernel(rotated, rows_ref, weight_ref, cosine_ref, sine_ref, *out_refs):
    product = jnp.dot(rows_ref[...], weight_ref[...], preferred_element_type=f32)
    cosine = cosine_ref[...]
    sine = sine_ref[...]
    head = 0
    for out_ref in out_refs:
        for place in range(out_ref.shape[1] // LANES):
            part = product[:, head * LANES : (head + 1) * LANES]
            if head < rotated:
                part = turn(part, cosine, sine)
            out_ref[:, place * LANES : (place + 1) * LANES] = part.astype(bf16)
            head += 1


def project(rows, weight, cosine, sine, rotated, widths, block):
    count, depth = rows.shape
    width = weight.shape[1]
    return pl.pallas_call(
        functools.partial(project_kernel, rotated),
        grid=(count // block,),
        in_specs=[
            pl.BlockSpec((block, depth), lambda i: (i, 0)),
            pl.BlockSpec((depth, width), lambda i: (0, 0)),
            pl.BlockSpec((block, LANES), lambda i: (i, 0)),
            pl.BlockSpec((block, LANES), lambda i: (i, 0)),
        ],
        out_specs=[pl.BlockSpec((block, part), lambda i: (i, 0)) for part in widths],
        out_shape=[jax.ShapeDtypeStruct((count, part), bf16) for part in widths],
        cost_estimate=pl.CostEstimate(
            flops=2 * count * depth * width,
            bytes_accessed=2 * (count * depth + depth * width + count * width),
            transcendentals=0,
        ),
        name="project",
    )(rows, weight, cosine, sine)


def pair_rows(ref, group):
    return jnp.concatenate([ref[:, h * LANES : (h + 1) * LANES] for h in range(group)], axis=0)


def place_row(ref, group):
    row = ref[0]
    return jnp.concatenate([row] * group, axis=1)


def masked(scores, first, last, base):
    index = lax.broadcasted_iota(jnp.int32, scores.shape, 0)
    allowed = (index >= first - base) & (index <= last - base)
    return jnp.where(allowed, scores, FAR)


def bounds(low_ref, query_block, rows, tile_rows, offset):
    high = (offset + (query_block + 1) * rows - 1) // tile_rows + 1
    return low_ref[query_block], high


def attend_kernel(tiles, group, factor, low_ref, query_ref, first_ref, *refs):
    keys = refs[:tiles]
    values = refs[tiles : 2 * tiles]
    out_ref, log_ref, key_window, value_turned, top, total, mixed = refs[2 * tiles :]
    query_block = pl.program_id(1)
    rows = query_ref.shape[0]
    stretch = keys[0].shape[0]
    tile_rows = key_window.shape[1]
    per_tile = stretch // tile_rows

    @pl.when(query_block == 0)
    def _():
        for tile in range(tiles):
            for part in range(per_tile):
                at = pl.ds(part * tile_rows, tile_rows)
                key_window[tile * per_tile + part] = keys[tile][at, :]
                value_turned[tile * per_tile + part] = values[tile][at, :].T

    offset = (tiles - 1) * stretch
    query = pair_rows(query_ref, group)
    first = place_row(first_ref, group)
    lane = lax.broadcasted_iota(jnp.int32, (1, rows), 1)
    last = jnp.concatenate([lane] * group, axis=1) + (offset + query_block * rows)
    top[...] = jnp.full_like(top, FAR)
    total[...] = jnp.zeros_like(total)
    mixed[...] = jnp.zeros_like(mixed)
    low, high = bounds(low_ref, query_block, rows, tile_rows, offset)

    def step(tile, unused):
        scores = lax.dot_general(
            key_window[tile], query, (((1,), (1,)), ((), ())), preferred_element_type=f32
        )
        scores = masked(scores, first, last, tile * tile_rows)
        before = top[...]
        after = jnp.maximum(before, jnp.max(scores, axis=0, keepdims=True))
        weights = jnp.exp2(scores * factor - after * factor)
        fade = jnp.exp2((before - after) * factor)
        top[...] = after
        total[...] = total[...] * fade + jnp.sum(weights, axis=0, keepdims=True)
        mixed[...] = mixed[...] * fade + jnp.dot(
            value_turned[tile], weights.astype(bf16), preferred_element_type=f32
        )
        return unused

    lax.fori_loop(low, high, step, 0)
    result = (mixed[...] / total[...]).T.astype(bf16)
    for head in range(group):
        out_ref[:, head * LANES : (head + 1) * LANES] = result[head * rows : (head + 1) * rows]
    log_ref[0, 0] = top[...] * factor + jnp.log2(total[...])


def window_specs(stretch, first_column):
    return [
        pl.BlockSpec((stretch, LANES), lambda g, i, *s, c=c: (0, c + g)) for c in first_column
    ]


def attend(queries_joined, windows, firsts, low, kv_heads, group, rows, tile_rows):
    stretch = queries_joined.shape[0]
    tiles = len(windows)
    blocks = stretch // rows
    pairs = group * rows
    window_tiles = tiles * stretch // tile_rows
    factor = HEAD_SIZE ** (-0.5) * math.log2(math.e)
    key_columns = [at for _, at in windows]
    value_columns = [at + kv_heads for _, at in windows]
    arrays = [a for a, _ in windows]
    grid_spec = pltpu.PrefetchScalarGridSpec(
        num_scalar_prefetch=1,
        grid=(kv_heads, blocks),
        in_specs=[
            pl.BlockSpec((rows, group * LANES), lambda g, i, *s: (i, g)),
            pl.BlockSpec((1, 1, rows), lambda g, i, *s: (i, 0, 0)),
        ]
        + window_specs(stretch, key_columns)
        + window_specs(stretch, value_columns),
        out_specs=[
            pl.BlockSpec((rows, group * LANES), lambda g, i, *s: (i, g)),
            pl.BlockSpec((1, 1, 1, pairs), lambda g, i, *s: (g, i, 0, 0)),
        ],
        scratch_shapes=[
            pltpu.VMEM((window_tiles, tile_rows, LANES), bf16),
            pltpu.VMEM((window_tiles, LANES, tile_rows), bf16),
            pltpu.VMEM((1, pairs), f32),
            pltpu.VMEM((1, pairs), f32),
            pltpu.VMEM((LANES, pairs), f32),
        ],
    )
    work = stretch * stretch * kv_heads * group
    return pl.pallas_call(
        functools.partial(attend_kernel, tiles, group, factor),
        grid_spec=grid_spec,
        out_shape=[
            jax.ShapeDtypeStruct((stretch, kv_heads * group * LANES), bf16),
            jax.ShapeDtypeStruct((kv_heads, blocks, 1, pairs), f32),
        ],
        cost_estimate=pl.CostEstimate(
            flops=16 * LANES * work, bytes_accessed=8 * stretch * stretch, transcendentals=work
        ),
        name="attend",
    )(low, queries_joined, firsts, *arrays, *arrays)


def attend_back_kernel(
    tiles, chunks, group, factor, scale, low_ref, slot_ref, query_ref, first_ref, *refs
):
    mixed_ref, log_ref, cosine_ref, sine_ref = refs[:4]
    grad_refs = refs[4 : 4 + chunks]
    refs = refs[4 + chunks :]
    keys = refs[:tiles]
    values = refs[tiles : 2 * tiles]
    (
        query_out,
        key_own,
        value_own,
        earlier_out,
        key_out,
        value_out,
        key_window,
        value_window,
        key_turned,
        query_total,
    ) = refs[2 * tiles :]
    query_block = pl.program_id(1)
    rows = query_ref.shape[0]
    stretch = keys[0].shape[0]
    tile_rows = key_window.shape[1]
    per_tile = stretch // tile_rows

    @pl.when(query_block == 0)
    def _():
        key_out[...] = jnp.zeros_like(key_out)
        value_out[...] = jnp.zeros_like(value_out)
        for tile in range(tiles):
            for part in range(per_tile):
                at = pl.ds(part * tile_rows, tile_rows)
                key_window[tile * per_tile + part] = keys[tile][at, :]
                key_turned[tile * per_tile + part] = keys[tile][at, :].T
                value_window[tile * per_tile + part] = values[tile][at, :]

    offset = (tiles - 1) * stretch
    query = pair_rows(query_ref, group)
    grad = jnp.concatenate(
        [ref[:, h * LANES : (h + 1) * LANES] for h in range(group) for ref in grad_refs], axis=0
    )
    mixed = pair_rows(mixed_ref, group)
    inner = jnp.sum((grad.astype(f32) * mixed.astype(f32)).T, axis=0, keepdims=True)
    log_total = log_ref[0, 0]
    first = place_row(first_ref, group)
    lane = lax.broadcasted_iota(jnp.int32, (1, rows), 1)
    last = jnp.concatenate([lane] * group, axis=1) + (offset + query_block * rows)
    query_total[...] = jnp.zeros_like(query_total)
    low, high = bounds(low_ref, query_block, rows, tile_rows, offset)
    both_last = (((1,), (1,)), ((), ()))

    def step(tile, unused):
        scores = lax.dot_general(key_window[tile], query, both_last, preferred_element_type=f32)
        scores = masked(scores, first, last, tile * tile_rows)
        weights = jnp.exp2(scores * factor - log_total)
        weight_grad = lax.dot_general(
            value_window[tile], grad, both_last, preferred_element_type=f32
        )
        score_grad = (weights * (weight_grad - inner) * scale).astype(bf16)
        at = pl.ds(pl.multiple_of(tile * tile_rows, tile_rows), tile_rows)
        value_out[at, :] += jnp.dot(weights.astype(bf16), grad, preferred_element_type=f32)
        key_out[at, :] += jnp.dot(score_grad, query, preferred_element_type=f32)
        query_total[...] += jnp.dot(key_turned[tile], score_grad, preferred_element_type=f32)
        return unused

    lax.fori_loop(low, high, step, 0)
    result = query_total[...].T
    for head in range(group):
        part = result[head * rows : (head + 1) * rows]
        query_out[:, head * LANES : (head + 1) * LANES] = turn_back(
            part, cosine_ref[...], sine_ref[...]
        ).astype(bf16)

    @pl.when(query_block == pl.num_programs(1) - 1)
    def _():
        for tile in range(tiles - 1):
            at = pl.ds(tile * stretch, stretch)
            earlier_out[tile, 0] = key_out[at, :].astype(bf16)
            earlier_out[tile, 1] = value_out[at, :].astype(bf16)
        key_own[...] = key_out[pl.ds(offset, stretch), :]
        value_own[...] = value_out[pl.ds(offset, stretch), :]


def attend_back(
    queries_joined, windows, firsts, low, slots, mixed, grads, logs, cosine, sine,
    kv_heads, group, rows, tile_rows,
):
    stretch = queries_joined.shape[0]
    tiles = len(windows)
    blocks = stretch // rows
    pairs = group * rows
    window_tiles = tiles * stretch // tile_rows
    chunks = len(grads)
    scale = HEAD_SIZE ** (-0.5)
    factor = scale * math.log2(math.e)
    key_columns = [at for _, at in windows]
    value_columns = [at + kv_heads for _, at in windows]
    arrays = [a for a, _ in windows]
    heads_spec = pl.BlockSpec((rows, group * LANES), lambda g, i, *s: (i, g))
    table_spec = pl.BlockSpec((rows, LANES), lambda g, i, *s: (i, 0))
    own_spec = pl.BlockSpec((stretch, LANES), lambda g, i, *s: (0, g))
    earlier_spec = pl.BlockSpec((tiles - 1, 2, stretch, LANES), lambda g, i, *s: (0, 0, 0, g))
    grid_spec = pltpu.PrefetchScalarGridSpec(
        num_scalar_prefetch=2,
        grid=(kv_heads, blocks),
        in_specs=[
            heads_spec,
            pl.BlockSpec((1, 1, rows), lambda g, i, *s: (i, 0, 0)),
            heads_spec,
            pl.BlockSpec((1, 1, 1, pairs), lambda g, i, *s: (g, i, 0, 0)),
            table_spec,
            table_spec,
        ]
        + [
            pl.BlockSpec((rows // chunks, group * LANES), lambda g, i, low, slot: (slot[i], g))
        ]
        * chunks
        + window_specs(stretch, key_columns)
        + window_specs(stretch, value_columns),
        out_specs=[heads_spec, own_spec, own_spec, earlier_spec],
        scratch_shapes=[
            pltpu.VMEM((tiles * stretch, LANES), f32),
            pltpu.VMEM((tiles * stretch, LANES), f32),
            pltpu.VMEM((window_tiles, tile_rows, LANES), bf16),
            pltpu.VMEM((window_tiles, tile_rows, LANES), bf16),
            pltpu.VMEM((window_tiles, LANES, tile_rows), bf16),
            pltpu.VMEM((LANES, pairs), f32),
        ],
    )
    work = stretch * stretch * kv_heads * group
    return pl.pallas_call(
        functools.partial(attend_back_kernel, tiles, chunks, group, factor, scale),
        grid_spec=grid_spec,
        out_shape=[
            jax.ShapeDtypeStruct((stretch, kv_heads * group * LANES), bf16),
            jax.ShapeDtypeStruct((stretch, kv_heads * LANES), f32),
            jax.ShapeDtypeStruct((stretch, kv_heads * LANES), f32),
            jax.ShapeDtypeStruct((tiles - 1, 2, stretch, kv_heads * LANES), bf16),
        ],
        cost_estimate=pl.CostEstimate(
            flops=40 * LANES * work, bytes_accessed=16 * stretch * stretch, transcendentals=work
        ),
        name="attend_back",
    )(low, slots, queries_joined, firsts, mixed, logs, cosine, sine, *grads, *arrays, *arrays)


def gather_back_kernel(kv_heads, parts, key_ref, value_ref, cosine_ref, sine_ref, *refs):
    out_ref = refs[parts]
    for head in range(kv_heads):
        at = pl.ds(head * LANES, LANES)
        key = key_ref[:, at]
        value = value_ref[:, at]
        for part in range(parts):
            key = key + refs[part][0, :, at].astype(f32)
            value = value + refs[part][1, :, at].astype(f32)
        out_ref[:, at] = turn_back(key, cosine_ref[...], sine_ref[...]).astype(bf16)
        out_ref[:, pl.ds((kv_heads + head) * LANES, LANES)] = value.astype(bf16)


def gather_back(key_totals, value_totals, received, cosine, sine, kv_heads, stretch, block):
    width = kv_heads * LANES
    own = pl.BlockSpec((block, width), lambda i: (i, 0))
    other = pl.BlockSpec((2, block, width), lambda i: (0, i, 0))
    table = pl.BlockSpec((block, LANES), lambda i: (i, 0))
    return pl.pallas_call(
        functools.partial(gather_back_kernel, kv_heads, len(received)),
        grid=(stretch // block,),
        in_specs=[own, own, table, table] + [other] * len(received),
        out_specs=pl.BlockSpec((block, 2 * width), lambda i: (i, 0)),
        out_shape=jax.ShapeDtypeStruct((stretch, 2 * width), bf16),
        name="gather_back",
    )(key_totals, value_totals, cosine, sine, *received)


class SharedProduct:

    def __init__(self, left, right, axis, order):
        self.left, self.right, self.axis, self.order = left, right, axis, order
        self.size = left.shape[1] // 2
        self.sent = self.times(0, True).astype(bf16)

    def bit(self, place):
        return (lax.axis_index(self.axis) >> place) & 1

    def times(self, place, other):
        bit = self.bit(self.order[place])
        offset = ((1 - bit) if other else bit) * self.size
        part = lax.dynamic_slice_in_dim(self.left, offset, self.size, 1)
        return jnp.dot(part.T, self.right, preferred_element_type=f32)

    def meet(self):
        got = exchange(self.sent, self.axis, 1 << self.order[0])
        self.value = self.times(0, False) + got.astype(f32)
        self.down = list(self.order[1:])
        self.up = list(reversed(self.order))
        return self.value

    def step(self):
        if self.down:
            place = self.down.pop(0)
            bit = self.bit(place)
            size = self.value.shape[0] // 2
            sent = lax.dynamic_slice_in_dim(self.value, (1 - bit) * size, size, 0).astype(bf16)
            got = exchange(sent, self.axis, 1 << place)
            kept = lax.dynamic_slice_in_dim(self.value, bit * size, size, 0)
            self.value = kept + got.astype(f32)
            return self.value
        place = self.up.pop(0)
        whole = self.value.astype(bf16)
        got = exchange(whole, self.axis, 1 << place)
        self.value = jnp.where(
            self.bit(place) == 1,
            jnp.concatenate([got, whole], axis=0),
            jnp.concatenate([whole, got], axis=0),
        )
        return self.value

    def finish(self):
        while self.up:
            self.step()
        return self.value


def sum_everywhere(value, axes):
    for axis in axes:
        count = lax.axis_size(axis)
        place = 1
        while place < count:
            value = value + exchange(value, axis, place)
            place *= 2
    return value


def scatter_low(product):
    return lax.psum_scatter(product.astype(bf16), "tensor", scatter_dimension=0, tiled=True)


def gather_rows(rows):
    return lax.all_gather(rows, "tensor", axis=0, tiled=True)


def per_device(
    block_input,
    positions,
    attn_gain,
    w_query,
    key_weight,
    value_weight,
    w_out,
    mlp_gain,
    w_gate,
    w_up,
    w_down,
    out_grad,
):
    stretch = positions.shape[0]
    reach = LONGEST_DOCUMENT // stretch
    heads = w_query.shape[1] // HEAD_SIZE
    kv_heads = key_weight.shape[1] // HEAD_SIZE
    group = heads // kv_heads
    rows = min(256, stretch)
    tile_rows = min(512, stretch)
    blocks = stretch // rows
    places = list(range((lax.axis_size("dp") - 1).bit_length()))
    crossed = places[:1] + places[:0:-1]
    tied = lax.optimization_barrier

    normed_own, inv_rms_attn = normalize(block_input, attn_gain)
    attention_normed = gather_rows(normed_own)
    out_low = gather_rows(out_grad.astype(bf16))

    query_spread = spread_matrix(heads)
    gap = -kv_heads * HEAD_SIZE % LANES
    kv_spread = spread_matrix(2 * kv_heads, kv_heads, gap)
    all_spread = spread_matrix(heads + 2 * kv_heads)
    w_joined = jnp.dot(
        jnp.concatenate([w_query, key_weight, value_weight], axis=1), all_spread,
        preferred_element_type=bf16,
    )
    w_out_spread = jnp.dot(query_spread.T, w_out, preferred_element_type=bf16)
    w_pair = jnp.concatenate([w_gate, w_up], axis=1)
    cosine, sine = rope_tables(positions)
    local = jnp.arange(stretch, dtype=jnp.int32)
    window_first = reach * stretch + local - positions
    firsts = window_first.reshape(blocks, 1, rows)
    low = jnp.min(window_first.reshape(blocks, rows), axis=1) // tile_rows

    queries, key_value = project(
        attention_normed, w_joined, cosine, sine, heads + kv_heads,
        (heads * LANES, 2 * kv_heads * LANES), rows,
    )
    windows = [(from_behind(key_value, "dp", d), 0) for d in range(reach, -1, -1)]
    attended, logs = attend(queries, windows, firsts, low, kv_heads, group, rows, tile_rows)
    hidden_grad = jnp.dot(out_low, w_down.T, preferred_element_type=f32)
    mixed = scatter_low(jnp.dot(attended, w_out_spread, preferred_element_type=f32))
    mixed, hidden_grad = tied((mixed, hidden_grad))
    residual = block_input + mixed.astype(f32)
    mlp_normed_own, inv_rms_mlp = normalize(residual, mlp_gain)
    normed_mlp = gather_rows(mlp_normed_own)

    width = w_gate.shape[1]
    pre = jnp.dot(normed_mlp, w_pair, preferred_element_type=f32)
    gate_pre, up_proj = pre[:, :width], pre[:, width:]
    sigmoid_gate = jax.nn.sigmoid(gate_pre)
    silu_gate = gate_pre * sigmoid_gate
    hidden = (silu_gate * up_proj).astype(bf16)
    gate_grad = hidden_grad * up_proj * sigmoid_gate * (1.0 + gate_pre * (1.0 - sigmoid_gate))
    up_grad = hidden_grad * silu_gate
    pair_grad = jnp.concatenate([gate_grad.astype(bf16), up_grad.astype(bf16)], axis=1)
    mlp_scattered = scatter_low(jnp.dot(pair_grad, w_pair.T, preferred_element_type=f32))
    down_product = jnp.dot(hidden, w_down, preferred_element_type=f32).astype(bf16)
    pair_shared = SharedProduct(normed_mlp, pair_grad, "dp", places)
    down_shared = SharedProduct(hidden, out_low, "dp", crossed)
    wide = (pair_shared, down_shared)
    for shared in wide:
        shared.meet()
        shared.step()
    mlp_scattered, down_product, pair_shared.value, down_shared.value = tied(
        (mlp_scattered, down_product, pair_shared.value, down_shared.value)
    )
    mlp_normed_grad = mlp_scattered.astype(f32)
    residual_part = normalize_back(residual, inv_rms_mlp, mlp_gain, mlp_normed_grad)
    residual_grad = out_grad + residual_part
    residual_low = gather_rows(residual_grad.astype(bf16))
    attended_plain = jnp.dot(attended, query_spread.T, preferred_element_type=bf16)
    for shared in wide:
        for _ in range(len(places) - 1):
            shared.step()
    residual_low, down_product, pair_shared.value, down_shared.value = tied(
        (residual_low, down_product, pair_shared.value, down_shared.value)
    )
    block_scattered = lax.psum_scatter(
        down_product, "tensor", scatter_dimension=0, tiled=True
    )
    block_output = residual + block_scattered.astype(f32)

    attended_gradient = jnp.dot(residual_low, w_out_spread.T, preferred_element_type=f32).astype(
        bf16
    )
    slots = jnp.arange(blocks, dtype=jnp.int32)
    query_grad, key_own, value_own, earlier = attend_back(
        queries, windows, firsts, low, slots, attended, [attended_gradient], logs, cosine,
        sine, kv_heads, group, rows, tile_rows,
    )
    for shared in wide:
        while len(shared.up) > 1:
            shared.step()
    earlier, pair_shared.value, down_shared.value, attended_plain = tied(
        (earlier, pair_shared.value, down_shared.value, attended_plain)
    )
    received = [
        from_behind(earlier[reach - d], "dp", -d) for d in range(1, reach + 1)
    ]
    out_shared = SharedProduct(attended_plain, residual_low, "dp", crossed)
    out_shared.meet()
    key_value_grad = gather_back(
        key_own, value_own, received, cosine, sine, kv_heads, stretch, rows
    )
    split = heads * LANES
    attn_normed_part = (
        jnp.dot(query_grad, w_joined[:, :split].T, preferred_element_type=f32)
        + jnp.dot(key_value_grad, w_joined[:, split:].T, preferred_element_type=f32)
    ).astype(bf16)
    attn_scattered = lax.psum_scatter(attn_normed_part, "tensor", scatter_dimension=0, tiled=True)
    query_plain = jnp.dot(query_grad, query_spread.T, preferred_element_type=bf16)
    kv_plain = jnp.dot(key_value_grad, kv_spread.T, preferred_element_type=bf16)
    joined_shared = SharedProduct(
        attention_normed, jnp.concatenate([query_plain, kv_plain], axis=1), "dp", places
    )
    joined_shared.meet()
    grad_joined = joined_shared.finish()
    grad_pair = pair_shared.finish()
    grad_down = down_shared.finish()
    grad_out = out_shared.finish()
    attn_gain_part = (
        jnp.sum(
            attn_normed_part.astype(f32) * attention_normed.astype(f32), axis=0, keepdims=True
        )
        / attn_gain
    )
    mlp_gain_part = jnp.sum(mlp_normed_grad * residual * inv_rms_mlp, axis=0, keepdims=True)
    gains = sum_everywhere(
        jnp.concatenate([attn_gain_part, mlp_gain_part], axis=0), ("tensor", "dp")
    )
    grad_attn_gain, grad_mlp_gain = gains[0], gains[1]

    attn_normed_grad = attn_scattered.astype(f32)
    input_part = normalize_back(block_input, inv_rms_attn, attn_gain, attn_normed_grad)
    input_grad = residual_grad + input_part
    query_width = w_query.shape[1]
    kv_width = key_weight.shape[1]
    grad_query = grad_joined[:, :query_width].astype(f32)
    grad_key = grad_joined[:, query_width : query_width + kv_width].astype(f32)
    grad_value = grad_joined[:, query_width + kv_width + gap :].astype(f32)
    return (
        block_output,
        input_grad,
        grad_query,
        grad_key,
        grad_value,
        grad_out.astype(f32),
        grad_pair[:, :width].astype(f32),
        grad_pair[:, width:].astype(f32),
        grad_down.astype(f32),
        grad_attn_gain,
        grad_mlp_gain,
    )


def solution(mesh):
    in_specs = (
        P(("dp", "tensor"), None),
        P("dp"),
        P(),
        P(None, "tensor"),
        P(None, "tensor"),
        P(None, "tensor"),
        P("tensor", None),
        P(),
        P(None, "tensor"),
        P(None, "tensor"),
        P("tensor", None),
        P(("dp", "tensor"), None),
    )
    out_specs = (
        P(("dp", "tensor"), None),
        P(("dp", "tensor"), None),
        P(None, "tensor"),
        P(None, "tensor"),
        P(None, "tensor"),
        P("tensor", None),
        P(None, "tensor"),
        P(None, "tensor"),
        P("tensor", None),
        P(),
        P(),
    )

    return jax.shard_map(
        per_device, mesh=mesh, in_specs=in_specs, out_specs=out_specs, check_vma=False
    )
```

```python
import functools
import math

import jax
import jax.numpy as jnp
from jax import lax
from jax.experimental import pallas as pl
from jax.experimental.pallas import tpu as pltpu
from jax.sharding import PartitionSpec as P


HEAD_SIZE = 96
LONGEST_DOCUMENT = 2048

LANES = 128
HALF_LANES = LANES // 2
FAR = -1e30


epsilon = 1e-05
rope_base = 100000.0

f32 = jnp.float32
bf16 = jnp.bfloat16


def from_behind(value, axis, steps):
    if steps == 0:
        return value
    count = lax.axis_size(axis)
    leading, last = (max(0, -steps), min(count, count - steps))
    return lax.ppermute(value, axis, [(source, source + steps) for source in range(leading, last)])


def exchange(value, axis, distance):
    count = lax.axis_size(axis)
    return lax.ppermute(value, axis, [(i, i ^ distance) for i in range(count)])


def rope_tables(positions):
    half_size = HEAD_SIZE // 2
    frequency = rope_base ** (-jnp.arange(half_size, dtype=f32) * 2.0 / HEAD_SIZE)
    rest = jnp.zeros((HALF_LANES - half_size,), f32)
    spread = jnp.concatenate([frequency, rest, frequency, rest])
    sign = jnp.where(jnp.arange(LANES) < HALF_LANES, -1.0, 1.0).astype(f32)
    angles = positions.astype(f32)[:, None] * spread[None, :]
    return (jnp.cos(angles), jnp.sin(angles) * sign[None, :])


def spread_matrix(heads, gap_after=0, gap=0, dtype=bf16):
    half_size = HEAD_SIZE // 2
    rows = jnp.arange(heads * HEAD_SIZE, dtype=jnp.int32)
    inner = rows % HEAD_SIZE
    lane = (rows // HEAD_SIZE) * LANES + jnp.where(
        inner < half_size, inner, inner - half_size + HALF_LANES
    )
    if gap:
        cut = gap_after * HEAD_SIZE
        lane = jnp.concatenate([lane[:cut], jnp.full((gap,), -1, jnp.int32), lane[cut:]])
    columns = jnp.arange(heads * LANES, dtype=jnp.int32)
    return (lane[:, None] == columns[None, :]).astype(dtype)


def normalize(rows, gain):
    inv_rms = lax.rsqrt(jnp.mean(rows * rows, axis=-1, keepdims=True) + epsilon)
    return ((rows * inv_rms * gain).astype(bf16), inv_rms)


def normalize_back(rows, inv_rms, gain, normed_grad):
    weighted = normed_grad * gain
    inner = jnp.mean(weighted * rows, axis=-1, keepdims=True)
    return inv_rms * weighted - rows * inv_rms**3 * inner


def turn(value, cosine, sine):
    return value * cosine + pltpu.roll(value, HALF_LANES, 1) * sine


def turn_back(value, cosine, sine):
    return value * cosine - pltpu.roll(value, HALF_LANES, 1) * sine


def project_kernel(rotated, rows_ref, weight_ref, cosine_ref, sine_ref, *out_refs):
    product = jnp.dot(rows_ref[...], weight_ref[...], preferred_element_type=f32)
    cosine = cosine_ref[...]
    sine = sine_ref[...]
    head = 0
    for out_ref in out_refs:
        for place in range(out_ref.shape[1] // LANES):
            part = product[:, head * LANES : (head + 1) * LANES]
            if head < rotated:
                part = turn(part, cosine, sine)
            out_ref[:, place * LANES : (place + 1) * LANES] = part.astype(bf16)
            head += 1


def project(rows, weight, cosine, sine, rotated, widths, block):
    count, depth = rows.shape
    width = weight.shape[1]
    return pl.pallas_call(
        functools.partial(project_kernel, rotated),
        grid=(count // block,),
        in_specs=[
            pl.BlockSpec((block, depth), lambda i: (i, 0)),
            pl.BlockSpec((depth, width), lambda i: (0, 0)),
            pl.BlockSpec((block, LANES), lambda i: (i, 0)),
            pl.BlockSpec((block, LANES), lambda i: (i, 0)),
        ],
        out_specs=[pl.BlockSpec((block, part), lambda i: (i, 0)) for part in widths],
        out_shape=[jax.ShapeDtypeStruct((count, part), bf16) for part in widths],
        cost_estimate=pl.CostEstimate(
            flops=2 * count * depth * width,
            bytes_accessed=2 * (count * depth + depth * width + count * width),
            transcendentals=0,
        ),
        name="project",
    )(rows, weight, cosine, sine)


def pair_rows(ref, group):
    return jnp.concatenate([ref[:, h * LANES : (h + 1) * LANES] for h in range(group)], axis=0)


def place_row(ref, group):
    row = ref[0]
    return jnp.concatenate([row] * group, axis=1)


def masked(scores, first, last, base):
    index = lax.broadcasted_iota(jnp.int32, scores.shape, 0)
    allowed = (index >= first - base) & (index <= last - base)
    return jnp.where(allowed, scores, FAR)


def bounds(low_ref, query_block, rows, tile_rows, offset):
    high = (offset + (query_block + 1) * rows - 1) // tile_rows + 1
    return low_ref[query_block], high


def attend_kernel(tiles, group, factor, low_ref, query_ref, first_ref, *refs):
    keys = refs[:tiles]
    values = refs[tiles : 2 * tiles]
    out_ref, log_ref, key_window, value_turned, top, total, mixed = refs[2 * tiles :]
    query_block = pl.program_id(1)
    rows = query_ref.shape[0]
    stretch = keys[0].shape[0]
    tile_rows = key_window.shape[1]
    per_tile = stretch // tile_rows

    @pl.when(query_block == 0)
    def _():
        for tile in range(tiles):
            for part in range(per_tile):
                at = pl.ds(part * tile_rows, tile_rows)
                key_window[tile * per_tile + part] = keys[tile][at, :]
                value_turned[tile * per_tile + part] = values[tile][at, :].T

    offset = (tiles - 1) * stretch
    query = pair_rows(query_ref, group)
    first = place_row(first_ref, group)
    lane = lax.broadcasted_iota(jnp.int32, (1, rows), 1)
    last = jnp.concatenate([lane] * group, axis=1) + (offset + query_block * rows)
    top[...] = jnp.full_like(top, FAR)
    total[...] = jnp.zeros_like(total)
    mixed[...] = jnp.zeros_like(mixed)
    low, high = bounds(low_ref, query_block, rows, tile_rows, offset)

    def step(tile, unused):
        scores = lax.dot_general(
            key_window[tile], query, (((1,), (1,)), ((), ())), preferred_element_type=f32
        )
        scores = masked(scores, first, last, tile * tile_rows)
        before = top[...]
        after = jnp.maximum(before, jnp.max(scores, axis=0, keepdims=True))
        weights = jnp.exp2(scores * factor - after * factor)
        fade = jnp.exp2((before - after) * factor)
        top[...] = after
        total[...] = total[...] * fade + jnp.sum(weights, axis=0, keepdims=True)
        mixed[...] = mixed[...] * fade + jnp.dot(
            value_turned[tile], weights.astype(bf16), preferred_element_type=f32
        )
        return unused

    lax.fori_loop(low, high, step, 0)
    result = (mixed[...] / total[...]).T.astype(bf16)
    for head in range(group):
        out_ref[:, head * LANES : (head + 1) * LANES] = result[head * rows : (head + 1) * rows]
    log_ref[0, 0] = top[...] * factor + jnp.log2(total[...])


def window_specs(stretch, first_column):
    return [
        pl.BlockSpec((stretch, LANES), lambda g, i, *s, c=c: (0, c + g)) for c in first_column
    ]


def attend(queries_joined, windows, firsts, low, kv_heads, group, rows, tile_rows):
    stretch = queries_joined.shape[0]
    tiles = len(windows)
    blocks = stretch // rows
    pairs = group * rows
    window_tiles = tiles * stretch // tile_rows
    factor = HEAD_SIZE ** (-0.5) * math.log2(math.e)
    key_columns = [at for _, at in windows]
    value_columns = [at + kv_heads for _, at in windows]
    arrays = [a for a, _ in windows]
    grid_spec = pltpu.PrefetchScalarGridSpec(
        num_scalar_prefetch=1,
        grid=(kv_heads, blocks),
        in_specs=[
            pl.BlockSpec((rows, group * LANES), lambda g, i, *s: (i, g)),
            pl.BlockSpec((1, 1, rows), lambda g, i, *s: (i, 0, 0)),
        ]
        + window_specs(stretch, key_columns)
        + window_specs(stretch, value_columns),
        out_specs=[
            pl.BlockSpec((rows, group * LANES), lambda g, i, *s: (i, g)),
            pl.BlockSpec((1, 1, 1, pairs), lambda g, i, *s: (g, i, 0, 0)),
        ],
        scratch_shapes=[
            pltpu.VMEM((window_tiles, tile_rows, LANES), bf16),
            pltpu.VMEM((window_tiles, LANES, tile_rows), bf16),
            pltpu.VMEM((1, pairs), f32),
            pltpu.VMEM((1, pairs), f32),
            pltpu.VMEM((LANES, pairs), f32),
        ],
    )
    work = stretch * stretch * kv_heads * group
    return pl.pallas_call(
        functools.partial(attend_kernel, tiles, group, factor),
        grid_spec=grid_spec,
        out_shape=[
            jax.ShapeDtypeStruct((stretch, kv_heads * group * LANES), bf16),
            jax.ShapeDtypeStruct((kv_heads, blocks, 1, pairs), f32),
        ],
        cost_estimate=pl.CostEstimate(
            flops=16 * LANES * work, bytes_accessed=8 * stretch * stretch, transcendentals=work
        ),
        name="attend",
    )(low, queries_joined, firsts, *arrays, *arrays)


def attend_back_kernel(
    tiles, chunks, group, factor, scale, low_ref, slot_ref, query_ref, first_ref, *refs
):
    mixed_ref, log_ref, cosine_ref, sine_ref = refs[:4]
    grad_refs = refs[4 : 4 + chunks]
    refs = refs[4 + chunks :]
    keys = refs[:tiles]
    values = refs[tiles : 2 * tiles]
    (
        query_out,
        key_own,
        value_own,
        earlier_out,
        key_out,
        value_out,
        key_window,
        value_window,
        key_turned,
        query_total,
    ) = refs[2 * tiles :]
    query_block = pl.program_id(1)
    rows = query_ref.shape[0]
    stretch = keys[0].shape[0]
    tile_rows = key_window.shape[1]
    per_tile = stretch // tile_rows

    @pl.when(query_block == 0)
    def _():
        key_out[...] = jnp.zeros_like(key_out)
        value_out[...] = jnp.zeros_like(value_out)
        for tile in range(tiles):
            for part in range(per_tile):
                at = pl.ds(part * tile_rows, tile_rows)
                key_window[tile * per_tile + part] = keys[tile][at, :]
                key_turned[tile * per_tile + part] = keys[tile][at, :].T
                value_window[tile * per_tile + part] = values[tile][at, :]

    offset = (tiles - 1) * stretch
    query = pair_rows(query_ref, group)
    grad = jnp.concatenate(
        [ref[:, h * LANES : (h + 1) * LANES] for h in range(group) for ref in grad_refs], axis=0
    )
    mixed = pair_rows(mixed_ref, group)
    inner = jnp.sum((grad.astype(f32) * mixed.astype(f32)).T, axis=0, keepdims=True)
    log_total = log_ref[0, 0]
    first = place_row(first_ref, group)
    lane = lax.broadcasted_iota(jnp.int32, (1, rows), 1)
    last = jnp.concatenate([lane] * group, axis=1) + (offset + query_block * rows)
    query_total[...] = jnp.zeros_like(query_total)
    low, high = bounds(low_ref, query_block, rows, tile_rows, offset)
    both_last = (((1,), (1,)), ((), ()))

    def step(tile, unused):
        scores = lax.dot_general(key_window[tile], query, both_last, preferred_element_type=f32)
        scores = masked(scores, first, last, tile * tile_rows)
        weights = jnp.exp2(scores * factor - log_total)
        weight_grad = lax.dot_general(
            value_window[tile], grad, both_last, preferred_element_type=f32
        )
        score_grad = (weights * (weight_grad - inner) * scale).astype(bf16)
        at = pl.ds(pl.multiple_of(tile * tile_rows, tile_rows), tile_rows)
        value_out[at, :] += jnp.dot(weights.astype(bf16), grad, preferred_element_type=f32)
        key_out[at, :] += jnp.dot(score_grad, query, preferred_element_type=f32)
        query_total[...] += jnp.dot(key_turned[tile], score_grad, preferred_element_type=f32)
        return unused

    lax.fori_loop(low, high, step, 0)
    result = query_total[...].T
    for head in range(group):
        part = result[head * rows : (head + 1) * rows]
        query_out[:, head * LANES : (head + 1) * LANES] = turn_back(
            part, cosine_ref[...], sine_ref[...]
        ).astype(bf16)

    @pl.when(query_block == pl.num_programs(1) - 1)
    def _():
        for tile in range(tiles - 1):
            at = pl.ds(tile * stretch, stretch)
            earlier_out[tile, 0] = key_out[at, :].astype(bf16)
            earlier_out[tile, 1] = value_out[at, :].astype(bf16)
        key_own[...] = key_out[pl.ds(offset, stretch), :]
        value_own[...] = value_out[pl.ds(offset, stretch), :]


def attend_back(
    queries_joined, windows, firsts, low, slots, mixed, grads, logs, cosine, sine,
    kv_heads, group, rows, tile_rows,
):
    stretch = queries_joined.shape[0]
    tiles = len(windows)
    blocks = stretch // rows
    pairs = group * rows
    window_tiles = tiles * stretch // tile_rows
    chunks = len(grads)
    scale = HEAD_SIZE ** (-0.5)
    factor = scale * math.log2(math.e)
    key_columns = [at for _, at in windows]
    value_columns = [at + kv_heads for _, at in windows]
    arrays = [a for a, _ in windows]
    heads_spec = pl.BlockSpec((rows, group * LANES), lambda g, i, *s: (i, g))
    table_spec = pl.BlockSpec((rows, LANES), lambda g, i, *s: (i, 0))
    own_spec = pl.BlockSpec((stretch, LANES), lambda g, i, *s: (0, g))
    earlier_spec = pl.BlockSpec((tiles - 1, 2, stretch, LANES), lambda g, i, *s: (0, 0, 0, g))
    grid_spec = pltpu.PrefetchScalarGridSpec(
        num_scalar_prefetch=2,
        grid=(kv_heads, blocks),
        in_specs=[
            heads_spec,
            pl.BlockSpec((1, 1, rows), lambda g, i, *s: (i, 0, 0)),
            heads_spec,
            pl.BlockSpec((1, 1, 1, pairs), lambda g, i, *s: (g, i, 0, 0)),
            table_spec,
            table_spec,
        ]
        + [
            pl.BlockSpec((rows // chunks, group * LANES), lambda g, i, low, slot: (slot[i], g))
        ]
        * chunks
        + window_specs(stretch, key_columns)
        + window_specs(stretch, value_columns),
        out_specs=[heads_spec, own_spec, own_spec, earlier_spec],
        scratch_shapes=[
            pltpu.VMEM((tiles * stretch, LANES), f32),
            pltpu.VMEM((tiles * stretch, LANES), f32),
            pltpu.VMEM((window_tiles, tile_rows, LANES), bf16),
            pltpu.VMEM((window_tiles, tile_rows, LANES), bf16),
            pltpu.VMEM((window_tiles, LANES, tile_rows), bf16),
            pltpu.VMEM((LANES, pairs), f32),
        ],
    )
    work = stretch * stretch * kv_heads * group
    return pl.pallas_call(
        functools.partial(attend_back_kernel, tiles, chunks, group, factor, scale),
        grid_spec=grid_spec,
        out_shape=[
            jax.ShapeDtypeStruct((stretch, kv_heads * group * LANES), bf16),
            jax.ShapeDtypeStruct((stretch, kv_heads * LANES), f32),
            jax.ShapeDtypeStruct((stretch, kv_heads * LANES), f32),
            jax.ShapeDtypeStruct((tiles - 1, 2, stretch, kv_heads * LANES), bf16),
        ],
        cost_estimate=pl.CostEstimate(
            flops=40 * LANES * work, bytes_accessed=16 * stretch * stretch, transcendentals=work
        ),
        name="attend_back",
    )(low, slots, queries_joined, firsts, mixed, logs, cosine, sine, *grads, *arrays, *arrays)


def gather_back_kernel(kv_heads, parts, key_ref, value_ref, cosine_ref, sine_ref, *refs):
    out_ref = refs[parts]
    for head in range(kv_heads):
        at = pl.ds(head * LANES, LANES)
        key = key_ref[:, at]
        value = value_ref[:, at]
        for part in range(parts):
            key = key + refs[part][0, :, at].astype(f32)
            value = value + refs[part][1, :, at].astype(f32)
        out_ref[:, at] = turn_back(key, cosine_ref[...], sine_ref[...]).astype(bf16)
        out_ref[:, pl.ds((kv_heads + head) * LANES, LANES)] = value.astype(bf16)


def gather_back(key_totals, value_totals, received, cosine, sine, kv_heads, stretch, block):
    width = kv_heads * LANES
    own = pl.BlockSpec((block, width), lambda i: (i, 0))
    other = pl.BlockSpec((2, block, width), lambda i: (0, i, 0))
    table = pl.BlockSpec((block, LANES), lambda i: (i, 0))
    return pl.pallas_call(
        functools.partial(gather_back_kernel, kv_heads, len(received)),
        grid=(stretch // block,),
        in_specs=[own, own, table, table] + [other] * len(received),
        out_specs=pl.BlockSpec((block, 2 * width), lambda i: (i, 0)),
        out_shape=jax.ShapeDtypeStruct((stretch, 2 * width), bf16),
        name="gather_back",
    )(key_totals, value_totals, cosine, sine, *received)


class SharedProduct:

    def __init__(self, left, right, axis, order):
        self.left, self.right, self.axis, self.order = left, right, axis, order
        self.size = left.shape[1] // 2
        self.sent = self.times(0, True).astype(bf16)

    def bit(self, place):
        return (lax.axis_index(self.axis) >> place) & 1

    def times(self, place, other):
        bit = self.bit(self.order[place])
        offset = ((1 - bit) if other else bit) * self.size
        part = lax.dynamic_slice_in_dim(self.left, offset, self.size, 1)
        return jnp.dot(part.T, self.right, preferred_element_type=f32)

    def meet(self):
        got = exchange(self.sent, self.axis, 1 << self.order[0])
        self.value = self.times(0, False) + got.astype(f32)
        self.down = list(self.order[1:])
        self.up = list(reversed(self.order))
        return self.value

    def step(self):
        if self.down:
            place = self.down.pop(0)
            bit = self.bit(place)
            size = self.value.shape[0] // 2
            sent = lax.dynamic_slice_in_dim(self.value, (1 - bit) * size, size, 0).astype(bf16)
            got = exchange(sent, self.axis, 1 << place)
            kept = lax.dynamic_slice_in_dim(self.value, bit * size, size, 0)
            self.value = kept + got.astype(f32)
            return self.value
        self.begin_up()
        return self.end_up()

    def begin_up(self):
        self.place = self.up.pop(0)
        self.value = self.value.astype(bf16)
        self.got = exchange(self.value, self.axis, 1 << self.place)

    def end_up(self):
        self.value = self.joined(self.value, self.got)
        return self.value

    def joined(self, whole, got):
        return jnp.where(
            self.bit(self.place) == 1,
            jnp.concatenate([got, whole], axis=0),
            jnp.concatenate([whole, got], axis=0),
        )

    def finish(self, *spans):
        while len(self.up) > 1:
            self.step()
        if self.up:
            self.begin_up()
        return [
            self.joined(self.value[:, a:b], self.got[:, a:b]).astype(f32)
            for a, b in spans
        ]


def sum_everywhere(value, axes):
    for axis in axes:
        count = lax.axis_size(axis)
        place = 1
        while place < count:
            value = value + exchange(value, axis, place)
            place *= 2
    return value


def scatter_low(product):
    return lax.psum_scatter(product.astype(bf16), "tensor", scatter_dimension=0, tiled=True)


def gather_rows(rows):
    return lax.all_gather(rows, "tensor", axis=0, tiled=True)


def per_device(
    block_input,
    positions,
    attn_gain,
    w_query,
    key_weight,
    value_weight,
    w_out,
    mlp_gain,
    w_gate,
    w_up,
    w_down,
    out_grad,
):
    stretch = positions.shape[0]
    reach = LONGEST_DOCUMENT // stretch
    heads = w_query.shape[1] // HEAD_SIZE
    kv_heads = key_weight.shape[1] // HEAD_SIZE
    group = heads // kv_heads
    rows = min(256, stretch)
    tile_rows = min(512, stretch)
    blocks = stretch // rows
    places = list(range((lax.axis_size("dp") - 1).bit_length()))
    crossed = places[:1] + places[:0:-1]
    tied = lax.optimization_barrier

    normed_own, inv_rms_attn = normalize(block_input, attn_gain)
    normed_own, out_own = tied((normed_own, out_grad.astype(bf16)))
    attention_normed = gather_rows(normed_own)
    out_low = gather_rows(out_own)

    query_spread = spread_matrix(heads)
    gap = -kv_heads * HEAD_SIZE % LANES
    kv_spread = spread_matrix(2 * kv_heads, kv_heads, gap)
    all_spread = spread_matrix(heads + 2 * kv_heads)
    w_joined = jnp.dot(
        jnp.concatenate([w_query, key_weight, value_weight], axis=1), all_spread,
        preferred_element_type=bf16,
    )
    w_out_spread = jnp.dot(query_spread.T, w_out, preferred_element_type=bf16)
    w_pair = jnp.concatenate([w_gate, w_up], axis=1)
    cosine, sine = rope_tables(positions)
    local = jnp.arange(stretch, dtype=jnp.int32)
    window_first = reach * stretch + local - positions
    firsts = window_first.reshape(blocks, 1, rows)
    low = jnp.min(window_first.reshape(blocks, rows), axis=1) // tile_rows

    queries, key_value = project(
        attention_normed, w_joined, cosine, sine, heads + kv_heads,
        (heads * LANES, 2 * kv_heads * LANES), rows,
    )
    windows = [(from_behind(key_value, "dp", d), 0) for d in range(reach, -1, -1)]
    attended, logs = attend(queries, windows, firsts, low, kv_heads, group, rows, tile_rows)
    hidden_grad = jnp.dot(out_low, w_down.T, preferred_element_type=f32)
    mixed = scatter_low(jnp.dot(attended, w_out_spread, preferred_element_type=f32))
    mixed, hidden_grad = tied((mixed, hidden_grad))
    residual = block_input + mixed.astype(f32)
    mlp_normed_own, inv_rms_mlp = normalize(residual, mlp_gain)
    normed_mlp = gather_rows(mlp_normed_own)

    width = w_gate.shape[1]
    pre = jnp.dot(normed_mlp, w_pair, preferred_element_type=f32)
    gate_pre, up_proj = pre[:, :width], pre[:, width:]
    sigmoid_gate = jax.nn.sigmoid(gate_pre)
    silu_gate = gate_pre * sigmoid_gate
    hidden = (silu_gate * up_proj).astype(bf16)
    gate_grad = hidden_grad * up_proj * sigmoid_gate * (1.0 + gate_pre * (1.0 - sigmoid_gate))
    up_grad = hidden_grad * silu_gate
    pair_grad = jnp.concatenate([gate_grad.astype(bf16), up_grad.astype(bf16)], axis=1)
    mlp_product = jnp.dot(pair_grad, w_pair.T, preferred_element_type=f32).astype(bf16)
    mlp_product, pair_grad, hidden = tied((mlp_product, pair_grad, hidden))
    mlp_scattered = scatter_low(mlp_product)
    down_product = jnp.dot(hidden, w_down, preferred_element_type=f32).astype(bf16)
    pair_shared = SharedProduct(normed_mlp, pair_grad, "dp", places)
    down_shared = SharedProduct(hidden, out_low, "dp", crossed)
    wide = (pair_shared, down_shared)
    for shared in wide:
        shared.meet()
        shared.step()
    mlp_scattered, down_product, pair_shared.value, down_shared.value = tied(
        (mlp_scattered, down_product, pair_shared.value, down_shared.value)
    )
    mlp_normed_grad = mlp_scattered.astype(f32)
    residual_part = normalize_back(residual, inv_rms_mlp, mlp_gain, mlp_normed_grad)
    residual_grad = out_grad + residual_part
    residual_low = gather_rows(residual_grad.astype(bf16))
    attended_plain = jnp.dot(attended, query_spread.T, preferred_element_type=bf16)
    for shared in wide:
        for _ in range(len(places) - 1):
            shared.step()
    residual_low, down_product, pair_shared.value, down_shared.value = tied(
        (residual_low, down_product, pair_shared.value, down_shared.value)
    )
    block_scattered = lax.psum_scatter(
        down_product, "tensor", scatter_dimension=0, tiled=True
    )
    block_output = residual + block_scattered.astype(f32)

    attended_gradient = jnp.dot(residual_low, w_out_spread.T, preferred_element_type=f32).astype(
        bf16
    )
    slots = jnp.arange(blocks, dtype=jnp.int32)
    query_grad, key_own, value_own, earlier = attend_back(
        queries, windows, firsts, low, slots, attended, [attended_gradient], logs, cosine,
        sine, kv_heads, group, rows, tile_rows,
    )
    for shared in wide:
        while len(shared.up) > 2:
            shared.step()
        shared.begin_up()
    earlier, pair_shared.got, down_shared.got, attended_plain = tied(
        (earlier, pair_shared.got, down_shared.got, attended_plain)
    )
    for shared in wide:
        shared.end_up()
    received = [
        from_behind(earlier[reach - d], "dp", -d) for d in range(1, reach + 1)
    ]
    out_shared = SharedProduct(attended_plain, residual_low, "dp", crossed)
    out_shared.meet()
    for shared in wide:
        shared.begin_up()
    received, pair_shared.got, down_shared.got, out_shared.value = tied(
        (received, pair_shared.got, down_shared.got, out_shared.value)
    )
    key_value_grad = gather_back(
        key_own, value_own, received, cosine, sine, kv_heads, stretch, rows
    )
    split = heads * LANES
    attn_normed_part = (
        jnp.dot(query_grad, w_joined[:, :split].T, preferred_element_type=f32)
        + jnp.dot(key_value_grad, w_joined[:, split:].T, preferred_element_type=f32)
    ).astype(bf16)
    attn_scattered = lax.psum_scatter(attn_normed_part, "tensor", scatter_dimension=0, tiled=True)
    query_plain = jnp.dot(query_grad, query_spread.T, preferred_element_type=bf16)
    kv_plain = jnp.dot(key_value_grad, kv_spread.T, preferred_element_type=bf16)
    joined_shared = SharedProduct(
        attention_normed, jnp.concatenate([query_plain, kv_plain], axis=1), "dp", places
    )
    joined_shared.meet()
    query_width = w_query.shape[1]
    kv_width = key_weight.shape[1]
    value_from = query_width + kv_width + gap
    grad_query, grad_key, grad_value = joined_shared.finish(
        (0, query_width),
        (query_width, query_width + kv_width),
        (value_from, value_from + kv_width),
    )
    grad_gate, grad_up = pair_shared.finish((0, width), (width, 2 * width))
    (grad_down,) = down_shared.finish((0, out_grad.shape[1]))
    (grad_out,) = out_shared.finish((0, out_grad.shape[1]))
    attn_gain_part = (
        jnp.sum(
            attn_normed_part.astype(f32) * attention_normed.astype(f32), axis=0, keepdims=True
        )
        / attn_gain
    )
    mlp_gain_part = jnp.sum(mlp_normed_grad * residual * inv_rms_mlp, axis=0, keepdims=True)
    gains = sum_everywhere(
        jnp.concatenate([attn_gain_part, mlp_gain_part], axis=0), ("tensor", "dp")
    )
    grad_attn_gain, grad_mlp_gain = gains[0], gains[1]

    attn_normed_grad = attn_scattered.astype(f32)
    input_part = normalize_back(block_input, inv_rms_attn, attn_gain, attn_normed_grad)
    input_grad = residual_grad + input_part
    return (
        block_output,
        input_grad,
        grad_query,
        grad_key,
        grad_value,
        grad_out,
        grad_gate,
        grad_up,
        grad_down,
        grad_attn_gain,
        grad_mlp_gain,
    )


def solution(mesh):
    in_specs = (
        P(("dp", "tensor"), None),
        P("dp"),
        P(),
        P(None, "tensor"),
        P(None, "tensor"),
        P(None, "tensor"),
        P("tensor", None),
        P(),
        P(None, "tensor"),
        P(None, "tensor"),
        P("tensor", None),
        P(("dp", "tensor"), None),
    )
    out_specs = (
        P(("dp", "tensor"), None),
        P(("dp", "tensor"), None),
        P(None, "tensor"),
        P(None, "tensor"),
        P(None, "tensor"),
        P("tensor", None),
        P(None, "tensor"),
        P(None, "tensor"),
        P("tensor", None),
        P(),
        P(),
    )

    return jax.shard_map(
        per_device, mesh=mesh, in_specs=in_specs, out_specs=out_specs, check_vma=False
    )
```

```python
import functools
import math

import jax
import jax.numpy as jnp
from jax import lax
from jax.experimental import pallas as pl
from jax.experimental.pallas import tpu as pltpu
from jax.sharding import PartitionSpec as P


HEAD_SIZE = 96
LONGEST_DOCUMENT = 2048

LANES = 128
HALF_LANES = LANES // 2
FAR = -1e30


epsilon = 1e-05
rope_base = 100000.0

f32 = jnp.float32
bf16 = jnp.bfloat16


def from_behind(value, axis, steps):
    if steps == 0:
        return value
    count = lax.axis_size(axis)
    leading, last = (max(0, -steps), min(count, count - steps))
    return lax.ppermute(value, axis, [(source, source + steps) for source in range(leading, last)])


def exchange(value, axis, distance):
    count = lax.axis_size(axis)
    return lax.ppermute(value, axis, [(i, i ^ distance) for i in range(count)])


def rope_tables(positions):
    half_size = HEAD_SIZE // 2
    frequency = rope_base ** (-jnp.arange(half_size, dtype=f32) * 2.0 / HEAD_SIZE)
    rest = jnp.zeros((HALF_LANES - half_size,), f32)
    spread = jnp.concatenate([frequency, rest, frequency, rest])
    sign = jnp.where(jnp.arange(LANES) < HALF_LANES, -1.0, 1.0).astype(f32)
    angles = positions.astype(f32)[:, None] * spread[None, :]
    return (jnp.cos(angles), jnp.sin(angles) * sign[None, :])


def spread_matrix(heads, gap_after=0, gap=0, dtype=bf16):
    half_size = HEAD_SIZE // 2
    rows = jnp.arange(heads * HEAD_SIZE, dtype=jnp.int32)
    inner = rows % HEAD_SIZE
    lane = (rows // HEAD_SIZE) * LANES + jnp.where(
        inner < half_size, inner, inner - half_size + HALF_LANES
    )
    if gap:
        cut = gap_after * HEAD_SIZE
        lane = jnp.concatenate([lane[:cut], jnp.full((gap,), -1, jnp.int32), lane[cut:]])
    columns = jnp.arange(heads * LANES, dtype=jnp.int32)
    return (lane[:, None] == columns[None, :]).astype(dtype)


def normalize(rows, gain):
    inv_rms = lax.rsqrt(jnp.mean(rows * rows, axis=-1, keepdims=True) + epsilon)
    return ((rows * inv_rms * gain).astype(bf16), inv_rms)


def normalize_back(rows, inv_rms, gain, normed_grad):
    weighted = normed_grad * gain
    inner = jnp.mean(weighted * rows, axis=-1, keepdims=True)
    return inv_rms * weighted - rows * inv_rms**3 * inner


def turn(value, cosine, sine):
    return value * cosine + pltpu.roll(value, HALF_LANES, 1) * sine


def turn_back(value, cosine, sine):
    return value * cosine - pltpu.roll(value, HALF_LANES, 1) * sine


def project_kernel(rotated, rows_ref, weight_ref, cosine_ref, sine_ref, *out_refs):
    product = jnp.dot(rows_ref[...], weight_ref[...], preferred_element_type=f32)
    cosine = cosine_ref[...]
    sine = sine_ref[...]
    head = 0
    for out_ref in out_refs:
        for place in range(out_ref.shape[1] // LANES):
            part = product[:, head * LANES : (head + 1) * LANES]
            if head < rotated:
                part = turn(part, cosine, sine)
            out_ref[:, place * LANES : (place + 1) * LANES] = part.astype(bf16)
            head += 1


def project(rows, weight, cosine, sine, rotated, widths, block):
    count, depth = rows.shape
    width = weight.shape[1]
    return pl.pallas_call(
        functools.partial(project_kernel, rotated),
        grid=(count // block,),
        in_specs=[
            pl.BlockSpec((block, depth), lambda i: (i, 0)),
            pl.BlockSpec((depth, width), lambda i: (0, 0)),
            pl.BlockSpec((block, LANES), lambda i: (i, 0)),
            pl.BlockSpec((block, LANES), lambda i: (i, 0)),
        ],
        out_specs=[pl.BlockSpec((block, part), lambda i: (i, 0)) for part in widths],
        out_shape=[jax.ShapeDtypeStruct((count, part), bf16) for part in widths],
        cost_estimate=pl.CostEstimate(
            flops=2 * count * depth * width,
            bytes_accessed=2 * (count * depth + depth * width + count * width),
            transcendentals=0,
        ),
        name="project",
    )(rows, weight, cosine, sine)


def pair_rows(ref, group):
    return jnp.concatenate([ref[:, h * LANES : (h + 1) * LANES] for h in range(group)], axis=0)


def place_row(ref, group):
    row = ref[0]
    return jnp.concatenate([row] * group, axis=1)


def masked(scores, first, last, base):
    index = lax.broadcasted_iota(jnp.int32, scores.shape, 0)
    allowed = (index >= first - base) & (index <= last - base)
    return jnp.where(allowed, scores, FAR)


def bounds(low_ref, query_block, rows, tile_rows, offset):
    high = (offset + (query_block + 1) * rows - 1) // tile_rows + 1
    return low_ref[query_block], high


def attend_kernel(tiles, group, factor, low_ref, query_ref, first_ref, *refs):
    keys = refs[:tiles]
    values = refs[tiles : 2 * tiles]
    out_ref, log_ref, key_window, value_turned, top, total, mixed = refs[2 * tiles :]
    query_block = pl.program_id(1)
    rows = query_ref.shape[0]
    stretch = keys[0].shape[0]
    tile_rows = key_window.shape[1]
    per_tile = stretch // tile_rows

    @pl.when(query_block == 0)
    def _():
        for tile in range(tiles):
            for part in range(per_tile):
                at = pl.ds(part * tile_rows, tile_rows)
                key_window[tile * per_tile + part] = keys[tile][at, :]
                value_turned[tile * per_tile + part] = values[tile][at, :].T

    offset = (tiles - 1) * stretch
    query = pair_rows(query_ref, group)
    first = place_row(first_ref, group)
    lane = lax.broadcasted_iota(jnp.int32, (1, rows), 1)
    last = jnp.concatenate([lane] * group, axis=1) + (offset + query_block * rows)
    top[...] = jnp.full_like(top, FAR)
    total[...] = jnp.zeros_like(total)
    mixed[...] = jnp.zeros_like(mixed)
    low, high = bounds(low_ref, query_block, rows, tile_rows, offset)

    def step(tile, unused):
        scores = lax.dot_general(
            key_window[tile], query, (((1,), (1,)), ((), ())), preferred_element_type=f32
        )
        scores = masked(scores, first, last, tile * tile_rows)
        before = top[...]
        after = jnp.maximum(before, jnp.max(scores, axis=0, keepdims=True))
        weights = jnp.exp2(scores * factor - after * factor)
        fade = jnp.exp2((before - after) * factor)
        top[...] = after
        total[...] = total[...] * fade + jnp.sum(weights, axis=0, keepdims=True)
        mixed[...] = mixed[...] * fade + jnp.dot(
            value_turned[tile], weights.astype(bf16), preferred_element_type=f32
        )
        return unused

    lax.fori_loop(low, high, step, 0)
    result = (mixed[...] / total[...]).T.astype(bf16)
    for head in range(group):
        out_ref[:, head * LANES : (head + 1) * LANES] = result[head * rows : (head + 1) * rows]
    log_ref[0, 0] = top[...] * factor + jnp.log2(total[...])


def window_specs(stretch, first_column):
    return [
        pl.BlockSpec((stretch, LANES), lambda g, i, *s, c=c: (0, c + g)) for c in first_column
    ]


def attend(queries_joined, windows, firsts, low, kv_heads, group, rows, tile_rows):
    stretch = queries_joined.shape[0]
    tiles = len(windows)
    blocks = stretch // rows
    pairs = group * rows
    window_tiles = tiles * stretch // tile_rows
    factor = HEAD_SIZE ** (-0.5) * math.log2(math.e)
    key_columns = [at for _, at in windows]
    value_columns = [at + kv_heads for _, at in windows]
    arrays = [a for a, _ in windows]
    grid_spec = pltpu.PrefetchScalarGridSpec(
        num_scalar_prefetch=1,
        grid=(kv_heads, blocks),
        in_specs=[
            pl.BlockSpec((rows, group * LANES), lambda g, i, *s: (i, g)),
            pl.BlockSpec((1, 1, rows), lambda g, i, *s: (i, 0, 0)),
        ]
        + window_specs(stretch, key_columns)
        + window_specs(stretch, value_columns),
        out_specs=[
            pl.BlockSpec((rows, group * LANES), lambda g, i, *s: (i, g)),
            pl.BlockSpec((1, 1, 1, pairs), lambda g, i, *s: (g, i, 0, 0)),
        ],
        scratch_shapes=[
            pltpu.VMEM((window_tiles, tile_rows, LANES), bf16),
            pltpu.VMEM((window_tiles, LANES, tile_rows), bf16),
            pltpu.VMEM((1, pairs), f32),
            pltpu.VMEM((1, pairs), f32),
            pltpu.VMEM((LANES, pairs), f32),
        ],
    )
    work = stretch * stretch * kv_heads * group
    return pl.pallas_call(
        functools.partial(attend_kernel, tiles, group, factor),
        grid_spec=grid_spec,
        out_shape=[
            jax.ShapeDtypeStruct((stretch, kv_heads * group * LANES), bf16),
            jax.ShapeDtypeStruct((kv_heads, blocks, 1, pairs), f32),
        ],
        cost_estimate=pl.CostEstimate(
            flops=16 * LANES * work, bytes_accessed=8 * stretch * stretch, transcendentals=work
        ),
        name="attend",
    )(low, queries_joined, firsts, *arrays, *arrays)


def attend_back_kernel(
    tiles, chunks, group, factor, scale, low_ref, slot_ref, query_ref, first_ref, *refs
):
    mixed_ref, log_ref, cosine_ref, sine_ref = refs[:4]
    grad_refs = refs[4 : 4 + chunks]
    refs = refs[4 + chunks :]
    keys = refs[:tiles]
    values = refs[tiles : 2 * tiles]
    (
        query_out,
        key_own,
        value_own,
        earlier_out,
        key_out,
        value_out,
        key_window,
        value_window,
        key_turned,
        query_total,
    ) = refs[2 * tiles :]
    query_block = pl.program_id(1)
    rows = query_ref.shape[0]
    stretch = keys[0].shape[0]
    tile_rows = key_window.shape[1]
    per_tile = stretch // tile_rows

    @pl.when(query_block == 0)
    def _():
        key_out[...] = jnp.zeros_like(key_out)
        value_out[...] = jnp.zeros_like(value_out)
        for tile in range(tiles):
            for part in range(per_tile):
                at = pl.ds(part * tile_rows, tile_rows)
                key_window[tile * per_tile + part] = keys[tile][at, :]
                key_turned[tile * per_tile + part] = keys[tile][at, :].T
                value_window[tile * per_tile + part] = values[tile][at, :]

    offset = (tiles - 1) * stretch
    query = pair_rows(query_ref, group)
    grad = jnp.concatenate(
        [ref[:, h * LANES : (h + 1) * LANES] for h in range(group) for ref in grad_refs], axis=0
    )
    mixed = pair_rows(mixed_ref, group)
    inner = jnp.sum((grad.astype(f32) * mixed.astype(f32)).T, axis=0, keepdims=True)
    log_total = log_ref[0, 0]
    first = place_row(first_ref, group)
    lane = lax.broadcasted_iota(jnp.int32, (1, rows), 1)
    last = jnp.concatenate([lane] * group, axis=1) + (offset + query_block * rows)
    query_total[...] = jnp.zeros_like(query_total)
    low, high = bounds(low_ref, query_block, rows, tile_rows, offset)
    both_last = (((1,), (1,)), ((), ()))

    def step(tile, unused):
        scores = lax.dot_general(key_window[tile], query, both_last, preferred_element_type=f32)
        scores = masked(scores, first, last, tile * tile_rows)
        weights = jnp.exp2(scores * factor - log_total)
        weight_grad = lax.dot_general(
            value_window[tile], grad, both_last, preferred_element_type=f32
        )
        score_grad = (weights * (weight_grad - inner) * scale).astype(bf16)
        at = pl.ds(pl.multiple_of(tile * tile_rows, tile_rows), tile_rows)
        value_out[at, :] += jnp.dot(weights.astype(bf16), grad, preferred_element_type=f32)
        key_out[at, :] += jnp.dot(score_grad, query, preferred_element_type=f32)
        query_total[...] += jnp.dot(key_turned[tile], score_grad, preferred_element_type=f32)
        return unused

    lax.fori_loop(low, high, step, 0)
    result = query_total[...].T
    for head in range(group):
        part = result[head * rows : (head + 1) * rows]
        query_out[:, head * LANES : (head + 1) * LANES] = turn_back(
            part, cosine_ref[...], sine_ref[...]
        ).astype(bf16)

    @pl.when(query_block == pl.num_programs(1) - 1)
    def _():
        for tile in range(tiles - 1):
            at = pl.ds(tile * stretch, stretch)
            earlier_out[tile, 0] = key_out[at, :].astype(bf16)
            earlier_out[tile, 1] = value_out[at, :].astype(bf16)
        key_own[...] = key_out[pl.ds(offset, stretch), :]
        value_own[...] = value_out[pl.ds(offset, stretch), :]


def attend_back(
    queries_joined, windows, firsts, low, slots, mixed, grads, logs, cosine, sine,
    kv_heads, group, rows, tile_rows,
):
    stretch = queries_joined.shape[0]
    tiles = len(windows)
    blocks = stretch // rows
    pairs = group * rows
    window_tiles = tiles * stretch // tile_rows
    chunks = len(grads)
    scale = HEAD_SIZE ** (-0.5)
    factor = scale * math.log2(math.e)
    key_columns = [at for _, at in windows]
    value_columns = [at + kv_heads for _, at in windows]
    arrays = [a for a, _ in windows]
    heads_spec = pl.BlockSpec((rows, group * LANES), lambda g, i, *s: (i, g))
    table_spec = pl.BlockSpec((rows, LANES), lambda g, i, *s: (i, 0))
    own_spec = pl.BlockSpec((stretch, LANES), lambda g, i, *s: (0, g))
    earlier_spec = pl.BlockSpec((tiles - 1, 2, stretch, LANES), lambda g, i, *s: (0, 0, 0, g))
    grid_spec = pltpu.PrefetchScalarGridSpec(
        num_scalar_prefetch=2,
        grid=(kv_heads, blocks),
        in_specs=[
            heads_spec,
            pl.BlockSpec((1, 1, rows), lambda g, i, *s: (i, 0, 0)),
            heads_spec,
            pl.BlockSpec((1, 1, 1, pairs), lambda g, i, *s: (g, i, 0, 0)),
            table_spec,
            table_spec,
        ]
        + [
            pl.BlockSpec((rows // chunks, group * LANES), lambda g, i, low, slot: (slot[i], g))
        ]
        * chunks
        + window_specs(stretch, key_columns)
        + window_specs(stretch, value_columns),
        out_specs=[heads_spec, own_spec, own_spec, earlier_spec],
        scratch_shapes=[
            pltpu.VMEM((tiles * stretch, LANES), f32),
            pltpu.VMEM((tiles * stretch, LANES), f32),
            pltpu.VMEM((window_tiles, tile_rows, LANES), bf16),
            pltpu.VMEM((window_tiles, tile_rows, LANES), bf16),
            pltpu.VMEM((window_tiles, LANES, tile_rows), bf16),
            pltpu.VMEM((LANES, pairs), f32),
        ],
    )
    work = stretch * stretch * kv_heads * group
    return pl.pallas_call(
        functools.partial(attend_back_kernel, tiles, chunks, group, factor, scale),
        grid_spec=grid_spec,
        out_shape=[
            jax.ShapeDtypeStruct((stretch, kv_heads * group * LANES), bf16),
            jax.ShapeDtypeStruct((stretch, kv_heads * LANES), f32),
            jax.ShapeDtypeStruct((stretch, kv_heads * LANES), f32),
            jax.ShapeDtypeStruct((tiles - 1, 2, stretch, kv_heads * LANES), bf16),
        ],
        cost_estimate=pl.CostEstimate(
            flops=40 * LANES * work, bytes_accessed=16 * stretch * stretch, transcendentals=work
        ),
        name="attend_back",
    )(low, slots, queries_joined, firsts, mixed, logs, cosine, sine, *grads, *arrays, *arrays)


def gather_back_kernel(kv_heads, parts, key_ref, value_ref, cosine_ref, sine_ref, *refs):
    out_ref = refs[parts]
    for head in range(kv_heads):
        at = pl.ds(head * LANES, LANES)
        key = key_ref[:, at]
        value = value_ref[:, at]
        for part in range(parts):
            key = key + refs[part][0, :, at].astype(f32)
            value = value + refs[part][1, :, at].astype(f32)
        out_ref[:, at] = turn_back(key, cosine_ref[...], sine_ref[...]).astype(bf16)
        out_ref[:, pl.ds((kv_heads + head) * LANES, LANES)] = value.astype(bf16)


def gather_back(key_totals, value_totals, received, cosine, sine, kv_heads, stretch, block):
    width = kv_heads * LANES
    own = pl.BlockSpec((block, width), lambda i: (i, 0))
    other = pl.BlockSpec((2, block, width), lambda i: (0, i, 0))
    table = pl.BlockSpec((block, LANES), lambda i: (i, 0))
    return pl.pallas_call(
        functools.partial(gather_back_kernel, kv_heads, len(received)),
        grid=(stretch // block,),
        in_specs=[own, own, table, table] + [other] * len(received),
        out_specs=pl.BlockSpec((block, 2 * width), lambda i: (i, 0)),
        out_shape=jax.ShapeDtypeStruct((stretch, 2 * width), bf16),
        name="gather_back",
    )(key_totals, value_totals, cosine, sine, *received)


class SharedProduct:

    def __init__(self, left, right, axis, order):
        self.left, self.right, self.axis, self.order = left, right, axis, order
        self.size = left.shape[1] // 2
        self.sent = self.times(0, True).astype(bf16)

    def bit(self, place):
        return (lax.axis_index(self.axis) >> place) & 1

    def times(self, place, other):
        bit = self.bit(self.order[place])
        offset = ((1 - bit) if other else bit) * self.size
        part = lax.dynamic_slice_in_dim(self.left, offset, self.size, 1)
        return jnp.dot(part.T, self.right, preferred_element_type=f32)

    def meet(self, *others):
        got = exchange(self.sent, self.axis, 1 << self.order[0])
        if others:
            got, *others = lax.optimization_barrier((got,) + others)
        self.value = self.times(0, False) + got.astype(f32)
        self.down = list(self.order[1:])
        self.up = list(reversed(self.order))
        return others

    def step(self):
        if self.down:
            place = self.down.pop(0)
            bit = self.bit(place)
            size = self.value.shape[0] // 2
            sent = lax.dynamic_slice_in_dim(self.value, (1 - bit) * size, size, 0).astype(bf16)
            got = exchange(sent, self.axis, 1 << place)
            kept = lax.dynamic_slice_in_dim(self.value, bit * size, size, 0)
            self.value = kept + got.astype(f32)
            return self.value
        self.begin_up()
        return self.end_up()

    def begin_up(self):
        self.place = self.up.pop(0)
        self.value = self.value.astype(bf16)
        self.got = exchange(self.value, self.axis, 1 << self.place)

    def end_up(self):
        self.value = self.joined(self.value, self.got)
        return self.value

    def joined(self, whole, got):
        return jnp.where(
            self.bit(self.place) == 1,
            jnp.concatenate([got, whole], axis=0),
            jnp.concatenate([whole, got], axis=0),
        )

    def finish(self, *spans):
        while len(self.up) > 1:
            self.step()
        if self.up:
            self.begin_up()
        return [
            self.joined(self.value[:, a:b], self.got[:, a:b]).astype(f32)
            for a, b in spans
        ]


def sum_everywhere(value, axes):
    for axis in axes:
        count = lax.axis_size(axis)
        place = 1
        while place < count:
            value = value + exchange(value, axis, place)
            place *= 2
    return value


def scatter_low(product):
    return lax.psum_scatter(product.astype(bf16), "tensor", scatter_dimension=0, tiled=True)


def gather_rows(rows):
    return lax.all_gather(rows, "tensor", axis=0, tiled=True)


def per_device(
    block_input,
    positions,
    attn_gain,
    w_query,
    key_weight,
    value_weight,
    w_out,
    mlp_gain,
    w_gate,
    w_up,
    w_down,
    out_grad,
):
    stretch = positions.shape[0]
    reach = LONGEST_DOCUMENT // stretch
    heads = w_query.shape[1] // HEAD_SIZE
    kv_heads = key_weight.shape[1] // HEAD_SIZE
    group = heads // kv_heads
    rows = min(256, stretch)
    tile_rows = min(512, stretch)
    blocks = stretch // rows
    places = list(range((lax.axis_size("dp") - 1).bit_length()))
    crossed = places[:1] + places[:0:-1]
    tied = lax.optimization_barrier

    normed_own, inv_rms_attn = normalize(block_input, attn_gain)
    normed_own, out_own = tied((normed_own, out_grad.astype(bf16)))
    attention_normed = gather_rows(normed_own)
    out_low = gather_rows(out_own)

    query_spread = spread_matrix(heads)
    gap = -kv_heads * HEAD_SIZE % LANES
    kv_spread = spread_matrix(2 * kv_heads, kv_heads, gap)
    all_spread = spread_matrix(heads + 2 * kv_heads)
    w_joined = jnp.dot(
        jnp.concatenate([w_query, key_weight, value_weight], axis=1), all_spread,
        preferred_element_type=bf16,
    )
    w_out_spread = jnp.dot(query_spread.T, w_out, preferred_element_type=bf16)
    w_pair = jnp.concatenate([w_gate, w_up], axis=1)
    cosine, sine = rope_tables(positions)
    local = jnp.arange(stretch, dtype=jnp.int32)
    window_first = reach * stretch + local - positions
    firsts = window_first.reshape(blocks, 1, rows)
    low = jnp.min(window_first.reshape(blocks, rows), axis=1) // tile_rows

    queries, key_value = project(
        attention_normed, w_joined, cosine, sine, heads + kv_heads,
        (heads * LANES, 2 * kv_heads * LANES), rows,
    )
    paired = reach == 2 and lax.axis_size("dp") % 2 == 0
    odd = lax.axis_index("dp") % 2 == 1
    if paired:
        two_back = from_behind(key_value, "dp", 2)
        one_back = exchange(jnp.where(odd, two_back, key_value), "dp", 1)
        windows = [(two_back, 0), (one_back, 0), (key_value, 0)]
    else:
        windows = [(from_behind(key_value, "dp", d), 0) for d in range(reach, -1, -1)]
    attended, logs = attend(queries, windows, firsts, low, kv_heads, group, rows, tile_rows)
    hidden_grad = jnp.dot(out_low, w_down.T, preferred_element_type=f32)
    mixed = scatter_low(jnp.dot(attended, w_out_spread, preferred_element_type=f32))
    mixed, hidden_grad = tied((mixed, hidden_grad))
    residual = block_input + mixed.astype(f32)
    mlp_normed_own, inv_rms_mlp = normalize(residual, mlp_gain)
    normed_mlp = gather_rows(mlp_normed_own)

    width = w_gate.shape[1]
    pre = jnp.dot(normed_mlp, w_pair, preferred_element_type=f32)
    gate_pre, up_proj = pre[:, :width], pre[:, width:]
    sigmoid_gate = jax.nn.sigmoid(gate_pre)
    silu_gate = gate_pre * sigmoid_gate
    hidden = (silu_gate * up_proj).astype(bf16)
    gate_grad = hidden_grad * up_proj * sigmoid_gate * (1.0 + gate_pre * (1.0 - sigmoid_gate))
    up_grad = hidden_grad * silu_gate
    pair_grad = jnp.concatenate([gate_grad.astype(bf16), up_grad.astype(bf16)], axis=1)
    mlp_product = jnp.dot(pair_grad, w_pair.T, preferred_element_type=f32).astype(bf16)
    mlp_product, pair_grad, hidden = tied((mlp_product, pair_grad, hidden))
    mlp_scattered = scatter_low(mlp_product)
    down_product = jnp.dot(hidden, w_down, preferred_element_type=f32).astype(bf16)
    pair_shared = SharedProduct(normed_mlp, pair_grad, "dp", places)
    down_shared = SharedProduct(hidden, out_low, "dp", crossed)
    wide = (pair_shared, down_shared)
    for shared in wide:
        shared.meet()
        shared.step()
    mlp_scattered, down_product, pair_shared.value, down_shared.value = tied(
        (mlp_scattered, down_product, pair_shared.value, down_shared.value)
    )
    mlp_normed_grad = mlp_scattered.astype(f32)
    residual_part = normalize_back(residual, inv_rms_mlp, mlp_gain, mlp_normed_grad)
    residual_grad = out_grad + residual_part
    residual_low = gather_rows(residual_grad.astype(bf16))
    attended_plain = jnp.dot(attended, query_spread.T, preferred_element_type=bf16)
    for shared in wide:
        for _ in range(len(places) - 1):
            shared.step()
    residual_low, down_product, pair_shared.value, down_shared.value = tied(
        (residual_low, down_product, pair_shared.value, down_shared.value)
    )
    block_scattered = lax.psum_scatter(
        down_product, "tensor", scatter_dimension=0, tiled=True
    )
    block_output = residual + block_scattered.astype(f32)

    attended_gradient = jnp.dot(residual_low, w_out_spread.T, preferred_element_type=f32).astype(
        bf16
    )
    slots = jnp.arange(blocks, dtype=jnp.int32)
    query_grad, key_own, value_own, earlier = attend_back(
        queries, windows, firsts, low, slots, attended, [attended_gradient], logs, cosine,
        sine, kv_heads, group, rows, tile_rows,
    )
    for shared in wide:
        while len(shared.up) > 2:
            shared.step()
        shared.begin_up()
    earlier = [earlier[reach - d] for d in range(1, reach + 1)]
    if paired:
        crossing = exchange(earlier[0], "dp", 1)
        both_back = earlier[1] + jnp.where(odd, crossing, 0)
        both_back, crossing, attended_plain = tied((both_back, crossing, attended_plain))
        received = [from_behind(both_back, "dp", -2), jnp.where(odd, 0, crossing)]
    else:
        earlier, attended_plain = tied((earlier, attended_plain))
        received = [from_behind(earlier[d - 1], "dp", -d) for d in range(1, reach + 1)]
    out_shared = SharedProduct(attended_plain, residual_low, "dp", crossed)
    pair_shared.got, down_shared.got = out_shared.meet(pair_shared.got, down_shared.got)
    for shared in wide:
        shared.end_up()
        shared.begin_up()
    received, pair_shared.got, down_shared.got, out_shared.value = tied(
        (received, pair_shared.got, down_shared.got, out_shared.value)
    )
    key_value_grad = gather_back(
        key_own, value_own, received, cosine, sine, kv_heads, stretch, rows
    )
    split = heads * LANES
    attn_normed_part = (
        jnp.dot(query_grad, w_joined[:, :split].T, preferred_element_type=f32)
        + jnp.dot(key_value_grad, w_joined[:, split:].T, preferred_element_type=f32)
    ).astype(bf16)
    attn_scattered = lax.psum_scatter(attn_normed_part, "tensor", scatter_dimension=0, tiled=True)
    query_plain = jnp.dot(query_grad, query_spread.T, preferred_element_type=bf16)
    kv_plain = jnp.dot(key_value_grad, kv_spread.T, preferred_element_type=bf16)
    joined_shared = SharedProduct(
        attention_normed, jnp.concatenate([query_plain, kv_plain], axis=1), "dp", places
    )
    joined_shared.meet()
    grad_gate, grad_up = pair_shared.finish((0, width), (width, 2 * width))
    (grad_down,) = down_shared.finish((0, out_grad.shape[1]))
    joined_shared.step()
    joined_shared.value, grad_down = tied((joined_shared.value, grad_down))
    joined_shared.step()
    joined_shared.value, grad_gate = tied((joined_shared.value, grad_gate))
    joined_shared.step()
    joined_shared.value, grad_up, block_output = tied(
        (joined_shared.value, grad_up, block_output)
    )
    query_width = w_query.shape[1]
    kv_width = key_weight.shape[1]
    value_from = query_width + kv_width + gap
    grad_query, grad_key, grad_value = joined_shared.finish(
        (0, query_width),
        (query_width, query_width + kv_width),
        (value_from, value_from + kv_width),
    )
    (grad_out,) = out_shared.finish((0, out_grad.shape[1]))
    attn_gain_part = (
        jnp.sum(
            attn_normed_part.astype(f32) * attention_normed.astype(f32), axis=0, keepdims=True
        )
        / attn_gain
    )
    mlp_gain_part = jnp.sum(mlp_normed_grad * residual * inv_rms_mlp, axis=0, keepdims=True)
    gains = sum_everywhere(
        jnp.concatenate([attn_gain_part, mlp_gain_part], axis=0), ("tensor", "dp")
    )
    grad_attn_gain, grad_mlp_gain = gains[0], gains[1]

    attn_normed_grad = attn_scattered.astype(f32)
    input_part = normalize_back(block_input, inv_rms_attn, attn_gain, attn_normed_grad)
    input_grad = residual_grad + input_part
    return (
        block_output,
        input_grad,
        grad_query,
        grad_key,
        grad_value,
        grad_out,
        grad_gate,
        grad_up,
        grad_down,
        grad_attn_gain,
        grad_mlp_gain,
    )


def solution(mesh):
    in_specs = (
        P(("dp", "tensor"), None),
        P("dp"),
        P(),
        P(None, "tensor"),
        P(None, "tensor"),
        P(None, "tensor"),
        P("tensor", None),
        P(),
        P(None, "tensor"),
        P(None, "tensor"),
        P("tensor", None),
        P(("dp", "tensor"), None),
    )
    out_specs = (
        P(("dp", "tensor"), None),
        P(("dp", "tensor"), None),
        P(None, "tensor"),
        P(None, "tensor"),
        P(None, "tensor"),
        P("tensor", None),
        P(None, "tensor"),
        P(None, "tensor"),
        P("tensor", None),
        P(),
        P(),
    )

    return jax.shard_map(
        per_device, mesh=mesh, in_specs=in_specs, out_specs=out_specs, check_vma=False
    )
```

```python
import functools
import math

import jax
import jax.numpy as jnp
from jax import lax
from jax.experimental import pallas as pl
from jax.experimental.pallas import tpu as pltpu
from jax.sharding import PartitionSpec as P


HEAD_SIZE = 96
LONGEST_DOCUMENT = 2048

LANES = 128
HALF_LANES = LANES // 2
FAR = -1e30


epsilon = 1e-05
rope_base = 100000.0

f32 = jnp.float32
bf16 = jnp.bfloat16


def from_behind(value, axis, steps):
    if steps == 0:
        return value
    count = lax.axis_size(axis)
    leading, last = (max(0, -steps), min(count, count - steps))
    return lax.ppermute(value, axis, [(source, source + steps) for source in range(leading, last)])


def exchange(value, axis, distance):
    count = lax.axis_size(axis)
    return lax.ppermute(value, axis, [(i, i ^ distance) for i in range(count)])


def rope_tables(positions):
    half_size = HEAD_SIZE // 2
    frequency = rope_base ** (-jnp.arange(half_size, dtype=f32) * 2.0 / HEAD_SIZE)
    rest = jnp.zeros((HALF_LANES - half_size,), f32)
    spread = jnp.concatenate([frequency, rest, frequency, rest])
    sign = jnp.where(jnp.arange(LANES) < HALF_LANES, -1.0, 1.0).astype(f32)
    angles = positions.astype(f32)[:, None] * spread[None, :]
    return (jnp.cos(angles), jnp.sin(angles) * sign[None, :])


def spread_matrix(heads, gap_after=0, gap=0, dtype=bf16):
    half_size = HEAD_SIZE // 2
    rows = jnp.arange(heads * HEAD_SIZE, dtype=jnp.int32)
    inner = rows % HEAD_SIZE
    lane = (rows // HEAD_SIZE) * LANES + jnp.where(
        inner < half_size, inner, inner - half_size + HALF_LANES
    )
    if gap:
        cut = gap_after * HEAD_SIZE
        lane = jnp.concatenate([lane[:cut], jnp.full((gap,), -1, jnp.int32), lane[cut:]])
    columns = jnp.arange(heads * LANES, dtype=jnp.int32)
    return (lane[:, None] == columns[None, :]).astype(dtype)


def normalize(rows, gain):
    inv_rms = lax.rsqrt(jnp.mean(rows * rows, axis=-1, keepdims=True) + epsilon)
    return ((rows * inv_rms * gain).astype(bf16), inv_rms)


def normalize_back(rows, inv_rms, gain, normed_grad):
    weighted = normed_grad * gain
    inner = jnp.mean(weighted * rows, axis=-1, keepdims=True)
    return inv_rms * weighted - rows * inv_rms**3 * inner


def turn(value, cosine, sine):
    return value * cosine + pltpu.roll(value, HALF_LANES, 1) * sine


def turn_back(value, cosine, sine):
    return value * cosine - pltpu.roll(value, HALF_LANES, 1) * sine


def project_kernel(rotated, rows_ref, weight_ref, cosine_ref, sine_ref, *out_refs):
    product = jnp.dot(rows_ref[...], weight_ref[...], preferred_element_type=f32)
    cosine = cosine_ref[...]
    sine = sine_ref[...]
    head = 0
    for out_ref in out_refs:
        for place in range(out_ref.shape[1] // LANES):
            part = product[:, head * LANES : (head + 1) * LANES]
            if head < rotated:
                part = turn(part, cosine, sine)
            out_ref[:, place * LANES : (place + 1) * LANES] = part.astype(bf16)
            head += 1


def project(rows, weight, cosine, sine, rotated, widths, block):
    count, depth = rows.shape
    width = weight.shape[1]
    return pl.pallas_call(
        functools.partial(project_kernel, rotated),
        grid=(count // block,),
        in_specs=[
            pl.BlockSpec((block, depth), lambda i: (i, 0)),
            pl.BlockSpec((depth, width), lambda i: (0, 0)),
            pl.BlockSpec((block, LANES), lambda i: (i, 0)),
            pl.BlockSpec((block, LANES), lambda i: (i, 0)),
        ],
        out_specs=[pl.BlockSpec((block, part), lambda i: (i, 0)) for part in widths],
        out_shape=[jax.ShapeDtypeStruct((count, part), bf16) for part in widths],
        cost_estimate=pl.CostEstimate(
            flops=2 * count * depth * width,
            bytes_accessed=2 * (count * depth + depth * width + count * width),
            transcendentals=0,
        ),
        name="project",
    )(rows, weight, cosine, sine)


def pair_rows(ref, group):
    return jnp.concatenate([ref[:, h * LANES : (h + 1) * LANES] for h in range(group)], axis=0)


def place_row(ref, group):
    row = ref[0]
    return jnp.concatenate([row] * group, axis=1)


def masked(scores, first, last, base):
    index = lax.broadcasted_iota(jnp.int32, scores.shape, 0)
    allowed = (index >= first - base) & (index <= last - base)
    return jnp.where(allowed, scores, FAR)


def bounds(low_ref, query_block, rows, tile_rows, offset):
    high = (offset + (query_block + 1) * rows - 1) // tile_rows + 1
    return low_ref[query_block], high


def attend_kernel(tiles, group, factor, low_ref, query_ref, first_ref, *refs):
    keys = refs[:tiles]
    values = refs[tiles : 2 * tiles]
    out_ref, log_ref, key_window, value_turned, top, total, mixed = refs[2 * tiles :]
    query_block = pl.program_id(1)
    rows = query_ref.shape[0]
    stretch = keys[0].shape[0]
    tile_rows = key_window.shape[1]
    per_tile = stretch // tile_rows

    @pl.when(query_block == 0)
    def _():
        for tile in range(tiles):
            for part in range(per_tile):
                at = pl.ds(part * tile_rows, tile_rows)
                key_window[tile * per_tile + part] = keys[tile][at, :]
                value_turned[tile * per_tile + part] = values[tile][at, :].T

    offset = (tiles - 1) * stretch
    query = pair_rows(query_ref, group)
    first = place_row(first_ref, group)
    lane = lax.broadcasted_iota(jnp.int32, (1, rows), 1)
    last = jnp.concatenate([lane] * group, axis=1) + (offset + query_block * rows)
    top[...] = jnp.full_like(top, FAR)
    total[...] = jnp.zeros_like(total)
    mixed[...] = jnp.zeros_like(mixed)
    low, high = bounds(low_ref, query_block, rows, tile_rows, offset)

    def step(tile, unused):
        scores = lax.dot_general(
            key_window[tile], query, (((1,), (1,)), ((), ())), preferred_element_type=f32
        )
        scores = masked(scores, first, last, tile * tile_rows)
        before = top[...]
        after = jnp.maximum(before, jnp.max(scores, axis=0, keepdims=True))
        weights = jnp.exp2(scores * factor - after * factor)
        fade = jnp.exp2((before - after) * factor)
        top[...] = after
        total[...] = total[...] * fade + jnp.sum(weights, axis=0, keepdims=True)
        mixed[...] = mixed[...] * fade + jnp.dot(
            value_turned[tile], weights.astype(bf16), preferred_element_type=f32
        )
        return unused

    lax.fori_loop(low, high, step, 0)
    result = (mixed[...] / total[...]).T.astype(bf16)
    for head in range(group):
        out_ref[:, head * LANES : (head + 1) * LANES] = result[head * rows : (head + 1) * rows]
    log_ref[0, 0] = top[...] * factor + jnp.log2(total[...])


def window_specs(stretch, first_column):
    return [
        pl.BlockSpec((stretch, LANES), lambda g, i, *s, c=c: (0, c + g)) for c in first_column
    ]


def attend(queries_joined, windows, firsts, low, kv_heads, group, rows, tile_rows):
    stretch = queries_joined.shape[0]
    tiles = len(windows)
    blocks = stretch // rows
    pairs = group * rows
    window_tiles = tiles * stretch // tile_rows
    factor = HEAD_SIZE ** (-0.5) * math.log2(math.e)
    key_columns = [at for _, at in windows]
    value_columns = [at + kv_heads for _, at in windows]
    arrays = [a for a, _ in windows]
    grid_spec = pltpu.PrefetchScalarGridSpec(
        num_scalar_prefetch=1,
        grid=(kv_heads, blocks),
        in_specs=[
            pl.BlockSpec((rows, group * LANES), lambda g, i, *s: (i, g)),
            pl.BlockSpec((1, 1, rows), lambda g, i, *s: (i, 0, 0)),
        ]
        + window_specs(stretch, key_columns)
        + window_specs(stretch, value_columns),
        out_specs=[
            pl.BlockSpec((rows, group * LANES), lambda g, i, *s: (i, g)),
            pl.BlockSpec((1, 1, 1, pairs), lambda g, i, *s: (g, i, 0, 0)),
        ],
        scratch_shapes=[
            pltpu.VMEM((window_tiles, tile_rows, LANES), bf16),
            pltpu.VMEM((window_tiles, LANES, tile_rows), bf16),
            pltpu.VMEM((1, pairs), f32),
            pltpu.VMEM((1, pairs), f32),
            pltpu.VMEM((LANES, pairs), f32),
        ],
    )
    work = stretch * stretch * kv_heads * group
    return pl.pallas_call(
        functools.partial(attend_kernel, tiles, group, factor),
        grid_spec=grid_spec,
        out_shape=[
            jax.ShapeDtypeStruct((stretch, kv_heads * group * LANES), bf16),
            jax.ShapeDtypeStruct((kv_heads, blocks, 1, pairs), f32),
        ],
        cost_estimate=pl.CostEstimate(
            flops=16 * LANES * work, bytes_accessed=8 * stretch * stretch, transcendentals=work
        ),
        name="attend",
    )(low, queries_joined, firsts, *arrays, *arrays)


def attend_back_kernel(
    tiles, chunks, group, factor, scale, low_ref, slot_ref, query_ref, first_ref, *refs
):
    mixed_ref, log_ref, cosine_ref, sine_ref = refs[:4]
    grad_refs = refs[4 : 4 + chunks]
    refs = refs[4 + chunks :]
    keys = refs[:tiles]
    values = refs[tiles : 2 * tiles]
    (
        query_out,
        key_own,
        value_own,
        earlier_out,
        key_out,
        value_out,
        key_window,
        value_window,
        key_turned,
        query_total,
    ) = refs[2 * tiles :]
    query_block = pl.program_id(1)
    rows = query_ref.shape[0]
    stretch = keys[0].shape[0]
    tile_rows = key_window.shape[1]
    per_tile = stretch // tile_rows

    @pl.when(query_block == 0)
    def _():
        key_out[...] = jnp.zeros_like(key_out)
        value_out[...] = jnp.zeros_like(value_out)
        for tile in range(tiles):
            for part in range(per_tile):
                at = pl.ds(part * tile_rows, tile_rows)
                key_window[tile * per_tile + part] = keys[tile][at, :]
                key_turned[tile * per_tile + part] = keys[tile][at, :].T
                value_window[tile * per_tile + part] = values[tile][at, :]

    offset = (tiles - 1) * stretch
    query = pair_rows(query_ref, group)
    grad = jnp.concatenate(
        [ref[:, h * LANES : (h + 1) * LANES] for h in range(group) for ref in grad_refs], axis=0
    )
    mixed = pair_rows(mixed_ref, group)
    inner = jnp.sum((grad.astype(f32) * mixed.astype(f32)).T, axis=0, keepdims=True)
    log_total = log_ref[0, 0]
    first = place_row(first_ref, group)
    lane = lax.broadcasted_iota(jnp.int32, (1, rows), 1)
    last = jnp.concatenate([lane] * group, axis=1) + (offset + query_block * rows)
    query_total[...] = jnp.zeros_like(query_total)
    low, high = bounds(low_ref, query_block, rows, tile_rows, offset)
    both_last = (((1,), (1,)), ((), ()))

    def step(tile, unused):
        scores = lax.dot_general(key_window[tile], query, both_last, preferred_element_type=f32)
        scores = masked(scores, first, last, tile * tile_rows)
        weights = jnp.exp2(scores * factor - log_total)
        weight_grad = lax.dot_general(
            value_window[tile], grad, both_last, preferred_element_type=f32
        )
        score_grad = (weights * (weight_grad - inner) * scale).astype(bf16)
        at = pl.ds(pl.multiple_of(tile * tile_rows, tile_rows), tile_rows)
        value_out[at, :] += jnp.dot(weights.astype(bf16), grad, preferred_element_type=f32)
        key_out[at, :] += jnp.dot(score_grad, query, preferred_element_type=f32)
        query_total[...] += jnp.dot(key_turned[tile], score_grad, preferred_element_type=f32)
        return unused

    lax.fori_loop(low, high, step, 0)
    result = query_total[...].T
    for head in range(group):
        part = result[head * rows : (head + 1) * rows]
        query_out[:, head * LANES : (head + 1) * LANES] = turn_back(
            part, cosine_ref[...], sine_ref[...]
        ).astype(bf16)

    @pl.when(query_block == pl.num_programs(1) - 1)
    def _():
        for tile in range(tiles - 1):
            at = pl.ds(tile * stretch, stretch)
            earlier_out[tile, 0] = key_out[at, :].astype(bf16)
            earlier_out[tile, 1] = value_out[at, :].astype(bf16)
        key_own[...] = key_out[pl.ds(offset, stretch), :]
        value_own[...] = value_out[pl.ds(offset, stretch), :]


def attend_back(
    queries_joined, windows, firsts, low, slots, mixed, grads, logs, cosine, sine,
    kv_heads, group, rows, tile_rows,
):
    stretch = queries_joined.shape[0]
    tiles = len(windows)
    blocks = stretch // rows
    pairs = group * rows
    window_tiles = tiles * stretch // tile_rows
    chunks = len(grads)
    scale = HEAD_SIZE ** (-0.5)
    factor = scale * math.log2(math.e)
    key_columns = [at for _, at in windows]
    value_columns = [at + kv_heads for _, at in windows]
    arrays = [a for a, _ in windows]
    heads_spec = pl.BlockSpec((rows, group * LANES), lambda g, i, *s: (i, g))
    table_spec = pl.BlockSpec((rows, LANES), lambda g, i, *s: (i, 0))
    own_spec = pl.BlockSpec((stretch, LANES), lambda g, i, *s: (0, g))
    earlier_spec = pl.BlockSpec((tiles - 1, 2, stretch, LANES), lambda g, i, *s: (0, 0, 0, g))
    grid_spec = pltpu.PrefetchScalarGridSpec(
        num_scalar_prefetch=2,
        grid=(kv_heads, blocks),
        in_specs=[
            heads_spec,
            pl.BlockSpec((1, 1, rows), lambda g, i, *s: (i, 0, 0)),
            heads_spec,
            pl.BlockSpec((1, 1, 1, pairs), lambda g, i, *s: (g, i, 0, 0)),
            table_spec,
            table_spec,
        ]
        + [
            pl.BlockSpec((rows // chunks, group * LANES), lambda g, i, low, slot: (slot[i], g))
        ]
        * chunks
        + window_specs(stretch, key_columns)
        + window_specs(stretch, value_columns),
        out_specs=[heads_spec, own_spec, own_spec, earlier_spec],
        scratch_shapes=[
            pltpu.VMEM((tiles * stretch, LANES), f32),
            pltpu.VMEM((tiles * stretch, LANES), f32),
            pltpu.VMEM((window_tiles, tile_rows, LANES), bf16),
            pltpu.VMEM((window_tiles, tile_rows, LANES), bf16),
            pltpu.VMEM((window_tiles, LANES, tile_rows), bf16),
            pltpu.VMEM((LANES, pairs), f32),
        ],
    )
    work = stretch * stretch * kv_heads * group
    return pl.pallas_call(
        functools.partial(attend_back_kernel, tiles, chunks, group, factor, scale),
        grid_spec=grid_spec,
        out_shape=[
            jax.ShapeDtypeStruct((stretch, kv_heads * group * LANES), bf16),
            jax.ShapeDtypeStruct((stretch, kv_heads * LANES), f32),
            jax.ShapeDtypeStruct((stretch, kv_heads * LANES), f32),
            jax.ShapeDtypeStruct((tiles - 1, 2, stretch, kv_heads * LANES), bf16),
        ],
        cost_estimate=pl.CostEstimate(
            flops=40 * LANES * work, bytes_accessed=16 * stretch * stretch, transcendentals=work
        ),
        name="attend_back",
    )(low, slots, queries_joined, firsts, mixed, logs, cosine, sine, *grads, *arrays, *arrays)


def gather_back_kernel(kv_heads, parts, key_ref, value_ref, cosine_ref, sine_ref, *refs):
    out_ref = refs[parts]
    for head in range(kv_heads):
        at = pl.ds(head * LANES, LANES)
        key = key_ref[:, at]
        value = value_ref[:, at]
        for part in range(parts):
            key = key + refs[part][0, :, at].astype(f32)
            value = value + refs[part][1, :, at].astype(f32)
        out_ref[:, at] = turn_back(key, cosine_ref[...], sine_ref[...]).astype(bf16)
        out_ref[:, pl.ds((kv_heads + head) * LANES, LANES)] = value.astype(bf16)


def gather_back(key_totals, value_totals, received, cosine, sine, kv_heads, stretch, block):
    width = kv_heads * LANES
    own = pl.BlockSpec((block, width), lambda i: (i, 0))
    other = pl.BlockSpec((2, block, width), lambda i: (0, i, 0))
    table = pl.BlockSpec((block, LANES), lambda i: (i, 0))
    return pl.pallas_call(
        functools.partial(gather_back_kernel, kv_heads, len(received)),
        grid=(stretch // block,),
        in_specs=[own, own, table, table] + [other] * len(received),
        out_specs=pl.BlockSpec((block, 2 * width), lambda i: (i, 0)),
        out_shape=jax.ShapeDtypeStruct((stretch, 2 * width), bf16),
        name="gather_back",
    )(key_totals, value_totals, cosine, sine, *received)


class SharedProduct:

    def __init__(self, left, right, axis, order):
        self.left, self.right, self.axis, self.order = left, right, axis, order
        self.size = left.shape[1] // 2
        self.sent = self.times(0, True).astype(bf16)

    def bit(self, place):
        return (lax.axis_index(self.axis) >> place) & 1

    def times(self, place, other):
        bit = self.bit(self.order[place])
        offset = ((1 - bit) if other else bit) * self.size
        part = lax.dynamic_slice_in_dim(self.left, offset, self.size, 1)
        return jnp.dot(part.T, self.right, preferred_element_type=f32)

    def meet(self, *others):
        got = exchange(self.sent, self.axis, 1 << self.order[0])
        if others:
            got, *others = lax.optimization_barrier((got,) + others)
        self.value = self.times(0, False) + got.astype(f32)
        self.down = list(self.order[1:])
        self.up = list(reversed(self.order))
        return others

    def step(self):
        if self.down:
            place = self.down.pop(0)
            bit = self.bit(place)
            size = self.value.shape[0] // 2
            sent = lax.dynamic_slice_in_dim(self.value, (1 - bit) * size, size, 0).astype(bf16)
            got = exchange(sent, self.axis, 1 << place)
            kept = lax.dynamic_slice_in_dim(self.value, bit * size, size, 0)
            self.value = kept + got.astype(f32)
            return self.value
        self.begin_up()
        return self.end_up()

    def begin_up(self):
        self.place = self.up.pop(0)
        self.value = self.value.astype(bf16)
        self.got = exchange(self.value, self.axis, 1 << self.place)

    def end_up(self):
        self.value = self.joined(self.value, self.got)
        return self.value

    def joined(self, whole, got):
        return jnp.where(
            self.bit(self.place) == 1,
            jnp.concatenate([got, whole], axis=0),
            jnp.concatenate([whole, got], axis=0),
        )

    def finish(self, *spans):
        while len(self.up) > 1:
            self.step()
        if self.up:
            self.begin_up()
        return [
            self.joined(self.value[:, a:b], self.got[:, a:b]).astype(f32)
            for a, b in spans
        ]


def scatter_low(product):
    return lax.psum_scatter(product.astype(bf16), "tensor", scatter_dimension=0, tiled=True)


def gather_rows(rows):
    return lax.all_gather(rows, "tensor", axis=0, tiled=True)


def per_device(
    block_input,
    positions,
    attn_gain,
    w_query,
    key_weight,
    value_weight,
    w_out,
    mlp_gain,
    w_gate,
    w_up,
    w_down,
    out_grad,
):
    stretch = positions.shape[0]
    reach = LONGEST_DOCUMENT // stretch
    heads = w_query.shape[1] // HEAD_SIZE
    kv_heads = key_weight.shape[1] // HEAD_SIZE
    group = heads // kv_heads
    rows = min(256, stretch)
    tile_rows = min(512, stretch)
    blocks = stretch // rows
    places = list(range((lax.axis_size("dp") - 1).bit_length()))
    crossed = places[:1] + places[:0:-1]
    tied = lax.optimization_barrier

    normed_own, inv_rms_attn = normalize(block_input, attn_gain)
    normed_own, out_own = tied((normed_own, out_grad.astype(bf16)))
    attention_normed = gather_rows(normed_own)
    out_low = gather_rows(out_own)

    query_spread = spread_matrix(heads)
    gap = -kv_heads * HEAD_SIZE % LANES
    kv_spread = spread_matrix(2 * kv_heads, kv_heads, gap)
    all_spread = spread_matrix(heads + 2 * kv_heads)
    w_joined = jnp.dot(
        jnp.concatenate([w_query, key_weight, value_weight], axis=1), all_spread,
        preferred_element_type=bf16,
    )
    w_out_spread = jnp.dot(query_spread.T, w_out, preferred_element_type=bf16)
    w_pair = jnp.concatenate([w_gate, w_up], axis=1)
    cosine, sine = rope_tables(positions)
    local = jnp.arange(stretch, dtype=jnp.int32)
    window_first = reach * stretch + local - positions
    firsts = window_first.reshape(blocks, 1, rows)
    low = jnp.min(window_first.reshape(blocks, rows), axis=1) // tile_rows

    queries, key_value = project(
        attention_normed, w_joined, cosine, sine, heads + kv_heads,
        (heads * LANES, 2 * kv_heads * LANES), rows,
    )
    paired = reach == 2 and lax.axis_size("dp") % 2 == 0
    odd = lax.axis_index("dp") % 2 == 1
    if paired:
        two_back = from_behind(key_value, "dp", 2)
        one_back = exchange(jnp.where(odd, two_back, key_value), "dp", 1)
        windows = [(two_back, 0), (one_back, 0), (key_value, 0)]
    else:
        windows = [(from_behind(key_value, "dp", d), 0) for d in range(reach, -1, -1)]
    attended, logs = attend(queries, windows, firsts, low, kv_heads, group, rows, tile_rows)
    hidden_grad = jnp.dot(out_low, w_down.T, preferred_element_type=f32)
    mixed = scatter_low(jnp.dot(attended, w_out_spread, preferred_element_type=f32))
    mixed, hidden_grad = tied((mixed, hidden_grad))
    residual = block_input + mixed.astype(f32)
    mlp_normed_own, inv_rms_mlp = normalize(residual, mlp_gain)
    normed_mlp = gather_rows(mlp_normed_own)

    width = w_gate.shape[1]
    pre = jnp.dot(normed_mlp, w_pair, preferred_element_type=f32)
    gate_pre, up_proj = pre[:, :width], pre[:, width:]
    sigmoid_gate = jax.nn.sigmoid(gate_pre)
    silu_gate = gate_pre * sigmoid_gate
    hidden = (silu_gate * up_proj).astype(bf16)
    gate_grad = hidden_grad * up_proj * sigmoid_gate * (1.0 + gate_pre * (1.0 - sigmoid_gate))
    up_grad = hidden_grad * silu_gate
    pair_grad = jnp.concatenate([gate_grad.astype(bf16), up_grad.astype(bf16)], axis=1)
    mlp_product = jnp.dot(pair_grad, w_pair.T, preferred_element_type=f32).astype(bf16)
    mlp_product, pair_grad, hidden = tied((mlp_product, pair_grad, hidden))
    mlp_scattered = scatter_low(mlp_product)
    down_product = jnp.dot(hidden, w_down, preferred_element_type=f32).astype(bf16)
    pair_shared = SharedProduct(normed_mlp, pair_grad, "dp", places)
    down_shared = SharedProduct(hidden, out_low, "dp", crossed)
    wide = (pair_shared, down_shared)
    for shared in wide:
        shared.meet()
        shared.step()
    mlp_scattered, down_product, pair_shared.value, down_shared.value = tied(
        (mlp_scattered, down_product, pair_shared.value, down_shared.value)
    )
    mlp_normed_grad = mlp_scattered.astype(f32)
    residual_part = normalize_back(residual, inv_rms_mlp, mlp_gain, mlp_normed_grad)
    residual_grad = out_grad + residual_part
    residual_low = gather_rows(residual_grad.astype(bf16))
    attended_plain = jnp.dot(attended, query_spread.T, preferred_element_type=bf16)
    for shared in wide:
        for _ in range(len(places) - 1):
            shared.step()
    residual_low, down_product, pair_shared.value, down_shared.value, attended_plain = tied(
        (residual_low, down_product, pair_shared.value, down_shared.value, attended_plain)
    )
    block_scattered = lax.psum_scatter(
        down_product, "tensor", scatter_dimension=0, tiled=True
    )
    block_output = residual + block_scattered.astype(f32)

    attended_gradient = jnp.dot(residual_low, w_out_spread.T, preferred_element_type=f32).astype(
        bf16
    )
    slots = jnp.arange(blocks, dtype=jnp.int32)
    query_grad, key_own, value_own, earlier = attend_back(
        queries, windows, firsts, low, slots, attended, [attended_gradient], logs, cosine,
        sine, kv_heads, group, rows, tile_rows,
    )
    for shared in wide:
        while len(shared.up) > 2:
            shared.step()
        shared.begin_up()
    earlier = [earlier[reach - d] for d in range(1, reach + 1)]
    if paired:
        crossing = exchange(earlier[0], "dp", 1)
        both_back = earlier[1] + jnp.where(odd, crossing, 0)
        both_back, crossing, attended_plain = tied((both_back, crossing, attended_plain))
        both_received = from_behind(both_back, "dp", -2)
        received = [both_received, jnp.where(odd, 0, crossing)]
    else:
        earlier, attended_plain = tied((earlier, attended_plain))
        received = [from_behind(earlier[d - 1], "dp", -d) for d in range(1, reach + 1)]
    out_shared = SharedProduct(attended_plain, residual_low, "dp", crossed)
    pair_shared.got, down_shared.got = out_shared.meet(pair_shared.got, down_shared.got)
    for shared in wide:
        shared.end_up()
        shared.begin_up()
    query_plain = jnp.dot(query_grad, query_spread.T, preferred_element_type=bf16)
    query_shared = SharedProduct(attention_normed, query_plain, "dp", places)
    query_shared.meet()
    received, pair_shared.got, down_shared.got, out_shared.value, query_shared.value = tied(
        (received, pair_shared.got, down_shared.got, out_shared.value, query_shared.value)
    )
    key_value_grad = gather_back(
        key_own, value_own, received, cosine, sine, kv_heads, stretch, rows
    )
    split = heads * LANES
    attn_normed_part = (
        jnp.dot(query_grad, w_joined[:, :split].T, preferred_element_type=f32)
        + jnp.dot(key_value_grad, w_joined[:, split:].T, preferred_element_type=f32)
    ).astype(bf16)
    attn_scattered = lax.psum_scatter(attn_normed_part, "tensor", scatter_dimension=0, tiled=True)
    attn_gain_part = (
        jnp.sum(
            attn_normed_part.astype(f32) * attention_normed.astype(f32), axis=0, keepdims=True
        )
        / attn_gain
    )
    mlp_gain_part = jnp.sum(mlp_normed_grad * residual * inv_rms_mlp, axis=0, keepdims=True)
    gains = jnp.concatenate([attn_gain_part, mlp_gain_part], axis=0)
    rounds = [
        (axis, 1 << place)
        for axis in ("tensor", "dp")
        for place in range((lax.axis_size(axis) - 1).bit_length())
    ]
    kv_plain = jnp.dot(key_value_grad, kv_spread.T, preferred_element_type=bf16)
    kv_shared = SharedProduct(attention_normed, kv_plain, "dp", crossed)
    kv_shared.meet()
    grad_gate, grad_up = pair_shared.finish((0, width), (width, 2 * width))
    (grad_down,) = down_shared.finish((0, out_grad.shape[1]))
    outputs = [grad_down, grad_gate, grad_up, block_output]
    for place in range(len(outputs)):
        query_shared.step()
        kv_shared.step()
        if rounds:
            axis, distance = rounds.pop(0)
            gains = gains + exchange(gains, axis, distance)
        kv_shared.value, query_shared.value, gains, outputs[place] = tied(
            (kv_shared.value, query_shared.value, gains, outputs[place])
        )
    grad_down, grad_gate, grad_up, block_output = outputs
    for axis, distance in rounds:
        gains = gains + exchange(gains, axis, distance)
    grad_attn_gain, grad_mlp_gain = gains[0], gains[1]
    query_width = w_query.shape[1]
    kv_width = key_weight.shape[1]
    (grad_query,) = query_shared.finish((0, query_width))
    grad_key, grad_value = kv_shared.finish(
        (0, kv_width), (kv_width + gap, 2 * kv_width + gap)
    )
    (grad_out,) = out_shared.finish((0, out_grad.shape[1]))
    attn_normed_grad = attn_scattered.astype(f32)
    input_part = normalize_back(block_input, inv_rms_attn, attn_gain, attn_normed_grad)
    input_grad = residual_grad + input_part
    return (
        block_output,
        input_grad,
        grad_query,
        grad_key,
        grad_value,
        grad_out,
        grad_gate,
        grad_up,
        grad_down,
        grad_attn_gain,
        grad_mlp_gain,
    )


def solution(mesh):
    in_specs = (
        P(("dp", "tensor"), None),
        P("dp"),
        P(),
        P(None, "tensor"),
        P(None, "tensor"),
        P(None, "tensor"),
        P("tensor", None),
        P(),
        P(None, "tensor"),
        P(None, "tensor"),
        P("tensor", None),
        P(("dp", "tensor"), None),
    )
    out_specs = (
        P(("dp", "tensor"), None),
        P(("dp", "tensor"), None),
        P(None, "tensor"),
        P(None, "tensor"),
        P(None, "tensor"),
        P("tensor", None),
        P(None, "tensor"),
        P(None, "tensor"),
        P("tensor", None),
        P(),
        P(),
    )

    return jax.shard_map(
        per_device, mesh=mesh, in_specs=in_specs, out_specs=out_specs, check_vma=False
    )
```

```python
import functools
import math

import jax
import jax.numpy as jnp
from jax import lax
from jax.experimental import pallas as pl
from jax.experimental.pallas import tpu as pltpu
from jax.sharding import PartitionSpec as P


HEAD_SIZE = 96
LONGEST_DOCUMENT = 2048

LANES = 128
HALF_LANES = LANES // 2
FAR = -1e30


epsilon = 1e-05
rope_base = 100000.0

f32 = jnp.float32
bf16 = jnp.bfloat16


def from_behind(value, axis, steps):
    if steps == 0:
        return value
    count = lax.axis_size(axis)
    leading, last = (max(0, -steps), min(count, count - steps))
    return lax.ppermute(value, axis, [(source, source + steps) for source in range(leading, last)])


def exchange(value, axis, distance):
    count = lax.axis_size(axis)
    return lax.ppermute(value, axis, [(i, i ^ distance) for i in range(count)])


def rope_tables(positions):
    half_size = HEAD_SIZE // 2
    frequency = rope_base ** (-jnp.arange(half_size, dtype=f32) * 2.0 / HEAD_SIZE)
    rest = jnp.zeros((HALF_LANES - half_size,), f32)
    spread = jnp.concatenate([frequency, rest, frequency, rest])
    sign = jnp.where(jnp.arange(LANES) < HALF_LANES, -1.0, 1.0).astype(f32)
    angles = positions.astype(f32)[:, None] * spread[None, :]
    return (jnp.cos(angles), jnp.sin(angles) * sign[None, :])


def spread_matrix(heads, gap_after=0, gap=0, dtype=bf16):
    half_size = HEAD_SIZE // 2
    rows = jnp.arange(heads * HEAD_SIZE, dtype=jnp.int32)
    inner = rows % HEAD_SIZE
    lane = (rows // HEAD_SIZE) * LANES + jnp.where(
        inner < half_size, inner, inner - half_size + HALF_LANES
    )
    if gap:
        cut = gap_after * HEAD_SIZE
        lane = jnp.concatenate([lane[:cut], jnp.full((gap,), -1, jnp.int32), lane[cut:]])
    columns = jnp.arange(heads * LANES, dtype=jnp.int32)
    return (lane[:, None] == columns[None, :]).astype(dtype)


def normalize(rows, gain):
    inv_rms = lax.rsqrt(jnp.mean(rows * rows, axis=-1, keepdims=True) + epsilon)
    return ((rows * inv_rms * gain).astype(bf16), inv_rms)


def normalize_back(rows, inv_rms, gain, normed_grad):
    weighted = normed_grad * gain
    inner = jnp.mean(weighted * rows, axis=-1, keepdims=True)
    return inv_rms * weighted - rows * inv_rms**3 * inner


def turn(value, cosine, sine):
    return value * cosine + pltpu.roll(value, HALF_LANES, 1) * sine


def turn_back(value, cosine, sine):
    return value * cosine - pltpu.roll(value, HALF_LANES, 1) * sine


def project_kernel(rotated, rows_ref, weight_ref, cosine_ref, sine_ref, *out_refs):
    product = jnp.dot(rows_ref[...], weight_ref[...], preferred_element_type=f32)
    cosine = cosine_ref[...]
    sine = sine_ref[...]
    head = 0
    for out_ref in out_refs:
        for place in range(out_ref.shape[1] // LANES):
            part = product[:, head * LANES : (head + 1) * LANES]
            if head < rotated:
                part = turn(part, cosine, sine)
            out_ref[:, place * LANES : (place + 1) * LANES] = part.astype(bf16)
            head += 1


def project(rows, weight, cosine, sine, rotated, widths, block):
    count, depth = rows.shape
    width = weight.shape[1]
    return pl.pallas_call(
        functools.partial(project_kernel, rotated),
        grid=(count // block,),
        in_specs=[
            pl.BlockSpec((block, depth), lambda i: (i, 0)),
            pl.BlockSpec((depth, width), lambda i: (0, 0)),
            pl.BlockSpec((block, LANES), lambda i: (i, 0)),
            pl.BlockSpec((block, LANES), lambda i: (i, 0)),
        ],
        out_specs=[pl.BlockSpec((block, part), lambda i: (i, 0)) for part in widths],
        out_shape=[jax.ShapeDtypeStruct((count, part), bf16) for part in widths],
        cost_estimate=pl.CostEstimate(
            flops=2 * count * depth * width,
            bytes_accessed=2 * (count * depth + depth * width + count * width),
            transcendentals=0,
        ),
        name="project",
    )(rows, weight, cosine, sine)


def pair_rows(ref, group):
    return jnp.concatenate([ref[:, h * LANES : (h + 1) * LANES] for h in range(group)], axis=0)


def place_row(ref, group):
    row = ref[0]
    return jnp.concatenate([row] * group, axis=1)


def masked(scores, first, last, base):
    index = lax.broadcasted_iota(jnp.int32, scores.shape, 0)
    allowed = (index >= first - base) & (index <= last - base)
    return jnp.where(allowed, scores, FAR)


def bounds(low_ref, query_block, rows, tile_rows, offset):
    high = (offset + (query_block + 1) * rows - 1) // tile_rows + 1
    return low_ref[0, query_block], high


def sweep(low_ref, query_block, rows, tile_rows, offset, step):
    low, high = bounds(low_ref, query_block, rows, tile_rows, offset)
    full_from = low_ref[1, query_block]
    full_to = (offset + query_block * rows) // tile_rows

    def turn_over(tile, unused):
        whole = (tile >= full_from) & (tile < full_to)
        pl.when(whole)(lambda: step(tile, False))
        pl.when(jnp.logical_not(whole))(lambda: step(tile, True))
        return unused

    lax.fori_loop(low, high, turn_over, 0)


def attend_kernel(tiles, group, factor, low_ref, query_ref, first_ref, *refs):
    keys = refs[:tiles]
    values = refs[tiles : 2 * tiles]
    out_ref, log_ref, key_window, value_turned, top, total, mixed = refs[2 * tiles :]
    query_block = pl.program_id(1)
    rows = query_ref.shape[0]
    stretch = keys[0].shape[0]
    tile_rows = key_window.shape[1]
    per_tile = stretch // tile_rows

    @pl.when(query_block == 0)
    def _():
        for tile in range(tiles):
            for part in range(per_tile):
                place = tile * per_tile + part

                @pl.when(place >= low_ref[0, 0])
                def _(tile=tile, place=place, at=pl.ds(part * tile_rows, tile_rows)):
                    key_window[place] = keys[tile][at, :]
                    value_turned[place] = values[tile][at, :].T

    offset = (tiles - 1) * stretch
    query = pair_rows(query_ref, group)
    first = place_row(first_ref, group)
    lane = lax.broadcasted_iota(jnp.int32, (1, rows), 1)
    last = jnp.concatenate([lane] * group, axis=1) + (offset + query_block * rows)
    top[...] = jnp.full_like(top, FAR)
    total[...] = jnp.zeros_like(total)
    mixed[...] = jnp.zeros_like(mixed)

    def step(tile, check):
        scores = lax.dot_general(
            key_window[tile], query, (((1,), (1,)), ((), ())), preferred_element_type=f32
        )
        if check:
            scores = masked(scores, first, last, tile * tile_rows)
        before = top[...]
        after = jnp.maximum(before, jnp.max(scores, axis=0, keepdims=True))
        weights = jnp.exp2(scores * factor - after * factor)
        fade = jnp.exp2((before - after) * factor)
        top[...] = after
        total[...] = total[...] * fade + jnp.sum(weights, axis=0, keepdims=True)
        mixed[...] = mixed[...] * fade + jnp.dot(
            value_turned[tile], weights.astype(bf16), preferred_element_type=f32
        )

    sweep(low_ref, query_block, rows, tile_rows, offset, step)
    result = (mixed[...] / total[...]).T.astype(bf16)
    for head in range(group):
        out_ref[:, head * LANES : (head + 1) * LANES] = result[head * rows : (head + 1) * rows]
    log_ref[0, 0] = top[...] * factor + jnp.log2(total[...])


def window_specs(stretch, first_column):
    return [
        pl.BlockSpec((stretch, LANES), lambda g, i, *s, c=c: (0, c + g)) for c in first_column
    ]


def attend(queries_joined, windows, firsts, low, kv_heads, group, rows, tile_rows):
    stretch = queries_joined.shape[0]
    tiles = len(windows)
    blocks = stretch // rows
    pairs = group * rows
    window_tiles = tiles * stretch // tile_rows
    factor = HEAD_SIZE ** (-0.5) * math.log2(math.e)
    key_columns = [at for _, at in windows]
    value_columns = [at + kv_heads for _, at in windows]
    arrays = [a for a, _ in windows]
    grid_spec = pltpu.PrefetchScalarGridSpec(
        num_scalar_prefetch=1,
        grid=(kv_heads, blocks),
        in_specs=[
            pl.BlockSpec((rows, group * LANES), lambda g, i, *s: (i, g)),
            pl.BlockSpec((1, 1, rows), lambda g, i, *s: (i, 0, 0)),
        ]
        + window_specs(stretch, key_columns)
        + window_specs(stretch, value_columns),
        out_specs=[
            pl.BlockSpec((rows, group * LANES), lambda g, i, *s: (i, g)),
            pl.BlockSpec((1, 1, 1, pairs), lambda g, i, *s: (g, i, 0, 0)),
        ],
        scratch_shapes=[
            pltpu.VMEM((window_tiles, tile_rows, LANES), bf16),
            pltpu.VMEM((window_tiles, LANES, tile_rows), bf16),
            pltpu.VMEM((1, pairs), f32),
            pltpu.VMEM((1, pairs), f32),
            pltpu.VMEM((LANES, pairs), f32),
        ],
    )
    work = stretch * stretch * kv_heads * group
    return pl.pallas_call(
        functools.partial(attend_kernel, tiles, group, factor),
        grid_spec=grid_spec,
        out_shape=[
            jax.ShapeDtypeStruct((stretch, kv_heads * group * LANES), bf16),
            jax.ShapeDtypeStruct((kv_heads, blocks, 1, pairs), f32),
        ],
        cost_estimate=pl.CostEstimate(
            flops=16 * LANES * work, bytes_accessed=8 * stretch * stretch, transcendentals=work
        ),
        name="attend",
    )(low, queries_joined, firsts, *arrays, *arrays)


def attend_back_kernel(
    tiles, chunks, group, factor, scale, low_ref, slot_ref, query_ref, first_ref, *refs
):
    mixed_ref, log_ref, cosine_ref, sine_ref = refs[:4]
    grad_refs = refs[4 : 4 + chunks]
    refs = refs[4 + chunks :]
    keys = refs[:tiles]
    values = refs[tiles : 2 * tiles]
    refs = refs[2 * tiles :]
    earlier_outs = refs[3 : 2 + tiles]
    query_out, key_own, value_own = refs[:3]
    (
        key_out,
        value_out,
        key_window,
        value_window,
        key_turned,
        query_total,
    ) = refs[2 + tiles :]
    query_block = pl.program_id(1)
    rows = query_ref.shape[0]
    stretch = keys[0].shape[0]
    tile_rows = key_window.shape[1]
    per_tile = stretch // tile_rows

    @pl.when(query_block == 0)
    def _():
        key_out[...] = jnp.zeros_like(key_out)
        value_out[...] = jnp.zeros_like(value_out)
        for tile in range(tiles):
            for part in range(per_tile):
                place = tile * per_tile + part

                @pl.when(place >= low_ref[0, 0])
                def _(tile=tile, place=place, at=pl.ds(part * tile_rows, tile_rows)):
                    key_window[place] = keys[tile][at, :]
                    key_turned[place] = keys[tile][at, :].T
                    value_window[place] = values[tile][at, :]

    offset = (tiles - 1) * stretch
    query = pair_rows(query_ref, group)
    grad = jnp.concatenate(
        [ref[:, h * LANES : (h + 1) * LANES] for h in range(group) for ref in grad_refs], axis=0
    )
    mixed = pair_rows(mixed_ref, group)
    inner = jnp.sum((grad.astype(f32) * mixed.astype(f32)).T, axis=0, keepdims=True)
    log_total = log_ref[0, 0]
    first = place_row(first_ref, group)
    lane = lax.broadcasted_iota(jnp.int32, (1, rows), 1)
    last = jnp.concatenate([lane] * group, axis=1) + (offset + query_block * rows)
    query_total[...] = jnp.zeros_like(query_total)
    both_last = (((1,), (1,)), ((), ()))

    def step(tile, check):
        scores = lax.dot_general(key_window[tile], query, both_last, preferred_element_type=f32)
        if check:
            scores = masked(scores, first, last, tile * tile_rows)
        weights = jnp.exp2(scores * factor - log_total)
        weight_grad = lax.dot_general(
            value_window[tile], grad, both_last, preferred_element_type=f32
        )
        score_grad = (weights * (weight_grad - inner) * scale).astype(bf16)
        at = pl.ds(pl.multiple_of(tile * tile_rows, tile_rows), tile_rows)
        value_out[at, :] += jnp.dot(weights.astype(bf16), grad, preferred_element_type=f32)
        key_out[at, :] += jnp.dot(score_grad, query, preferred_element_type=f32)
        query_total[...] += jnp.dot(key_turned[tile], score_grad, preferred_element_type=f32)

    sweep(low_ref, query_block, rows, tile_rows, offset, step)
    result = query_total[...].T
    for head in range(group):
        part = result[head * rows : (head + 1) * rows]
        query_out[:, head * LANES : (head + 1) * LANES] = turn_back(
            part, cosine_ref[...], sine_ref[...]
        ).astype(bf16)

    @pl.when(query_block == pl.num_programs(1) - 1)
    def _():
        for tile in range(tiles - 1):
            at = pl.ds(tile * stretch, stretch)
            earlier_outs[tile][0] = key_out[at, :].astype(bf16)
            earlier_outs[tile][1] = value_out[at, :].astype(bf16)
        key_own[...] = key_out[pl.ds(offset, stretch), :]
        value_own[...] = value_out[pl.ds(offset, stretch), :]


def attend_back(
    queries_joined, windows, firsts, low, slots, mixed, grads, logs, cosine, sine,
    kv_heads, group, rows, tile_rows,
):
    stretch = queries_joined.shape[0]
    tiles = len(windows)
    blocks = stretch // rows
    pairs = group * rows
    window_tiles = tiles * stretch // tile_rows
    chunks = len(grads)
    scale = HEAD_SIZE ** (-0.5)
    factor = scale * math.log2(math.e)
    key_columns = [at for _, at in windows]
    value_columns = [at + kv_heads for _, at in windows]
    arrays = [a for a, _ in windows]
    heads_spec = pl.BlockSpec((rows, group * LANES), lambda g, i, *s: (i, g))
    table_spec = pl.BlockSpec((rows, LANES), lambda g, i, *s: (i, 0))
    own_spec = pl.BlockSpec((stretch, LANES), lambda g, i, *s: (0, g))
    earlier_spec = pl.BlockSpec((2, stretch, LANES), lambda g, i, *s: (0, 0, g))
    grid_spec = pltpu.PrefetchScalarGridSpec(
        num_scalar_prefetch=2,
        grid=(kv_heads, blocks),
        in_specs=[
            heads_spec,
            pl.BlockSpec((1, 1, rows), lambda g, i, *s: (i, 0, 0)),
            heads_spec,
            pl.BlockSpec((1, 1, 1, pairs), lambda g, i, *s: (g, i, 0, 0)),
            table_spec,
            table_spec,
        ]
        + [
            pl.BlockSpec((rows // chunks, group * LANES), lambda g, i, low, slot: (slot[i], g))
        ]
        * chunks
        + window_specs(stretch, key_columns)
        + window_specs(stretch, value_columns),
        out_specs=[heads_spec, own_spec, own_spec] + [earlier_spec] * (tiles - 1),
        scratch_shapes=[
            pltpu.VMEM((tiles * stretch, LANES), f32),
            pltpu.VMEM((tiles * stretch, LANES), f32),
            pltpu.VMEM((window_tiles, tile_rows, LANES), bf16),
            pltpu.VMEM((window_tiles, tile_rows, LANES), bf16),
            pltpu.VMEM((window_tiles, LANES, tile_rows), bf16),
            pltpu.VMEM((LANES, pairs), f32),
        ],
    )
    work = stretch * stretch * kv_heads * group
    return pl.pallas_call(
        functools.partial(attend_back_kernel, tiles, chunks, group, factor, scale),
        grid_spec=grid_spec,
        out_shape=[
            jax.ShapeDtypeStruct((stretch, kv_heads * group * LANES), bf16),
            jax.ShapeDtypeStruct((stretch, kv_heads * LANES), f32),
            jax.ShapeDtypeStruct((stretch, kv_heads * LANES), f32),
        ]
        + [jax.ShapeDtypeStruct((2, stretch, kv_heads * LANES), bf16)] * (tiles - 1),
        cost_estimate=pl.CostEstimate(
            flops=40 * LANES * work, bytes_accessed=16 * stretch * stretch, transcendentals=work
        ),
        name="attend_back",
    )(low, slots, queries_joined, firsts, mixed, logs, cosine, sine, *grads, *arrays, *arrays)


def gather_back_kernel(kv_heads, parts, key_ref, value_ref, cosine_ref, sine_ref, *refs):
    out_ref = refs[parts]
    for head in range(kv_heads):
        at = pl.ds(head * LANES, LANES)
        key = key_ref[:, at]
        value = value_ref[:, at]
        for part in range(parts):
            key = key + refs[part][0, :, at].astype(f32)
            value = value + refs[part][1, :, at].astype(f32)
        out_ref[:, at] = turn_back(key, cosine_ref[...], sine_ref[...]).astype(bf16)
        out_ref[:, pl.ds((kv_heads + head) * LANES, LANES)] = value.astype(bf16)


def gather_back(key_totals, value_totals, received, cosine, sine, kv_heads, stretch, block):
    width = kv_heads * LANES
    own = pl.BlockSpec((block, width), lambda i: (i, 0))
    other = pl.BlockSpec((2, block, width), lambda i: (0, i, 0))
    table = pl.BlockSpec((block, LANES), lambda i: (i, 0))
    return pl.pallas_call(
        functools.partial(gather_back_kernel, kv_heads, len(received)),
        grid=(stretch // block,),
        in_specs=[own, own, table, table] + [other] * len(received),
        out_specs=pl.BlockSpec((block, 2 * width), lambda i: (i, 0)),
        out_shape=jax.ShapeDtypeStruct((stretch, 2 * width), bf16),
        name="gather_back",
    )(key_totals, value_totals, cosine, sine, *received)


class SharedProduct:

    def __init__(self, left, right, axis, order):
        self.left, self.right, self.axis, self.order = left, right, axis, order
        self.size = left.shape[1] // 2
        self.sent = self.times(0, True).astype(bf16)

    def bit(self, place):
        return (lax.axis_index(self.axis) >> place) & 1

    def times(self, place, other):
        bit = self.bit(self.order[place])
        offset = ((1 - bit) if other else bit) * self.size
        part = lax.dynamic_slice_in_dim(self.left, offset, self.size, 1)
        return jnp.dot(part.T, self.right, preferred_element_type=f32)

    def meet(self, *others):
        got = exchange(self.sent, self.axis, 1 << self.order[0])
        if others:
            got, *others = lax.optimization_barrier((got,) + others)
        self.value = self.times(0, False) + got.astype(f32)
        self.down = list(self.order[1:])
        self.up = list(reversed(self.order))
        return others

    def step(self):
        if self.down:
            place = self.down.pop(0)
            bit = self.bit(place)
            size = self.value.shape[0] // 2
            sent = lax.dynamic_slice_in_dim(self.value, (1 - bit) * size, size, 0).astype(bf16)
            got = exchange(sent, self.axis, 1 << place)
            kept = lax.dynamic_slice_in_dim(self.value, bit * size, size, 0)
            self.value = kept + got.astype(f32)
            return self.value
        self.begin_up()
        return self.end_up()

    def begin_up(self):
        self.place = self.up.pop(0)
        self.value = self.value.astype(bf16)
        self.got = exchange(self.value, self.axis, 1 << self.place)

    def end_up(self):
        self.value = self.joined(self.value, self.got)
        return self.value

    def joined(self, whole, got):
        return jnp.where(
            self.bit(self.place) == 1,
            jnp.concatenate([got, whole], axis=0),
            jnp.concatenate([whole, got], axis=0),
        )

    def finish(self, *spans):
        while len(self.up) > 1:
            self.step()
        if self.up:
            self.begin_up()
        return [
            self.joined(self.value[:, a:b], self.got[:, a:b]).astype(f32)
            for a, b in spans
        ]


def scatter_low(product):
    return lax.psum_scatter(product.astype(bf16), "tensor", scatter_dimension=0, tiled=True)


def gather_rows(rows):
    return lax.all_gather(rows, "tensor", axis=0, tiled=True)


def per_device(
    block_input,
    positions,
    attn_gain,
    w_query,
    key_weight,
    value_weight,
    w_out,
    mlp_gain,
    w_gate,
    w_up,
    w_down,
    out_grad,
):
    stretch = positions.shape[0]
    reach = LONGEST_DOCUMENT // stretch
    heads = w_query.shape[1] // HEAD_SIZE
    kv_heads = key_weight.shape[1] // HEAD_SIZE
    group = heads // kv_heads
    rows = min(512, stretch)
    tile_rows = min(512, stretch)
    blocks = stretch // rows
    places = list(range((lax.axis_size("dp") - 1).bit_length()))
    crossed = places[:1] + places[:0:-1]
    tied = lax.optimization_barrier

    normed_own, inv_rms_attn = normalize(block_input, attn_gain)
    normed_own, out_own = tied((normed_own, out_grad.astype(bf16)))
    attention_normed = gather_rows(normed_own)
    out_low = gather_rows(out_own)

    query_spread = spread_matrix(heads)
    gap = -kv_heads * HEAD_SIZE % LANES
    kv_spread = spread_matrix(2 * kv_heads, kv_heads, gap)
    all_spread = spread_matrix(heads + 2 * kv_heads)
    w_joined = jnp.dot(
        jnp.concatenate([w_query, key_weight, value_weight], axis=1), all_spread,
        preferred_element_type=bf16,
    )
    w_out_spread = jnp.dot(query_spread.T, w_out, preferred_element_type=bf16)
    w_pair = jnp.concatenate([w_gate, w_up], axis=1)
    cosine, sine = rope_tables(positions)
    local = jnp.arange(stretch, dtype=jnp.int32)
    window_first = reach * stretch + local - positions
    firsts = window_first.reshape(blocks, 1, rows)
    cut_first = window_first.reshape(blocks, rows)
    low = jnp.stack(
        [
            jnp.min(cut_first, axis=1) // tile_rows,
            (jnp.max(cut_first, axis=1) + tile_rows - 1) // tile_rows,
        ]
    )

    queries, key_value = project(
        attention_normed, w_joined, cosine, sine, heads + kv_heads,
        (heads * LANES, 2 * kv_heads * LANES), min(256, stretch),
    )
    paired = reach == 2 and lax.axis_size("dp") % 2 == 0
    odd = lax.axis_index("dp") % 2 == 1
    if paired:
        two_back = from_behind(key_value, "dp", 2)
        one_back = exchange(jnp.where(odd, two_back, key_value), "dp", 1)
        windows = [(two_back, 0), (one_back, 0), (key_value, 0)]
    else:
        windows = [(from_behind(key_value, "dp", d), 0) for d in range(reach, -1, -1)]
    attended, logs = attend(queries, windows, firsts, low, kv_heads, group, rows, tile_rows)
    hidden_grad = jnp.dot(out_low, w_down.T, preferred_element_type=f32)
    mixed = scatter_low(jnp.dot(attended, w_out_spread, preferred_element_type=f32))
    mixed, hidden_grad = tied((mixed, hidden_grad))
    residual = block_input + mixed.astype(f32)
    mlp_normed_own, inv_rms_mlp = normalize(residual, mlp_gain)
    normed_mlp = gather_rows(mlp_normed_own)

    width = w_gate.shape[1]
    pre = jnp.dot(normed_mlp, w_pair, preferred_element_type=f32)
    gate_pre, up_proj = pre[:, :width], pre[:, width:]
    sigmoid_gate = jax.nn.sigmoid(gate_pre)
    silu_gate = gate_pre * sigmoid_gate
    hidden = (silu_gate * up_proj).astype(bf16)
    gate_grad = hidden_grad * up_proj * sigmoid_gate * (1.0 + gate_pre * (1.0 - sigmoid_gate))
    up_grad = hidden_grad * silu_gate
    pair_grad = jnp.concatenate([gate_grad.astype(bf16), up_grad.astype(bf16)], axis=1)
    mlp_product = jnp.dot(pair_grad, w_pair.T, preferred_element_type=f32).astype(bf16)
    mlp_product, pair_grad, hidden = tied((mlp_product, pair_grad, hidden))
    mlp_scattered = scatter_low(mlp_product)
    down_product = jnp.dot(hidden, w_down, preferred_element_type=f32).astype(bf16)
    pair_shared = SharedProduct(normed_mlp, pair_grad, "dp", places)
    down_shared = SharedProduct(hidden, out_low, "dp", crossed)
    wide = (pair_shared, down_shared)
    for shared in wide:
        shared.meet()
        shared.step()
    mlp_scattered, down_product, pair_shared.value, down_shared.value = tied(
        (mlp_scattered, down_product, pair_shared.value, down_shared.value)
    )
    mlp_normed_grad = mlp_scattered.astype(f32)
    residual_part = normalize_back(residual, inv_rms_mlp, mlp_gain, mlp_normed_grad)
    residual_grad = out_grad + residual_part
    residual_low = gather_rows(residual_grad.astype(bf16))
    attended_plain = jnp.dot(attended, query_spread.T, preferred_element_type=bf16)
    for shared in wide:
        for _ in range(len(places) - 1):
            shared.step()
    residual_low, down_product, pair_shared.value, down_shared.value, attended_plain = tied(
        (residual_low, down_product, pair_shared.value, down_shared.value, attended_plain)
    )
    block_scattered = lax.psum_scatter(
        down_product, "tensor", scatter_dimension=0, tiled=True
    )
    block_output = residual + block_scattered.astype(f32)

    attended_gradient = jnp.dot(residual_low, w_out_spread.T, preferred_element_type=f32).astype(
        bf16
    )
    slots = jnp.arange(blocks, dtype=jnp.int32)
    query_grad, key_own, value_own, *earlier = attend_back(
        queries, windows, firsts, low, slots, attended, [attended_gradient], logs, cosine,
        sine, kv_heads, group, rows, tile_rows,
    )
    for shared in wide:
        while len(shared.up) > 2:
            shared.step()
        shared.begin_up()
    earlier = [earlier[reach - d] for d in range(1, reach + 1)]
    if paired:
        crossing = exchange(earlier[0], "dp", 1)
        both_back = earlier[1] + jnp.where(odd, crossing, 0)
        both_back, crossing, attended_plain = tied((both_back, crossing, attended_plain))
        both_received = from_behind(both_back, "dp", -2)
        received = [both_received, jnp.where(odd, 0, crossing)]
    else:
        earlier, attended_plain = tied((earlier, attended_plain))
        received = [from_behind(earlier[d - 1], "dp", -d) for d in range(1, reach + 1)]
    out_shared = SharedProduct(attended_plain, residual_low, "dp", crossed)
    pair_shared.got, down_shared.got = out_shared.meet(pair_shared.got, down_shared.got)
    for shared in wide:
        shared.end_up()
        shared.begin_up()
    query_plain = jnp.dot(query_grad, query_spread.T, preferred_element_type=bf16)
    query_shared = SharedProduct(attention_normed, query_plain, "dp", places)
    query_shared.meet()
    received, pair_shared.got, down_shared.got, out_shared.value, query_shared.value = tied(
        (received, pair_shared.got, down_shared.got, out_shared.value, query_shared.value)
    )
    key_value_grad = gather_back(
        key_own, value_own, received, cosine, sine, kv_heads, stretch, min(256, stretch)
    )
    split = heads * LANES
    attn_normed_part = (
        jnp.dot(query_grad, w_joined[:, :split].T, preferred_element_type=f32)
        + jnp.dot(key_value_grad, w_joined[:, split:].T, preferred_element_type=f32)
    ).astype(bf16)
    attn_scattered = lax.psum_scatter(attn_normed_part, "tensor", scatter_dimension=0, tiled=True)
    attn_gain_part = (
        jnp.sum(
            attn_normed_part.astype(f32) * attention_normed.astype(f32), axis=0, keepdims=True
        )
        / attn_gain
    )
    mlp_gain_part = jnp.sum(mlp_normed_grad * residual * inv_rms_mlp, axis=0, keepdims=True)
    gains = jnp.concatenate([attn_gain_part, mlp_gain_part], axis=0)
    rounds = [
        (axis, 1 << place)
        for axis in ("tensor", "dp")
        for place in range((lax.axis_size(axis) - 1).bit_length())
    ]
    kv_plain = jnp.dot(key_value_grad, kv_spread.T, preferred_element_type=bf16)
    kv_shared = SharedProduct(attention_normed, kv_plain, "dp", crossed)
    kv_shared.meet()
    grad_gate, grad_up = pair_shared.finish((0, width), (width, 2 * width))
    (grad_down,) = down_shared.finish((0, out_grad.shape[1]))
    outputs = [grad_down, grad_gate, grad_up, block_output]
    for place in range(len(outputs)):
        query_shared.step()
        kv_shared.step()
        if rounds:
            axis, distance = rounds.pop(0)
            gains = gains + exchange(gains, axis, distance)
        kv_shared.value, query_shared.value, gains, outputs[place] = tied(
            (kv_shared.value, query_shared.value, gains, outputs[place])
        )
    grad_down, grad_gate, grad_up, block_output = outputs
    for axis, distance in rounds:
        gains = gains + exchange(gains, axis, distance)
    grad_attn_gain, grad_mlp_gain = gains[0], gains[1]
    query_width = w_query.shape[1]
    kv_width = key_weight.shape[1]
    (grad_query,) = query_shared.finish((0, query_width))
    grad_key, grad_value = kv_shared.finish(
        (0, kv_width), (kv_width + gap, 2 * kv_width + gap)
    )
    (grad_out,) = out_shared.finish((0, out_grad.shape[1]))
    attn_normed_grad = attn_scattered.astype(f32)
    input_part = normalize_back(block_input, inv_rms_attn, attn_gain, attn_normed_grad)
    input_grad = residual_grad + input_part
    return (
        block_output,
        input_grad,
        grad_query,
        grad_key,
        grad_value,
        grad_out,
        grad_gate,
        grad_up,
        grad_down,
        grad_attn_gain,
        grad_mlp_gain,
    )


def solution(mesh):
    in_specs = (
        P(("dp", "tensor"), None),
        P("dp"),
        P(),
        P(None, "tensor"),
        P(None, "tensor"),
        P(None, "tensor"),
        P("tensor", None),
        P(),
        P(None, "tensor"),
        P(None, "tensor"),
        P("tensor", None),
        P(("dp", "tensor"), None),
    )
    out_specs = (
        P(("dp", "tensor"), None),
        P(("dp", "tensor"), None),
        P(None, "tensor"),
        P(None, "tensor"),
        P(None, "tensor"),
        P("tensor", None),
        P(None, "tensor"),
        P(None, "tensor"),
        P("tensor", None),
        P(),
        P(),
    )

    return jax.shard_map(
        per_device, mesh=mesh, in_specs=in_specs, out_specs=out_specs, check_vma=False
    )
```

```python
import functools
import math

import jax
import jax.numpy as jnp
from jax import lax
from jax.experimental import pallas as pl
from jax.experimental.pallas import tpu as pltpu
from jax.sharding import PartitionSpec as P


HEAD_SIZE = 96
LONGEST_DOCUMENT = 2048

LANES = 128
HALF_LANES = LANES // 2
FAR = -1e30


epsilon = 1e-05
rope_base = 100000.0

f32 = jnp.float32
bf16 = jnp.bfloat16


def from_behind(value, axis, steps):
    if steps == 0:
        return value
    count = lax.axis_size(axis)
    leading, last = (max(0, -steps), min(count, count - steps))
    return lax.ppermute(value, axis, [(source, source + steps) for source in range(leading, last)])


def exchange(value, axis, distance):
    count = lax.axis_size(axis)
    return lax.ppermute(value, axis, [(i, i ^ distance) for i in range(count)])


def rope_tables(positions):
    half_size = HEAD_SIZE // 2
    frequency = rope_base ** (-jnp.arange(half_size, dtype=f32) * 2.0 / HEAD_SIZE)
    rest = jnp.zeros((HALF_LANES - half_size,), f32)
    spread = jnp.concatenate([frequency, rest, frequency, rest])
    sign = jnp.where(jnp.arange(LANES) < HALF_LANES, -1.0, 1.0).astype(f32)
    angles = positions.astype(f32)[:, None] * spread[None, :]
    return (jnp.cos(angles), jnp.sin(angles) * sign[None, :])


def spread_matrix(heads, gap_after=0, gap=0, dtype=bf16):
    half_size = HEAD_SIZE // 2
    rows = jnp.arange(heads * HEAD_SIZE, dtype=jnp.int32)
    inner = rows % HEAD_SIZE
    lane = (rows // HEAD_SIZE) * LANES + jnp.where(
        inner < half_size, inner, inner - half_size + HALF_LANES
    )
    if gap:
        cut = gap_after * HEAD_SIZE
        lane = jnp.concatenate([lane[:cut], jnp.full((gap,), -1, jnp.int32), lane[cut:]])
    columns = jnp.arange(heads * LANES, dtype=jnp.int32)
    return (lane[:, None] == columns[None, :]).astype(dtype)


def normalize(rows, gain):
    inv_rms = lax.rsqrt(jnp.mean(rows * rows, axis=-1, keepdims=True) + epsilon)
    return ((rows * inv_rms * gain).astype(bf16), inv_rms)


def normalize_back(rows, inv_rms, gain, normed_grad):
    weighted = normed_grad * gain
    inner = jnp.mean(weighted * rows, axis=-1, keepdims=True)
    return inv_rms * weighted - rows * inv_rms**3 * inner


def turn(value, cosine, sine):
    return value * cosine + pltpu.roll(value, HALF_LANES, 1) * sine


def turn_back(value, cosine, sine):
    return value * cosine - pltpu.roll(value, HALF_LANES, 1) * sine


def project_kernel(rotated, rows_ref, weight_ref, cosine_ref, sine_ref, *out_refs):
    product = jnp.dot(rows_ref[...], weight_ref[...], preferred_element_type=f32)
    cosine = cosine_ref[...]
    sine = sine_ref[...]
    head = 0
    for out_ref in out_refs:
        for place in range(out_ref.shape[1] // LANES):
            part = product[:, head * LANES : (head + 1) * LANES]
            if head < rotated:
                part = turn(part, cosine, sine)
            out_ref[:, place * LANES : (place + 1) * LANES] = part.astype(bf16)
            head += 1


def project(rows, weight, cosine, sine, rotated, widths, block):
    count, depth = rows.shape
    width = weight.shape[1]
    return pl.pallas_call(
        functools.partial(project_kernel, rotated),
        grid=(count // block,),
        in_specs=[
            pl.BlockSpec((block, depth), lambda i: (i, 0)),
            pl.BlockSpec((depth, width), lambda i: (0, 0)),
            pl.BlockSpec((block, LANES), lambda i: (i, 0)),
            pl.BlockSpec((block, LANES), lambda i: (i, 0)),
        ],
        out_specs=[pl.BlockSpec((block, part), lambda i: (i, 0)) for part in widths],
        out_shape=[jax.ShapeDtypeStruct((count, part), bf16) for part in widths],
        cost_estimate=pl.CostEstimate(
            flops=2 * count * depth * width,
            bytes_accessed=2 * (count * depth + depth * width + count * width),
            transcendentals=0,
        ),
        name="project",
    )(rows, weight, cosine, sine)


def pair_rows(ref, group):
    return jnp.concatenate([ref[:, h * LANES : (h + 1) * LANES] for h in range(group)], axis=0)


def place_row(ref, group):
    row = ref[0]
    return jnp.concatenate([row] * group, axis=1)


def masked(scores, first, last, base):
    index = lax.broadcasted_iota(jnp.int32, scores.shape, 0)
    allowed = (index >= first - base) & (index <= last - base)
    return jnp.where(allowed, scores, FAR)


def bounds(low_ref, query_block, rows, tile_rows, offset):
    high = (offset + (query_block + 1) * rows - 1) // tile_rows + 1
    return low_ref[0, query_block], high


def sweep(low_ref, query_block, rows, tile_rows, offset, step):
    low, high = bounds(low_ref, query_block, rows, tile_rows, offset)
    full_from = low_ref[1, query_block]
    full_to = (offset + query_block * rows) // tile_rows

    def turn_over(tile, unused):
        whole = (tile >= full_from) & (tile < full_to)
        pl.when(whole)(lambda: step(tile, False))
        pl.when(jnp.logical_not(whole))(lambda: step(tile, True))
        return unused

    lax.fori_loop(low, high, turn_over, 0)


def attend_kernel(tiles, group, factor, low_ref, query_ref, first_ref, *refs):
    keys = refs[:tiles]
    values = refs[tiles : 2 * tiles]
    out_ref, log_ref, key_window, value_turned, top, total, mixed = refs[2 * tiles :]
    query_block = pl.program_id(1)
    rows = query_ref.shape[0]
    stretch = keys[0].shape[0]
    tile_rows = key_window.shape[1]
    per_tile = stretch // tile_rows

    @pl.when(query_block == 0)
    def _():
        for tile in range(tiles):
            for part in range(per_tile):
                place = tile * per_tile + part

                @pl.when(place >= low_ref[0, 0])
                def _(tile=tile, place=place, at=pl.ds(part * tile_rows, tile_rows)):
                    key_window[place] = keys[tile][at, :]
                    value_turned[place] = values[tile][at, :].T

    offset = (tiles - 1) * stretch
    query = pair_rows(query_ref, group)
    first = place_row(first_ref, group)
    lane = lax.broadcasted_iota(jnp.int32, (1, rows), 1)
    last = jnp.concatenate([lane] * group, axis=1) + (offset + query_block * rows)
    top[...] = jnp.full_like(top, FAR)
    total[...] = jnp.zeros_like(total)
    mixed[...] = jnp.zeros_like(mixed)

    def step(tile, check):
        scores = lax.dot_general(
            key_window[tile], query, (((1,), (1,)), ((), ())), preferred_element_type=f32
        )
        if check:
            scores = masked(scores, first, last, tile * tile_rows)
        before = top[...]
        after = jnp.maximum(before, jnp.max(scores, axis=0, keepdims=True))
        weights = jnp.exp2(scores * factor - after * factor)
        fade = jnp.exp2((before - after) * factor)
        top[...] = after
        total[...] = total[...] * fade + jnp.sum(weights, axis=0, keepdims=True)
        mixed[...] = mixed[...] * fade + jnp.dot(
            value_turned[tile], weights.astype(bf16), preferred_element_type=f32
        )

    sweep(low_ref, query_block, rows, tile_rows, offset, step)
    result = (mixed[...] / total[...]).T.astype(bf16)
    for head in range(group):
        out_ref[:, head * LANES : (head + 1) * LANES] = result[head * rows : (head + 1) * rows]
    log_ref[0, 0] = top[...] * factor + jnp.log2(total[...])


def window_specs(stretch, first_column):
    return [
        pl.BlockSpec((stretch, LANES), lambda g, i, *s, c=c: (0, c + g)) for c in first_column
    ]


def attend(queries_joined, windows, firsts, low, kv_heads, group, rows, tile_rows):
    stretch = queries_joined.shape[0]
    tiles = len(windows)
    blocks = stretch // rows
    pairs = group * rows
    window_tiles = tiles * stretch // tile_rows
    factor = HEAD_SIZE ** (-0.5) * math.log2(math.e)
    key_columns = [at for _, at in windows]
    value_columns = [at + kv_heads for _, at in windows]
    arrays = [a for a, _ in windows]
    grid_spec = pltpu.PrefetchScalarGridSpec(
        num_scalar_prefetch=1,
        grid=(kv_heads, blocks),
        in_specs=[
            pl.BlockSpec((rows, group * LANES), lambda g, i, *s: (i, g)),
            pl.BlockSpec((1, 1, rows), lambda g, i, *s: (i, 0, 0)),
        ]
        + window_specs(stretch, key_columns)
        + window_specs(stretch, value_columns),
        out_specs=[
            pl.BlockSpec((rows, group * LANES), lambda g, i, *s: (i, g)),
            pl.BlockSpec((1, 1, 1, pairs), lambda g, i, *s: (g, i, 0, 0)),
        ],
        scratch_shapes=[
            pltpu.VMEM((window_tiles, tile_rows, LANES), bf16),
            pltpu.VMEM((window_tiles, LANES, tile_rows), bf16),
            pltpu.VMEM((1, pairs), f32),
            pltpu.VMEM((1, pairs), f32),
            pltpu.VMEM((LANES, pairs), f32),
        ],
    )
    work = stretch * stretch * kv_heads * group
    return pl.pallas_call(
        functools.partial(attend_kernel, tiles, group, factor),
        grid_spec=grid_spec,
        out_shape=[
            jax.ShapeDtypeStruct((stretch, kv_heads * group * LANES), bf16),
            jax.ShapeDtypeStruct((kv_heads, blocks, 1, pairs), f32),
        ],
        cost_estimate=pl.CostEstimate(
            flops=16 * LANES * work, bytes_accessed=8 * stretch * stretch, transcendentals=work
        ),
        name="attend",
    )(low, queries_joined, firsts, *arrays, *arrays)


def attend_back_kernel(
    tiles, chunks, group, factor, scale, low_ref, slot_ref, query_ref, first_ref, *refs
):
    mixed_ref, log_ref, cosine_ref, sine_ref = refs[:4]
    grad_refs = refs[4 : 4 + chunks]
    refs = refs[4 + chunks :]
    keys = refs[:tiles]
    values = refs[tiles : 2 * tiles]
    refs = refs[2 * tiles :]
    earlier_outs = refs[3 : 2 + tiles]
    query_out, key_own, value_own = refs[:3]
    (
        key_out,
        value_out,
        key_window,
        value_window,
        key_turned,
        query_total,
    ) = refs[2 + tiles :]
    query_block = pl.program_id(1)
    rows = query_ref.shape[0]
    stretch = keys[0].shape[0]
    tile_rows = key_window.shape[1]
    per_tile = stretch // tile_rows

    @pl.when(query_block == 0)
    def _():
        key_out[...] = jnp.zeros_like(key_out)
        value_out[...] = jnp.zeros_like(value_out)
        for tile in range(tiles):
            for part in range(per_tile):
                place = tile * per_tile + part

                @pl.when(place >= low_ref[0, 0])
                def _(tile=tile, place=place, at=pl.ds(part * tile_rows, tile_rows)):
                    key_window[place] = keys[tile][at, :]
                    key_turned[place] = keys[tile][at, :].T
                    value_window[place] = values[tile][at, :]

    offset = (tiles - 1) * stretch
    query = pair_rows(query_ref, group)
    grad = jnp.concatenate(
        [ref[:, h * LANES : (h + 1) * LANES] for h in range(group) for ref in grad_refs], axis=0
    )
    mixed = pair_rows(mixed_ref, group)
    inner = jnp.sum((grad.astype(f32) * mixed.astype(f32)).T, axis=0, keepdims=True)
    log_total = log_ref[0, 0]
    first = place_row(first_ref, group)
    lane = lax.broadcasted_iota(jnp.int32, (1, rows), 1)
    last = jnp.concatenate([lane] * group, axis=1) + (offset + query_block * rows)
    query_total[...] = jnp.zeros_like(query_total)
    both_last = (((1,), (1,)), ((), ()))

    def step(tile, check):
        scores = lax.dot_general(key_window[tile], query, both_last, preferred_element_type=f32)
        if check:
            scores = masked(scores, first, last, tile * tile_rows)
        weights = jnp.exp2(scores * factor - log_total)
        weight_grad = lax.dot_general(
            value_window[tile], grad, both_last, preferred_element_type=f32
        )
        score_grad = (weights * (weight_grad - inner) * scale).astype(bf16)
        at = pl.ds(pl.multiple_of(tile * tile_rows, tile_rows), tile_rows)
        value_out[at, :] += jnp.dot(weights.astype(bf16), grad, preferred_element_type=f32)
        key_out[at, :] += jnp.dot(score_grad, query, preferred_element_type=f32)
        query_total[...] += jnp.dot(key_turned[tile], score_grad, preferred_element_type=f32)

    sweep(low_ref, query_block, rows, tile_rows, offset, step)
    result = query_total[...].T
    for head in range(group):
        part = result[head * rows : (head + 1) * rows]
        query_out[:, head * LANES : (head + 1) * LANES] = turn_back(
            part, cosine_ref[...], sine_ref[...]
        ).astype(bf16)

    @pl.when(query_block == pl.num_programs(1) - 1)
    def _():
        for tile in range(tiles - 1):
            at = pl.ds(tile * stretch, stretch)
            earlier_outs[tile][0] = key_out[at, :].astype(bf16)
            earlier_outs[tile][1] = value_out[at, :].astype(bf16)
        key_own[...] = key_out[pl.ds(offset, stretch), :]
        value_own[...] = value_out[pl.ds(offset, stretch), :]


def attend_back(
    queries_joined, windows, firsts, low, slots, mixed, grads, logs, cosine, sine,
    kv_heads, group, rows, tile_rows,
):
    stretch = queries_joined.shape[0]
    tiles = len(windows)
    blocks = stretch // rows
    pairs = group * rows
    window_tiles = tiles * stretch // tile_rows
    chunks = len(grads)
    scale = HEAD_SIZE ** (-0.5)
    factor = scale * math.log2(math.e)
    key_columns = [at for _, at in windows]
    value_columns = [at + kv_heads for _, at in windows]
    arrays = [a for a, _ in windows]
    heads_spec = pl.BlockSpec((rows, group * LANES), lambda g, i, *s: (i, g))
    table_spec = pl.BlockSpec((rows, LANES), lambda g, i, *s: (i, 0))
    own_spec = pl.BlockSpec((stretch, LANES), lambda g, i, *s: (0, g))
    earlier_spec = pl.BlockSpec((2, stretch, LANES), lambda g, i, *s: (0, 0, g))
    grid_spec = pltpu.PrefetchScalarGridSpec(
        num_scalar_prefetch=2,
        grid=(kv_heads, blocks),
        in_specs=[
            heads_spec,
            pl.BlockSpec((1, 1, rows), lambda g, i, *s: (i, 0, 0)),
            heads_spec,
            pl.BlockSpec((1, 1, 1, pairs), lambda g, i, *s: (g, i, 0, 0)),
            table_spec,
            table_spec,
        ]
        + [
            pl.BlockSpec((rows // chunks, group * LANES), lambda g, i, low, slot: (slot[i], g))
        ]
        * chunks
        + window_specs(stretch, key_columns)
        + window_specs(stretch, value_columns),
        out_specs=[heads_spec, own_spec, own_spec] + [earlier_spec] * (tiles - 1),
        scratch_shapes=[
            pltpu.VMEM((tiles * stretch, LANES), f32),
            pltpu.VMEM((tiles * stretch, LANES), f32),
            pltpu.VMEM((window_tiles, tile_rows, LANES), bf16),
            pltpu.VMEM((window_tiles, tile_rows, LANES), bf16),
            pltpu.VMEM((window_tiles, LANES, tile_rows), bf16),
            pltpu.VMEM((LANES, pairs), f32),
        ],
    )
    work = stretch * stretch * kv_heads * group
    return pl.pallas_call(
        functools.partial(attend_back_kernel, tiles, chunks, group, factor, scale),
        grid_spec=grid_spec,
        out_shape=[
            jax.ShapeDtypeStruct((stretch, kv_heads * group * LANES), bf16),
            jax.ShapeDtypeStruct((stretch, kv_heads * LANES), f32),
            jax.ShapeDtypeStruct((stretch, kv_heads * LANES), f32),
        ]
        + [jax.ShapeDtypeStruct((2, stretch, kv_heads * LANES), bf16)] * (tiles - 1),
        cost_estimate=pl.CostEstimate(
            flops=40 * LANES * work, bytes_accessed=16 * stretch * stretch, transcendentals=work
        ),
        name="attend_back",
    )(low, slots, queries_joined, firsts, mixed, logs, cosine, sine, *grads, *arrays, *arrays)


def gather_back_kernel(
    kv_heads, parts, key_ref, value_ref, cosine_ref, sine_ref, share_ref, *refs
):
    out_ref = refs[parts]
    for head in range(kv_heads):
        at = pl.ds(head * LANES, LANES)
        key = key_ref[:, at]
        value = value_ref[:, at]
        for part in range(parts):
            share = share_ref[part : part + 1, :]
            key = key + share * refs[part][0, :, at].astype(f32)
            value = value + share * refs[part][1, :, at].astype(f32)
        out_ref[:, at] = turn_back(key, cosine_ref[...], sine_ref[...]).astype(bf16)
        out_ref[:, pl.ds((kv_heads + head) * LANES, LANES)] = value.astype(bf16)


def gather_back(
    key_totals, value_totals, received, shares, cosine, sine, kv_heads, stretch, block
):
    width = kv_heads * LANES
    own = pl.BlockSpec((block, width), lambda i: (i, 0))
    other = pl.BlockSpec((2, block, width), lambda i: (0, i, 0))
    table = pl.BlockSpec((block, LANES), lambda i: (i, 0))
    return pl.pallas_call(
        functools.partial(gather_back_kernel, kv_heads, len(received)),
        grid=(stretch // block,),
        in_specs=[own, own, table, table, pl.BlockSpec(shares.shape, lambda i: (0, 0))]
        + [other] * len(received),
        out_specs=pl.BlockSpec((block, 2 * width), lambda i: (i, 0)),
        out_shape=jax.ShapeDtypeStruct((stretch, 2 * width), bf16),
        name="gather_back",
    )(key_totals, value_totals, cosine, sine, shares, *received)


class SharedProduct:

    def __init__(self, left, right, axis, order):
        self.left, self.right, self.axis, self.order = left, right, axis, order
        self.size = left.shape[1] // 2
        self.sent = self.times(0, True).astype(bf16)

    def bit(self, place):
        return (lax.axis_index(self.axis) >> place) & 1

    def times(self, place, other):
        bit = self.bit(self.order[place])
        offset = ((1 - bit) if other else bit) * self.size
        part = lax.dynamic_slice_in_dim(self.left, offset, self.size, 1)
        return jnp.dot(part.T, self.right, preferred_element_type=f32)

    def meet(self):
        got = exchange(self.sent, self.axis, 1 << self.order[0])
        self.value = self.times(0, False) + got.astype(f32)
        self.down = list(self.order[1:])
        self.up = list(reversed(self.order))

    def step(self):
        if self.down:
            place = self.down.pop(0)
            bit = self.bit(place)
            size = self.value.shape[0] // 2
            sent = lax.dynamic_slice_in_dim(self.value, (1 - bit) * size, size, 0).astype(bf16)
            got = exchange(sent, self.axis, 1 << place)
            kept = lax.dynamic_slice_in_dim(self.value, bit * size, size, 0)
            self.value = kept + got.astype(f32)
            return self.value
        self.begin_up()
        return self.end_up()

    def begin_up(self):
        self.place = self.up.pop(0)
        self.value = self.value.astype(bf16)
        self.got = exchange(self.value, self.axis, 1 << self.place)

    def end_up(self):
        self.value = self.joined(self.value, self.got)
        return self.value

    def joined(self, whole, got):
        return jnp.where(
            self.bit(self.place) == 1,
            jnp.concatenate([got, whole], axis=0),
            jnp.concatenate([whole, got], axis=0),
        )

    def finish(self, *spans):
        while len(self.up) > 1:
            self.step()
        if self.up:
            self.begin_up()
        return [
            self.joined(self.value[:, a:b], self.got[:, a:b]).astype(f32)
            for a, b in spans
        ]


def scatter_low(product):
    return lax.psum_scatter(product.astype(bf16), "tensor", scatter_dimension=0, tiled=True)


def gather_rows(rows):
    return lax.all_gather(rows, "tensor", axis=0, tiled=True)


def per_device(
    block_input,
    positions,
    attn_gain,
    w_query,
    key_weight,
    value_weight,
    w_out,
    mlp_gain,
    w_gate,
    w_up,
    w_down,
    out_grad,
):
    stretch = positions.shape[0]
    reach = LONGEST_DOCUMENT // stretch
    heads = w_query.shape[1] // HEAD_SIZE
    kv_heads = key_weight.shape[1] // HEAD_SIZE
    group = heads // kv_heads
    rows = min(512, stretch)
    tile_rows = min(512, stretch)
    blocks = stretch // rows
    places = list(range((lax.axis_size("dp") - 1).bit_length()))
    crossed = places[:1] + places[:0:-1]
    tied = lax.optimization_barrier

    normed_own, inv_rms_attn = normalize(block_input, attn_gain)
    normed_own, out_own = tied((normed_own, out_grad.astype(bf16)))
    attention_normed = gather_rows(normed_own)
    out_low = gather_rows(out_own)

    query_spread = spread_matrix(heads)
    gap = -kv_heads * HEAD_SIZE % LANES
    kv_spread = spread_matrix(2 * kv_heads, kv_heads, gap)
    all_spread = spread_matrix(heads + 2 * kv_heads)
    w_joined = jnp.dot(
        jnp.concatenate([w_query, key_weight, value_weight], axis=1), all_spread,
        preferred_element_type=bf16,
    )
    w_out_spread = jnp.dot(query_spread.T, w_out, preferred_element_type=bf16)
    w_pair = jnp.concatenate([w_gate, w_up], axis=1)
    cosine, sine = rope_tables(positions)
    local = jnp.arange(stretch, dtype=jnp.int32)
    window_first = reach * stretch + local - positions
    firsts = window_first.reshape(blocks, 1, rows)
    cut_first = window_first.reshape(blocks, rows)
    low = jnp.stack(
        [
            jnp.min(cut_first, axis=1) // tile_rows,
            (jnp.max(cut_first, axis=1) + tile_rows - 1) // tile_rows,
        ]
    )

    queries, key_value = project(
        attention_normed, w_joined, cosine, sine, heads + kv_heads,
        (heads * LANES, 2 * kv_heads * LANES), min(256, stretch),
    )
    paired = reach == 2 and lax.axis_size("dp") % 2 == 0
    odd = lax.axis_index("dp") % 2 == 1
    if paired:
        two_back = from_behind(key_value, "dp", 2)
        one_back = exchange(jnp.where(odd, two_back, key_value), "dp", 1)
        windows = [(two_back, 0), (one_back, 0), (key_value, 0)]
    else:
        windows = [(from_behind(key_value, "dp", d), 0) for d in range(reach, -1, -1)]
    attended, logs = attend(queries, windows, firsts, low, kv_heads, group, rows, tile_rows)
    hidden_grad = jnp.dot(out_low, w_down.T, preferred_element_type=f32)
    mixed = scatter_low(jnp.dot(attended, w_out_spread, preferred_element_type=f32))
    mixed, hidden_grad = tied((mixed, hidden_grad))
    residual = block_input + mixed.astype(f32)
    mlp_normed_own, inv_rms_mlp = normalize(residual, mlp_gain)
    normed_mlp = gather_rows(mlp_normed_own)

    width = w_gate.shape[1]
    pre = jnp.dot(normed_mlp, w_pair, preferred_element_type=f32)
    gate_pre, up_proj = pre[:, :width], pre[:, width:]
    sigmoid_gate = jax.nn.sigmoid(gate_pre)
    silu_gate = gate_pre * sigmoid_gate
    hidden = (silu_gate * up_proj).astype(bf16)
    gate_grad = hidden_grad * up_proj * sigmoid_gate * (1.0 + gate_pre * (1.0 - sigmoid_gate))
    up_grad = hidden_grad * silu_gate
    pair_grad = jnp.concatenate([gate_grad.astype(bf16), up_grad.astype(bf16)], axis=1)
    mlp_product = jnp.dot(pair_grad, w_pair.T, preferred_element_type=f32).astype(bf16)
    mlp_product, pair_grad, hidden = tied((mlp_product, pair_grad, hidden))
    mlp_scattered = scatter_low(mlp_product)
    down_product = jnp.dot(hidden, w_down, preferred_element_type=f32).astype(bf16)
    pair_shared = SharedProduct(normed_mlp, pair_grad, "dp", places)
    down_shared = SharedProduct(hidden, out_low, "dp", crossed)
    wide = (pair_shared, down_shared)
    for shared in wide:
        shared.meet()
        shared.step()
    mlp_scattered, down_product, pair_shared.value, down_shared.value = tied(
        (mlp_scattered, down_product, pair_shared.value, down_shared.value)
    )
    mlp_normed_grad = mlp_scattered.astype(f32)
    residual_part = normalize_back(residual, inv_rms_mlp, mlp_gain, mlp_normed_grad)
    residual_grad = out_grad + residual_part
    residual_low = gather_rows(residual_grad.astype(bf16))
    attended_plain = jnp.dot(attended, query_spread.T, preferred_element_type=bf16)
    for shared in wide:
        for _ in range(len(places) - 1):
            shared.step()
    residual_low, down_product, pair_shared.value, down_shared.value, attended_plain = tied(
        (residual_low, down_product, pair_shared.value, down_shared.value, attended_plain)
    )
    block_scattered = lax.psum_scatter(
        down_product, "tensor", scatter_dimension=0, tiled=True
    )
    block_output = residual + block_scattered.astype(f32)

    attended_gradient = jnp.dot(residual_low, w_out_spread.T, preferred_element_type=f32).astype(
        bf16
    )
    slots = jnp.arange(blocks, dtype=jnp.int32)
    query_grad, key_own, value_own, *earlier = attend_back(
        queries, windows, firsts, low, slots, attended, [attended_gradient], logs, cosine,
        sine, kv_heads, group, rows, tile_rows,
    )
    for shared in wide:
        while len(shared.up) > 2:
            shared.step()
        shared.begin_up()
    earlier = [earlier[reach - d] for d in range(1, reach + 1)]
    if paired:
        crossing = exchange(earlier[0], "dp", 1)
        both_back = earlier[1] + jnp.where(odd, crossing, 0)
        both_back, crossing, attended_plain = tied((both_back, crossing, attended_plain))
        both_received = from_behind(both_back, "dp", -2)
        received = [both_received, crossing]
        counts = [1.0, jnp.where(odd, 0.0, 1.0)]
    else:
        earlier, attended_plain = tied((earlier, attended_plain))
        received = [from_behind(earlier[d - 1], "dp", -d) for d in range(1, reach + 1)]
        counts = [1.0] * reach
    shares = jnp.stack([jnp.full((LANES,), count, f32) for count in counts])
    out_shared = SharedProduct(attended_plain, residual_low, "dp", crossed)
    out_shared.meet()
    for shared in wide:
        shared.end_up()
        shared.begin_up()
    query_plain = jnp.dot(query_grad, query_spread.T, preferred_element_type=bf16)
    query_shared = SharedProduct(attention_normed, query_plain, "dp", places)
    query_shared.meet()
    received, pair_shared.got, down_shared.got, out_shared.value, query_shared.value = tied(
        (received, pair_shared.got, down_shared.got, out_shared.value, query_shared.value)
    )
    key_value_grad = gather_back(
        key_own, value_own, received, shares, cosine, sine, kv_heads, stretch, min(256, stretch)
    )
    split = heads * LANES
    attn_normed_part = (
        jnp.dot(query_grad, w_joined[:, :split].T, preferred_element_type=f32)
        + jnp.dot(key_value_grad, w_joined[:, split:].T, preferred_element_type=f32)
    ).astype(bf16)
    attn_scattered = lax.psum_scatter(attn_normed_part, "tensor", scatter_dimension=0, tiled=True)
    attn_gain_part = (
        jnp.sum(
            attn_normed_part.astype(f32) * attention_normed.astype(f32), axis=0, keepdims=True
        )
        / attn_gain
    )
    mlp_gain_part = jnp.sum(mlp_normed_grad * residual * inv_rms_mlp, axis=0, keepdims=True)
    gains = jnp.concatenate([attn_gain_part, mlp_gain_part], axis=0)
    rounds = [
        (axis, 1 << place)
        for axis in ("tensor", "dp")
        for place in range((lax.axis_size(axis) - 1).bit_length())
    ]
    kv_plain = jnp.dot(key_value_grad, kv_spread.T, preferred_element_type=bf16)
    kv_shared = SharedProduct(attention_normed, kv_plain, "dp", crossed)
    kv_shared.meet()
    grad_gate, grad_up = pair_shared.finish((0, width), (width, 2 * width))
    (grad_down,) = down_shared.finish((0, out_grad.shape[1]))
    if rounds:
        axis, distance = rounds.pop(0)
        gains = gains + exchange(gains, axis, distance)
    outputs = [grad_down, grad_gate, grad_up, block_output]
    for place in range(len(outputs)):
        query_shared.step()
        kv_shared.step()
        if rounds:
            axis, distance = rounds.pop(0)
            gains = gains + exchange(gains, axis, distance)
        kv_shared.value, query_shared.value, gains, outputs[place] = tied(
            (kv_shared.value, query_shared.value, gains, outputs[place])
        )
    grad_down, grad_gate, grad_up, block_output = outputs
    for axis, distance in rounds:
        gains = gains + exchange(gains, axis, distance)
    grad_attn_gain, grad_mlp_gain = gains[0], gains[1]
    query_width = w_query.shape[1]
    kv_width = key_weight.shape[1]
    (grad_query,) = query_shared.finish((0, query_width))
    grad_key, grad_value = kv_shared.finish(
        (0, kv_width), (kv_width + gap, 2 * kv_width + gap)
    )
    (grad_out,) = out_shared.finish((0, out_grad.shape[1]))
    attn_normed_grad = attn_scattered.astype(f32)
    input_part = normalize_back(block_input, inv_rms_attn, attn_gain, attn_normed_grad)
    input_grad = residual_grad + input_part
    return (
        block_output,
        input_grad,
        grad_query,
        grad_key,
        grad_value,
        grad_out,
        grad_gate,
        grad_up,
        grad_down,
        grad_attn_gain,
        grad_mlp_gain,
    )


def solution(mesh):
    in_specs = (
        P(("dp", "tensor"), None),
        P("dp"),
        P(),
        P(None, "tensor"),
        P(None, "tensor"),
        P(None, "tensor"),
        P("tensor", None),
        P(),
        P(None, "tensor"),
        P(None, "tensor"),
        P("tensor", None),
        P(("dp", "tensor"), None),
    )
    out_specs = (
        P(("dp", "tensor"), None),
        P(("dp", "tensor"), None),
        P(None, "tensor"),
        P(None, "tensor"),
        P(None, "tensor"),
        P("tensor", None),
        P(None, "tensor"),
        P(None, "tensor"),
        P("tensor", None),
        P(),
        P(),
    )

    return jax.shard_map(
        per_device, mesh=mesh, in_specs=in_specs, out_specs=out_specs, check_vma=False
    )
```
